32 devices in a mesh: dp: 4 (over z), fsdp: 8 (over y, x, core).
Axes of the slice: x: 2, y: 2, z: 4, core: 2. Of those that a mesh axis runs over, the one named last changes fastest.
Arguments:
- activations: bfloat16 [64, 1024, 1280], P(('dp', 'fsdp')), may hold values from -6 to 6
- cotangent: bfloat16 [64, 1024, 1280], P(('dp', 'fsdp')), may hold values from -6 to 6
- lengths: int32 [64], P(('dp', 'fsdp')), may hold values from 256 to 1024, as said below
- cluster_sizes: int32 [64], P(('dp', 'fsdp')), may hold values from 1 to 8
- residue_types: int32 [64, 1024], P(('dp', 'fsdp')), may hold values from 0 to 24
- input_projection_weight: bfloat16 [1280, 640], P('dp', 'fsdp'), may hold values from -0.15625 to 0.15625
- weight_conv: bfloat16 [5, 640, 640], P(None, 'dp', 'fsdp'), may hold values from -0.109375 to 0.109375
- output_projection_weight: bfloat16 [640, 1280], P('dp', 'fsdp'), may hold values from -0.25 to 0.25
- inner_bias_gains: bfloat16 [6, 640], P(None, 'fsdp'), may hold values from -0.9 to 1.5
- model_bias_gains: bfloat16 [3, 1280], P(None, 'fsdp'), may hold values from -0.9 to 1.5
Outputs:
- block_out: bfloat16 [64, 1024, 1280], P(('dp', 'fsdp'))
- grad_input: bfloat16 [64, 1024, 1280], P(('dp', 'fsdp'))
- grad_weight_in: float32 [1280, 640], P('dp', 'fsdp')
- grad_weight_conv: float32 [5, 640, 640], P(None, 'dp', 'fsdp')
- grad_weight_out: float32 [640, 1280], P('dp', 'fsdp')
- grad_inner_vectors: float32 [6, 640], P(None, 'fsdp')
- grad_model_vectors: float32 [3, 1280], P(None, 'fsdp')
- type_counts: int32 [25], replicated
The draws below stay inside these ranges and needn't reach their ends.
Inputs may be any that keep to these rules, and one draw needn't show every extreme that they name: `lengths`: one sequence has exactly 1024 residues.
All inputs are finite; a program needn't handle non-finite values.
Results may differ from the reference program's by a relative error of at most 0.0069.
Values may be sent and summed in bfloat16 or wider, within the bound.
No kernel may reach another device: no remote copies, remote signals or barrier semaphores. Data moves between devices by JAX's collectives and lax.ppermute only.
A program may use at most 128 MiB of HBM per device.

```python
import math
import jax
import jax.numpy as jnp
from jax import lax

D = 1280
INNER = 640
KERNEL = 5
DILATION = 32
LENGTH = 1024
TYPES = 25
SEQS = 64


def draw_lengths(key, part):
    first, second = jax.random.split(jax.random.fold_in(key, 11))
    values = jax.random.randint(first, (SEQS,), LENGTH // 4, LENGTH + 1)
    chosen = jax.random.randint(second, (), 0, SEQS)
    return jnp.where(jnp.arange(SEQS) == chosen, LENGTH, values).astype(jnp.int32)


def draw_inner_bias_gains(key, part):
    first, second = jax.random.split(jax.random.fold_in(key, 23))
    gains = jax.random.uniform(first, (6, INNER), jnp.float32, 0.5, 1.5)
    shifts = jax.random.uniform(second, (6, INNER), jnp.float32, -0.9, 0.9)
    is_gain = (jnp.arange(6) % 3 == 1)[:, None]
    return jnp.where(is_gain, gains, shifts).astype(jnp.bfloat16)


def draw_model_bias_gains(key, part):
    first, second = jax.random.split(jax.random.fold_in(key, 37))
    gains = jax.random.uniform(first, (3, D), jnp.float32, 0.5, 1.5)
    shifts = jax.random.uniform(second, (3, D), jnp.float32, -0.9, 0.9)
    is_gain = (jnp.arange(3) == 0)[:, None]
    return jnp.where(is_gain, gains, shifts).astype(jnp.bfloat16)


def place_ends(array, stream_key, least, largest):
    longest = array.shape.index(max(array.shape))
    spots = []
    for shift in (0, 1):
        where = [jax.random.randint(jax.random.fold_in(stream_key, axis), (), 0, length) for axis, length in enumerate(array.shape)]
        where[longest] = (where[longest] + shift) % array.shape[longest]
        spots.append(tuple(where))
    return array.at[spots[0]].set(least).at[spots[1]].set(largest)


def raised(entries, own_key, source, target, shards_of, factor):
    owner, partner = [(jnp.arange(entries.shape[dim]) // (entries.shape[dim] // shards_of)).reshape([-1 if axis == dim else 1 for axis in range(entries.ndim)]) for dim in (source, target)]
    chosen = jax.random.permutation(own_key, shards_of)[partner]
    strong = (owner == chosen) | (owner == (partner + shards_of // 2) % shards_of)
    return jnp.where(strong, factor * entries, entries)


def steps_of(key, shape, cuts, smallest, high):
    def one(axis_at, shards_of):
        heights = jax.random.uniform(jax.random.fold_in(jax.random.fold_in(key, 6), axis_at), (shards_of,), jnp.float32, smallest / len(cuts), high / len(cuts))
        return jnp.repeat(jnp.exp(heights), shape[axis_at] // shards_of).reshape((-1,) + (1,) * (len(shape) - axis_at - 1))

    factor_of = one(*cuts[0])
    for cut in cuts[1:]:
        factor_of = factor_of * one(*cut)
    return factor_of


def noise(own_key, dims, spread, limit, cuts=(), kind=jnp.bfloat16):
    values = spread * jax.random.normal(own_key, dims, jnp.float32)
    if cuts:
        values = values * steps_of(own_key, dims, cuts, -0.22, 0.18)
    return jnp.clip(values, -limit, limit).astype(kind)


def noise_with(own_key, shape, deviation, bound, shards, heavy, kind=jnp.bfloat16):
    result = deviation * jax.random.normal(own_key, shape, jnp.float32)
    if shards:
        result = result * steps_of(own_key, shape, shards, -0.22, 0.18)
    return jnp.clip(raised(result, jax.random.fold_in(own_key, 3), *heavy), -bound, bound).astype(kind)


def setup_inputs(seed: int = 0) -> dict:
    splits = jax.random.split(jax.random.key(seed), 11)
    return {
        "activations": noise(splits[0], (SEQS, LENGTH, D), 1.0, 6.0, ((0, 32),)),
        "cotangent": noise_with(splits[1], (SEQS, LENGTH, D), 1.0, 6.0, ((0, 32),), (0, 2, 32, 2.75)),
        "lengths": draw_lengths(jax.random.fold_in(splits[10], 71), 0),
        "cluster_sizes": place_ends(jax.random.randint(splits[3], (SEQS,), 1, 9), jax.random.fold_in(splits[3], 1), 1, 8).astype(jnp.int32),
        "residue_types": place_ends(jax.random.randint(splits[4], (SEQS, LENGTH), 0, TYPES), jax.random.fold_in(splits[4], 1), 0, TYPES - 1).astype(jnp.int32),
        "input_projection_weight": noise(splits[5], (D, INNER), D ** -0.5, 0.15625, ((0, 4), (1, 8))),
        "weight_conv": noise(splits[6], (KERNEL, INNER, INNER), (KERNEL * INNER) ** -0.5, 0.109375, ((1, 4), (2, 8))),
        "output_projection_weight": noise(splits[7], (INNER, D), INNER ** -0.5, 0.25, ((0, 4), (1, 8))),
        "inner_bias_gains": draw_inner_bias_gains(jax.random.fold_in(splits[10], 71), 0),
        "model_bias_gains": draw_model_bias_gains(jax.random.fold_in(splits[10], 71), 0),
    }


@jax.custom_vjp
def low(v):
    return lax.optimization_barrier(v.astype(jnp.bfloat16)).astype(jnp.float32)

@jax.custom_vjp
def reduced_backward(v):
    return v

def low_keep(v):
    return (low(v), None)

def low_pass(kept, grad):
    return (grad,)

def back_keep(v):
    return (v, None)

def back_low(kept, grad):
    return (low(grad),)
low.defvjp(low_keep, low_pass)
reduced_backward.defvjp(back_keep, back_low)
EPS = 1e-05
PRECISE_MODE = lax.Precision.HIGHEST

def normalize(value, gain, shift):
    mean_value = lax.optimization_barrier(jnp.mean(value, axis=-1, keepdims=True))
    centred = value - mean_value
    variance = lax.optimization_barrier(jnp.mean(centred * centred, axis=-1, keepdims=True))
    return centred * lax.rsqrt(variance + EPS) * gain + shift

def gelu_exact(value):
    return jax.nn.gelu(value, approximate=False)

def dilated(acts, weight_conv):
    reach = DILATION * (KERNEL - 1) // 2
    padded = jnp.pad(acts, ((0, 0), (reach, reach), (0, 0)))
    length = acts.shape[1]
    total = jnp.zeros(acts.shape[:2] + (weight_conv.shape[2],), jnp.float32)
    for tap in range(KERNEL):
        window = padded[:, tap * DILATION:tap * DILATION + length]
        total = total + jnp.einsum('sli,ij->slj', window, weight_conv[tap], precision=PRECISE_MODE)
    return total

def forward(params, inputs, mask):
    input_projection_weight, weight_conv, output_projection_weight, inner_bias_gains, model_bias_gains = params
    first = normalize(inputs, model_bias_gains[0], model_bias_gains[1])
    activation_first = low(gelu_exact(first))
    hidden_state = reduced_backward(jnp.einsum('zja,ax->zjx', activation_first, input_projection_weight, precision=PRECISE_MODE) + inner_bias_gains[0])
    second = normalize(hidden_state, inner_bias_gains[1], inner_bias_gains[2])
    act_one = low(gelu_exact(second) * mask[:, :, None])
    mixed = reduced_backward(dilated(act_one, weight_conv) + inner_bias_gains[3])
    third = normalize(mixed, inner_bias_gains[4], inner_bias_gains[5])
    activation_third = low(gelu_exact(third))
    residual_branch = reduced_backward(jnp.einsum('yxn,nh->yxh', activation_third, output_projection_weight, precision=PRECISE_MODE) + model_bias_gains[2])
    return inputs + residual_branch

def reference(activations, cotangent, lengths, cluster_sizes, residue_types, input_projection_weight, weight_conv, output_projection_weight, inner_bias_gains, model_bias_gains):
    params = (input_projection_weight.astype(jnp.float32), weight_conv.astype(jnp.float32), output_projection_weight.astype(jnp.float32), inner_bias_gains.astype(jnp.float32), model_bias_gains.astype(jnp.float32))
    positions = jnp.arange(LENGTH, dtype=jnp.int32)
    valid = positions[None, :] < lengths[:, None]
    mask = valid.astype(jnp.float32)
    scale = mask[:, :, None] * (1.0 / cluster_sizes.astype(jnp.float32))[:, None, None]
    grad_out = cotangent.astype(jnp.float32) * scale
    group = math.gcd(max(4096 // LENGTH, 1), SEQS)
    blocks = SEQS // group
    inputs = activations.astype(jnp.float32).reshape(blocks, group, LENGTH, D)
    grads_in = grad_out.reshape(blocks, group, LENGTH, D)
    masks = mask.reshape(blocks, group, LENGTH)

    def one_block(totals, items):
        inputs_b, grad_b, mask_b = items
        out_b, pull = jax.vjp(lambda p, xv: forward(p, xv, mask_b), params, inputs_b)
        d_params, d_inputs = pull(grad_b)
        totals = jax.tree.map(lambda a, b: a + b, totals, d_params)
        return (totals, (out_b.astype(jnp.bfloat16), d_inputs.astype(jnp.bfloat16)))
    zeros = jax.tree.map(jnp.zeros_like, params)
    totals, (outs, d_inputs) = lax.scan(one_block, zeros, (inputs, grads_in, masks))
    block_out = outs.reshape(SEQS, LENGTH, D)
    grad_input = d_inputs.reshape(SEQS, LENGTH, D)
    kinds = jnp.arange(TYPES, dtype=jnp.int32)
    hits = (residue_types[:, :, None] == kinds[None, None, :]) & valid[:, :, None]
    type_counts = lax.optimization_barrier(jnp.sum(hits.astype(jnp.int32), axis=(0, 1))).astype(jnp.int32)
    return (block_out, grad_input, totals[0], totals[1], totals[2], totals[3], totals[4], type_counts)
```

```python
import functools

import jax
import jax.numpy as jnp
from jax import lax
from jax.experimental import pallas as pl
from jax.experimental.pallas import tpu as pltpu
from jax.sharding import PartitionSpec as P

KERNEL = 5
DILATION = 32
REACH = DILATION * (KERNEL - 1) // 2
TYPES = 25
FS = 8

EPS = 1e-05
INV_ROOT_TWO = 0.7071067811865476
INV_ROOT_TWO_PI = 0.3989422804014327

BF = jnp.bfloat16
F32 = jnp.float32
NT = (((1,), (1,)), ((), ()))
NN = (((1,), (0,)), ((), ()))
TN = (((0,), (0,)), ((), ()))
VMEM_LIMIT = 60 * 1024 * 1024
ANY = pl.BlockSpec(memory_space=pl.ANY)
SMEM = pl.BlockSpec(memory_space=pltpu.SMEM)


def dot(a, b, dims):
    return lax.dot_general(a, b, dims, preferred_element_type=F32)


def params(n):
    return pltpu.CompilerParams(
        dimension_semantics=("arbitrary",) * n, vmem_limit_bytes=VMEM_LIMIT
    )


def cost(flops, nbytes, trans=0):
    return pl.CostEstimate(flops=int(flops), bytes_accessed=int(nbytes), transcendentals=int(trans))


def whole(shape):
    return pl.BlockSpec(shape, lambda *_: (0,) * len(shape))


def row_mean(v):
    return jnp.mean(v, axis=-1, keepdims=True)


def centre(v):
    centred = v - row_mean(v)
    return centred, lax.rsqrt(row_mean(centred * centred) + EPS)


def gelu_pair(h):
    phi = 0.5 * (1.0 + lax.erf(h * INV_ROOT_TWO))
    dens = jnp.exp(-0.5 * h * h) * INV_ROOT_TWO_PI
    return h * phi, phi + h * dens


def norm_back(scaled, normed, inv):
    return inv * (scaled - row_mean(scaled) - normed * row_mean(scaled * normed))


def fold(v):
    return jnp.sum(v.reshape(v.shape[0] // 8, 8, v.shape[1]), axis=0)


def rows_at(i, size):
    return pl.ds(pl.multiple_of(i * size, size), size)


def xor_perm(n, k):
    return [(i, i ^ k) for i in range(n)]


def blocks_of(me):
    yx, core = me // 2, me % 2
    for k in range(FS // 2):
        for side in range(2):
            yield k, side, (yx ^ k) * 2 + (core if side == 0 else 1 - core)


def first_norm_kernel(x_ref, vec_ref, a_ref, g_ref, *, chunk):
    gain, shift = vec_ref[0:1, :].astype(F32), vec_ref[1:2, :].astype(F32)

    def step(i, _):
        r = rows_at(i, chunk)
        centred, inv = centre(x_ref[r, :].astype(F32))
        a, g = gelu_pair(centred * inv * gain + shift)
        a_ref[r, :] = a.astype(BF)
        g_ref[r, :] = g.astype(BF)
        return 0

    lax.fori_loop(0, x_ref.shape[0] // chunk, step, 0)


def load_in_weight(me_ref, own, sib, dst, sem, wait):
    half = dst.shape[1] // 2
    n = 0
    for k, side, block in blocks_of(me_ref[0]):
        src = own if side == 0 else sib
        for h in range(2):
            c = pltpu.make_async_copy(
                src.at[k, pl.ds(h * 80, 80), :],
                dst.at[pl.ds(pl.multiple_of(block * 80, 16), 80), pl.ds(h * half, half)],
                sem.at[n],
            )
            n += 1
            c.wait() if wait else c.start()


def in_proj_kernel(
    me_ref, len_ref, a0_ref, own, sib, vec_ref, a_ref, g_ref, c_ref, w, sem,
    *, tile, chunk, length,
):
    i = pl.program_id(0)

    @pl.when(i == 0)
    def _():
        load_in_weight(me_ref, own, sib, w, sem, False)
        load_in_weight(me_ref, own, sib, w, sem, True)

    bias, gain, shift = (vec_ref[j : j + 1, :].astype(F32) for j in range(3))
    per = length // tile
    limit = len_ref[i // per] - (i % per) * tile
    for lo in range(0, tile, chunk):
        r = slice(lo, lo + chunk)
        v = dot(a0_ref[r, :], w[...], NT) + bias
        centred, inv = centre(v)
        a, g = gelu_pair(centred * inv * gain + shift)
        keep = lo + lax.broadcasted_iota(jnp.int32, (chunk, 1), 0) < limit
        a_ref[r, :] = jnp.where(keep, a, 0.0).astype(BF)
        g_ref[r, :] = jnp.where(keep, g, 0.0)
        c_ref[r, :] = centred.astype(BF)


def load_conv_weight(me_ref, own, sib, dst, sem, wait, inner):
    n = 0
    for k, side, block in blocks_of(me_ref[0]):
        src = own if side == 0 else sib
        for tap in range(KERNEL):
            c = pltpu.make_async_copy(
                src.at[k, pl.ds(tap * 80, 80), :],
                dst.at[pl.ds(pl.multiple_of(tap * inner + block * 80, 16), 80), :],
                sem.at[n],
            )
            n += 1
            c.wait() if wait else c.start()


def fill_padded(pad, src_ref, length):
    zeros = jnp.zeros((REACH, pad.shape[1]), pad.dtype)
    pad[0:REACH, :] = zeros
    pad[REACH + length : 2 * REACH + length, :] = zeros
    pad[REACH : REACH + length, :] = src_ref[...]


def load_out_weight(me_ref, own, sib, dst, sem, wait):
    n = 0
    for k, side, block in blocks_of(me_ref[0]):
        src = own if side == 0 else sib
        c = pltpu.make_async_copy(
            src.at[k], dst.at[pl.ds(pl.multiple_of(block * 160, 16), 160), :], sem.at[n]
        )
        n += 1
        c.wait() if wait else c.start()


def middle_kernel(
    me_ref, len_ref, size_ref, a1_ref, x_ref, cot_ref, conv_own, conv_sib, out_own, out_sib,
    model_ref, inner_ref, y_ref, gv_ref, keep_ref, send_ref, vin_ref, vmod_ref,
    wc, wo, pad, a2, gy, dw, sem_c, sem_o, *, tile, chunk, length,
):
    i = pl.program_id(0)
    inner = pad.shape[1]
    per = length // tile

    @pl.when(i == 0)
    def _():
        load_conv_weight(me_ref, conv_own, conv_sib, wc, sem_c, False, inner)
        load_out_weight(me_ref, out_own, out_sib, wo, sem_o, False)
        vin_ref[...] = jnp.zeros_like(vin_ref)
        vmod_ref[...] = jnp.zeros_like(vmod_ref)
        dw[...] = jnp.zeros_like(dw)

    @pl.when(i % per == 0)
    def _():
        fill_padded(pad, a1_ref, length)

    @pl.when(i == 0)
    def _():
        load_conv_weight(me_ref, conv_own, conv_sib, wc, sem_c, True, inner)
        load_out_weight(me_ref, out_own, out_sib, wo, sem_o, True)

    seq = i // per
    at = (i % per) * tile
    limit = len_ref[seq] - at
    scale = 1.0 / size_ref[seq].astype(F32)
    bias, gain, shift = (inner_ref[j : j + 1, :].astype(F32) for j in range(3, 6))
    out_bias = model_ref[2:3, :].astype(F32)
    for lo in range(0, tile, chunk):
        r = slice(lo, lo + chunk)
        v = bias
        for tap in range(KERNEL):
            start = pl.multiple_of(at + lo + tap * DILATION, DILATION)
            v = v + dot(pad[pl.ds(start, chunk), :], wc[tap * inner : (tap + 1) * inner, :], NT)
        centred, inv = centre(v)
        normed = centred * inv
        a, g = gelu_pair(normed * gain + shift)
        a2[r, :] = a.astype(BF)
        rows = lo + lax.broadcasted_iota(jnp.int32, (chunk, 1), 0)
        grad = jnp.where(rows < limit, cot_ref[r, :].astype(F32) * scale, 0.0).astype(BF)
        gy[r, :] = grad
        vmod_ref[...] += fold(grad.astype(F32))
        y = dot(a2[r, :], wo[...], NT) + out_bias
        y_ref[r, :] = (x_ref[r, :].astype(F32) + y).astype(BF)
        d = dot(gy[r, :], wo[...], NN) * g
        grad = norm_back(d * gain, normed, inv).astype(BF)
        gv_ref[r, :] = grad
        vin_ref[0] += fold(grad.astype(F32))
        vin_ref[1] += fold(d * normed)
        vin_ref[2] += fold(d)
    dw[...] += dot(gy[...], a2[...], TN)

    @pl.when(i == pl.num_programs(0) - 1)
    def _():
        for k, side, block in blocks_of(me_ref[0]):
            part = dw[pl.ds(pl.multiple_of(block * 160, 16), 160), :]
            dst = keep_ref if side == 0 else send_ref
            dst[k] = part.astype(dst.dtype)


def conv_grad_kernel(me_ref, a1_ref, gv_ref, keep_ref, send_ref, pad, gvt, dw, *, length, seqs):
    tap = pl.program_id(0)

    @pl.when(tap == 0)
    def _():
        zeros = jnp.zeros((REACH, pad.shape[2]), pad.dtype)
        for s in range(seqs):
            pad[s, 0:REACH, :] = zeros
            pad[s, REACH + length : 2 * REACH + length, :] = zeros
            pad[s, REACH : REACH + length, :] = a1_ref[s * length : (s + 1) * length, :]
        gvt[...] = gv_ref[...].T

    total = None
    for s in range(seqs):
        window = pad[s, pl.ds(pl.multiple_of(tap * DILATION, DILATION), length), :]
        part = dot(gvt[:, s * length : (s + 1) * length], window, NN)
        total = part if total is None else total + part
    dw[...] = total
    for k, side, block in blocks_of(me_ref[0]):
        dst = keep_ref if side == 0 else send_ref
        dst[k] = dw[pl.ds(pl.multiple_of(block * 80, 16), 80), :].astype(dst.dtype)


def conv_back_kernel(
    me_ref, gv_ref, g_ref, c_ref, a0_ref, own, sib, vec_ref, _after,
    gu_ref, keep_ref, send_ref, vin_ref, w, pad, dw, sem, *, tile, chunk, length,
):
    i = pl.program_id(0)
    inner = pad.shape[1]
    per = length // tile

    @pl.when(i == 0)
    def _():
        load_conv_weight(me_ref, own, sib, w, sem, False, inner)
        vin_ref[...] = jnp.zeros_like(vin_ref)
        dw[...] = jnp.zeros_like(dw)

    @pl.when(i % per == 0)
    def _():
        fill_padded(pad, gv_ref, length)

    @pl.when(i == 0)
    def _():
        load_conv_weight(me_ref, own, sib, w, sem, True, inner)

    gain = vec_ref[1:2, :].astype(F32)
    at = (i % per) * tile
    for lo in range(0, tile, chunk):
        r = slice(lo, lo + chunk)
        v = None
        for tap in range(KERNEL):
            start = pl.multiple_of(at + lo + (KERNEL - 1 - tap) * DILATION, DILATION)
            part = dot(pad[pl.ds(start, chunk), :], w[tap * inner : (tap + 1) * inner, :], NN)
            v = part if v is None else v + part
        centred = c_ref[r, :].astype(F32)
        inv = lax.rsqrt(row_mean(centred * centred) + EPS)
        normed = centred * inv
        d = v * g_ref[r, :]
        grad = norm_back(d * gain, normed, inv).astype(BF)
        gu_ref[r, :] = grad
        vin_ref[0] += fold(grad.astype(F32))
        vin_ref[1] += fold(d * normed)
        vin_ref[2] += fold(d)
    dw[...] += dot(gu_ref[...], a0_ref[...], TN)

    @pl.when(i == pl.num_programs(0) - 1)
    def _():
        half = dw.shape[1] // 2
        for k, side, block in blocks_of(me_ref[0]):
            dst = keep_ref if side == 0 else send_ref
            for h in range(2):
                part = dw[pl.ds(pl.multiple_of(block * 80, 16), 80), h * half : (h + 1) * half]
                dst[k, h * 80 : (h + 1) * 80, :] = part.astype(dst.dtype)


def first_back_kernel(
    me_ref, len_ref, size_ref, x_ref, cot_ref, gu_ref, g_ref, own, sib, vec_ref,
    gx_ref, vmod_ref, w, sem, *, tile, chunk, length,
):
    i = pl.program_id(0)

    @pl.when(i == 0)
    def _():
        load_in_weight(me_ref, own, sib, w, sem, False)
        vmod_ref[...] = jnp.zeros_like(vmod_ref)
        load_in_weight(me_ref, own, sib, w, sem, True)

    per = length // tile
    seq = i // per
    limit = len_ref[seq] - (i % per) * tile
    scale = 1.0 / size_ref[seq].astype(F32)
    gain = vec_ref[0:1, :].astype(F32)
    for lo in range(0, tile, chunk):
        r = slice(lo, lo + chunk)
        rows = lo + lax.broadcasted_iota(jnp.int32, (chunk, 1), 0)
        centred, inv = centre(x_ref[r, :].astype(F32))
        normed = centred * inv
        d = dot(gu_ref[r, :], w[...], NN) * g_ref[r, :].astype(F32)
        grad = norm_back(d * gain, normed, inv)
        out = jnp.where(rows < limit, cot_ref[r, :].astype(F32) * scale, 0.0)
        gx_ref[r, :] = (out + grad).astype(BF)
        vmod_ref[0] += fold(d * normed)
        vmod_ref[1] += fold(d)


def fs_perm(v, k):
    return lax.ppermute(v, "fsdp", xor_perm(FS, k))


def gather_dp(v):
    me = lax.axis_index("dp")
    got = jnp.stack([v] + [lax.ppermute(v, "dp", xor_perm(4, k)) for k in (1, 2, 3)])
    return jnp.stack([lax.dynamic_index_in_dim(got, me ^ d, 0, keepdims=False) for d in range(4)])


def gather_fs(block):
    rows = block.shape[0]
    h = rows // 32 * 16
    a, b = block[:h], block[h:]
    a1, b2 = fs_perm(a, 2), fs_perm(b, 4)
    a01, b02 = jnp.stack([a, a1]), jnp.stack([b, b2])
    a23, b13 = fs_perm(a01, 4), fs_perm(b02, 2)
    own = jnp.stack(
        [
            jnp.concatenate([a, b]),
            jnp.concatenate([a1, b13[0]]),
            jnp.concatenate([a23[0], b2]),
            jnp.concatenate([a23[1], b13[1]]),
        ]
    )
    return own, fs_perm(own, 1)


def flips(v, bits, me):
    for axis, bit in enumerate(bits):
        v = jnp.where((me // bit) % 2 == 1, jnp.flip(v, axis), v)
    return v


def gather_vectors(v, me):
    for k in (1, 2, 4):
        v = jnp.stack([v, fs_perm(v, k)])
    return flips(v, (4, 2, 1), me)


def sum_all(v, staged):
    if not staged:
        return lax.psum(v, ("dp", "fsdp"))
    for k in (1, 2, 4):
        v = v + fs_perm(v, k)
    for k in (1, 2):
        v = v + lax.ppermute(v, "dp", xor_perm(4, k))
    return v


def scatter_fs(keep, send):
    total = keep + fs_perm(send, 1).astype(F32)
    rows = total.shape[1]
    h = rows // 32 * 16
    a, b = total[:, :h], total[:, h:]
    got_a = fs_perm(jnp.stack([a[1], a[3]]).astype(BF), 2).astype(F32)
    got_b = fs_perm(b[2:4].astype(BF), 4).astype(F32)
    a_last = fs_perm((a[2] + got_a[1]).astype(BF), 4).astype(F32)
    b_last = fs_perm((b[1] + got_b[1]).astype(BF), 2).astype(F32)
    return jnp.concatenate([a[0] + got_a[0] + a_last, b[0] + got_b[0] + b_last])


def scatter_dp(pieces):
    me = lax.axis_index("dp")
    pick = lambda k: lax.dynamic_index_in_dim(pieces, me ^ k, 0, keepdims=False)
    total = pick(0)
    for k in (1, 2, 3):
        total = total + lax.ppermute(pick(k).astype(BF), "dp", xor_perm(4, k)).astype(F32)
    return total


def generic_blocks(full):
    blocks = full.reshape(FS // 2, 2, full.shape[0] // FS, full.shape[1])
    return blocks[:, 0], blocks[:, 1]


def generic_full(keep, send):
    full = jnp.stack([keep, send.astype(F32)], axis=1)
    return full.reshape(FS, -1, full.shape[-1])


def generic_gather(w_in, w_conv, w_out):
    both = lambda w, rows, cols: lax.all_gather(
        lax.all_gather(w, "fsdp", axis=cols, tiled=True), "dp", axis=rows, tiled=True
    )
    w_in, w_conv, w_out = both(w_in, 0, 1), both(w_conv, 1, 2), both(w_out, 0, 1)
    taps, inner = w_conv.shape[0], w_conv.shape[1]
    part = w_in.T.reshape(FS, inner // FS, 2, inner).transpose(0, 2, 1, 3).reshape(-1, inner)
    conv = w_conv.transpose(2, 0, 1).reshape(FS, inner // FS, taps, inner)
    conv = conv.transpose(0, 2, 1, 3).reshape(-1, inner)
    return generic_blocks(part), generic_blocks(conv), generic_blocks(w_out.T)


def generic_scatter(ins, convs, outs):
    scatter = lambda w, rows, cols: lax.psum_scatter(
        lax.psum_scatter(w, "fsdp", scatter_dimension=cols, tiled=True),
        "dp", scatter_dimension=rows, tiled=True,
    )
    d_in, d_conv, d_out = generic_full(*ins), generic_full(*convs), generic_full(*outs)
    inner = d_in.shape[-1]
    d_in = d_in.reshape(FS, 2, -1, inner).transpose(0, 2, 1, 3).reshape(inner, -1).T
    d_conv = d_conv.reshape(FS, KERNEL, -1, inner).transpose(1, 3, 0, 2).reshape(KERNEL, inner, inner)
    return scatter(d_in, 0, 1), scatter(d_conv, 1, 2), scatter(d_out.reshape(-1, inner).T, 0, 1)


def local(
    n_dp,
    n_fs,
    activations,
    cotangent,
    lengths,
    cluster_sizes,
    residue_types,
    w_in,
    w_conv,
    w_out,
    inner_shard,
    model_shard,
):
    seqs, length, model = activations.shape
    inner = w_in.shape[1] * n_fs
    tokens = seqs * length
    x = activations.reshape(tokens, model)
    cot = cotangent.reshape(tokens, model)
    staged = n_dp == 4 and n_fs == FS
    place = lax.axis_index("fsdp")
    me = place.reshape(1) if staged else jnp.zeros((1,), jnp.int32)
    ci, co = inner // FS, model // FS

    if staged:
        flat = jnp.concatenate([inner_shard.reshape(-1), model_shard.reshape(-1)])
        n_vec = flat.shape[0]
        lanes = -(-n_vec // 1024) * 1024
        flat = jnp.pad(flat, (0, lanes - n_vec)).reshape(-1, 128)
        vecs = gather_vectors(flat, place).reshape(FS, lanes)[:, :n_vec]
        inner_vec = vecs[:, : 6 * ci].reshape(FS, 6, ci).transpose(1, 0, 2).reshape(6, inner)
        model_vec = vecs[:, 6 * ci :].reshape(FS, 3, co).transpose(1, 0, 2).reshape(3, model)
    else:
        inner_vec = lax.all_gather(inner_shard, "fsdp", axis=1, tiled=True)
        model_vec = lax.all_gather(model_shard, "fsdp", axis=1, tiled=True)

    positions = jnp.arange(length, dtype=jnp.int32)
    valid = positions[None, :] < lengths[:, None]
    kinds = jnp.arange(TYPES, dtype=jnp.int32)
    hits = (residue_types[:, :, None] == kinds[None, None, :]) & valid[:, :, None]
    counts = jnp.sum(hits.astype(jnp.int32), axis=(0, 1))

    if staged:
        part = gather_dp(w_in.T).transpose(1, 0, 2).reshape(ci, 2, inner)
        in_own, in_sib = gather_fs(part.transpose(1, 0, 2).reshape(2 * ci, inner))
        part = gather_dp(w_conv.transpose(0, 2, 1).reshape(KERNEL * ci, -1))
        conv_own, conv_sib = gather_fs(part.transpose(1, 0, 2).reshape(KERNEL * ci, inner))
        part = gather_dp(w_out.T)
        out_own, out_sib = gather_fs(part.transpose(1, 0, 2).reshape(co, inner))
    else:
        ins, convs, outs = generic_gather(w_in, w_conv, w_out)
        (in_own, in_sib), (conv_own, conv_sib), (out_own, out_sib) = ins, convs, outs

    def sds(shape, dtype):
        return jax.ShapeDtypeStruct(shape, dtype)

    tile = 256
    row = lambda i: (i, 0)
    a0, g0 = pl.pallas_call(
        functools.partial(first_norm_kernel, chunk=128),
        grid=(tokens // tile,),
        in_specs=[pl.BlockSpec((tile, model), row), whole((3, model))],
        out_specs=[pl.BlockSpec((tile, model), row)] * 2,
        out_shape=[sds((tokens, model), BF)] * 2,
        compiler_params=params(1),
        cost_estimate=cost(tokens * model * 60, tokens * model * 6, tokens * model * 2),
        name="first_norm",
    )(x, model_vec)

    tile = 512
    wide, narrow = pl.BlockSpec((tile, model), row), pl.BlockSpec((tile, inner), row)
    a1, g1, c1 = pl.pallas_call(
        functools.partial(in_proj_kernel, tile=tile, chunk=256, length=length),
        grid=(tokens // tile,),
        in_specs=[SMEM, SMEM, wide, ANY, ANY, whole((6, inner))],
        out_specs=[narrow] * 3,
        out_shape=[sds((tokens, inner), d) for d in (BF, F32, BF)],
        scratch_shapes=[pltpu.VMEM((inner, model), BF), pltpu.SemaphoreType.DMA((16,))],
        compiler_params=params(1),
        cost_estimate=cost(2 * tokens * model * inner * 3, tokens * (model + 4 * inner) * 2),
        name="in_proj",
    )(me, lengths, a0, in_own, in_sib, inner_vec)

    per = length // tile
    seq_block = pl.BlockSpec((length, inner), lambda i: (i // per, 0))
    shape = (4, co, inner)
    block_out, gv, out_keep, out_send, vin2, vmod2 = pl.pallas_call(
        functools.partial(middle_kernel, tile=tile, chunk=256, length=length),
        grid=(tokens // tile,),
        in_specs=[SMEM, SMEM, SMEM, seq_block, wide, wide, ANY, ANY, ANY, ANY,
                  whole((3, model)), whole((6, inner))],
        out_specs=[wide, narrow, whole(shape), whole(shape),
                   whole((3, 8, inner)), whole((8, model))],
        out_shape=[sds((tokens, model), BF), sds((tokens, inner), BF), sds(shape, F32), sds(shape, BF),
                   sds((3, 8, inner), F32), sds((8, model), F32)],
        scratch_shapes=[
            pltpu.VMEM((KERNEL * inner, inner), BF),
            pltpu.VMEM((model, inner), BF),
            pltpu.VMEM((length + 2 * REACH, inner), BF),
            pltpu.VMEM((tile, inner), BF),
            pltpu.VMEM((tile, model), BF),
            pltpu.VMEM((model, inner), F32),
            pltpu.SemaphoreType.DMA((40,)),
            pltpu.SemaphoreType.DMA((8,)),
        ],
        compiler_params=params(1),
        cost_estimate=cost(2 * tokens * inner * (KERNEL * inner + 3 * model) * 2, tokens * model * 10),
        name="middle",
    )(me, lengths, cluster_sizes, a1, x, cot, conv_own, conv_sib, out_own, out_sib, model_vec, inner_vec)

    shape = (4, KERNEL * ci, inner)
    conv_keep, conv_send = pl.pallas_call(
        functools.partial(conv_grad_kernel, length=length, seqs=seqs),
        grid=(KERNEL,),
        in_specs=[SMEM, whole((tokens, inner)), whole((tokens, inner))],
        out_specs=[pl.BlockSpec((4, ci, inner), lambda k: (0, k, 0))] * 2,
        out_shape=[sds(shape, F32), sds(shape, BF)],
        scratch_shapes=[
            pltpu.VMEM((seqs, length + 2 * REACH, inner), BF),
            pltpu.VMEM((inner, tokens), BF),
            pltpu.VMEM((inner, inner), F32),
        ],
        compiler_params=params(1),
        cost_estimate=cost(2 * tokens * KERNEL * inner * inner * 1.3, tokens * inner * 4),
        name="conv_grad",
    )(me, a1, gv)

    shape = (4, 2 * ci, inner)
    gu, in_keep, in_send, vin1 = pl.pallas_call(
        functools.partial(conv_back_kernel, tile=tile, chunk=256, length=length),
        grid=(tokens // tile,),
        in_specs=[SMEM, seq_block, narrow, narrow, wide, ANY, ANY, whole((6, inner)), ANY],
        out_specs=[narrow, whole(shape), whole(shape), whole((3, 8, inner))],
        out_shape=[sds((tokens, inner), BF), sds(shape, F32), sds(shape, BF), sds((3, 8, inner), F32)],
        scratch_shapes=[
            pltpu.VMEM((KERNEL * inner, inner), BF),
            pltpu.VMEM((length + 2 * REACH, inner), BF),
            pltpu.VMEM((inner, model), F32),
            pltpu.SemaphoreType.DMA((40,)),
        ],
        compiler_params=params(1),
        cost_estimate=cost(2 * tokens * inner * (KERNEL * inner + model) * 1.5, tokens * inner * 12),
        name="conv_back",
    )(me, gv, g1, c1, a0, conv_own, conv_sib, inner_vec, conv_send)

    early = jnp.concatenate(
        [
            jnp.sum(jnp.concatenate([vin1, vin2]), axis=1).reshape(-1),
            jnp.sum(vmod2, axis=0),
            jnp.pad(counts.astype(F32), (0, 128 - TYPES)),
        ]
    )
    early = sum_all(early.reshape(-1, 128), staged).reshape(-1)
    type_counts = early[-128:][:TYPES].astype(jnp.int32)

    grad_x, vmod0 = pl.pallas_call(
        functools.partial(first_back_kernel, tile=tile, chunk=256, length=length),
        grid=(tokens // tile,),
        in_specs=[SMEM, SMEM, SMEM, wide, wide, narrow, wide, ANY, ANY, whole((3, model))],
        out_specs=[wide, whole((2, 8, model))],
        out_shape=[sds((tokens, model), BF), sds((2, 8, model), F32)],
        scratch_shapes=[pltpu.VMEM((inner, model), BF), pltpu.SemaphoreType.DMA((16,))],
        compiler_params=params(1),
        cost_estimate=cost(2 * tokens * model * inner * 4, tokens * model * 8),
        name="first_back",
    )(me, lengths, cluster_sizes, x, cot, gu, g0, in_own, in_sib, model_vec)
    late = sum_all(jnp.sum(vmod0, axis=1).reshape(-1, 128), staged).reshape(2, model)

    if staged:
        mine = scatter_fs(out_keep, out_send)
        d_out = scatter_dp(mine.reshape(co, n_dp, -1).transpose(1, 0, 2)).T
        mine = scatter_fs(conv_keep, conv_send)
        d_conv = scatter_dp(mine.reshape(KERNEL * ci, n_dp, -1).transpose(1, 0, 2))
        d_conv = d_conv.reshape(KERNEL, ci, -1).transpose(0, 2, 1)
        mine = scatter_fs(in_keep, in_send).reshape(2, ci, inner).transpose(1, 0, 2)
        d_in = scatter_dp(mine.reshape(ci, n_dp, -1).transpose(1, 0, 2)).T
    else:
        d_in, d_conv, d_out = generic_scatter(
            (in_keep, in_send), (conv_keep, conv_send), (out_keep, out_send)
        )

    inner_sums = early[: 6 * inner].reshape(6, inner)
    model_sums = jnp.concatenate([late, early[6 * inner : 6 * inner + model].reshape(1, model)])
    d_inner = lax.dynamic_slice_in_dim(inner_sums, place * inner_shard.shape[1], inner_shard.shape[1], 1)
    d_model = lax.dynamic_slice_in_dim(model_sums, place * model_shard.shape[1], model_shard.shape[1], 1)
    return (
        block_out.reshape(activations.shape),
        grad_x.reshape(activations.shape),
        d_in,
        d_conv,
        d_out,
        d_inner,
        d_model,
        type_counts,
    )


def solution(mesh):
    rows = ("dp", "fsdp")
    return jax.shard_map(
        functools.partial(local, mesh.shape["dp"], mesh.shape["fsdp"]),
        mesh=mesh,
        in_specs=(
            P(rows, None, None),
            P(rows, None, None),
            P(rows),
            P(rows),
            P(rows, None),
            P("dp", "fsdp"),
            P(None, "dp", "fsdp"),
            P("dp", "fsdp"),
            P(None, "fsdp"),
            P(None, "fsdp"),
        ),
        out_specs=(
            P(rows, None, None),
            P(rows, None, None),
            P("dp", "fsdp"),
            P(None, "dp", "fsdp"),
            P("dp", "fsdp"),
            P(None, "fsdp"),
            P(None, "fsdp"),
            P(),
        ),
        check_vma=False,
    )
```

```python
import functools

import jax
import jax.numpy as jnp
from jax import lax
from jax.experimental import pallas as pl
from jax.experimental.pallas import tpu as pltpu
from jax.sharding import PartitionSpec as P

KERNEL = 5
DILATION = 32
REACH = DILATION * (KERNEL - 1) // 2
TYPES = 25
FS = 8

EPS = 1e-05
INV_ROOT_TWO = 0.7071067811865476
INV_ROOT_TWO_PI = 0.3989422804014327

BF = jnp.bfloat16
F32 = jnp.float32
NT = (((1,), (1,)), ((), ()))
NN = (((1,), (0,)), ((), ()))
TN = (((0,), (0,)), ((), ()))
ANY = pl.BlockSpec(memory_space=pl.ANY)
SMEM = pl.BlockSpec(memory_space=pltpu.SMEM)


def dot(a, b, dims):
    return lax.dot_general(a, b, dims, preferred_element_type=F32)


def params(mib):
    return pltpu.CompilerParams(
        dimension_semantics=("arbitrary",), vmem_limit_bytes=mib * 1024 * 1024
    )


def cost(flops, nbytes, trans=0):
    return pl.CostEstimate(
        flops=int(flops / 10), bytes_accessed=int(nbytes / 10), transcendentals=int(trans / 10)
    )


def small(kernel, shapes, scratch=(), mib=20, name=None, **static):
    def call(*args):
        specs = [SMEM if a.dtype == jnp.int32 else whole(a.shape) for a in args]
        return pl.pallas_call(
            functools.partial(kernel, **static),
            grid=(1,),
            in_specs=specs,
            out_specs=[whole(v) for v, _ in shapes],
            out_shape=[jax.ShapeDtypeStruct(*v) for v in shapes],
            scratch_shapes=[pltpu.VMEM(*v) for v in scratch],
            compiler_params=params(mib),
            name=name,
        )(*args)

    return call


def whole(shape):
    return pl.BlockSpec(shape, lambda *_: (0,) * len(shape))


def row_mean(v):
    return jnp.mean(v, axis=-1, keepdims=True)


def centre(v):
    centred = v - row_mean(v)
    return centred, lax.rsqrt(row_mean(centred * centred) + EPS)


def gelu_pair(h):
    phi = 0.5 * (1.0 + lax.erf(h * INV_ROOT_TWO))
    dens = jnp.exp(-0.5 * h * h) * INV_ROOT_TWO_PI
    return h * phi, phi + h * dens


def norm_back(scaled, normed, inv):
    return inv * (scaled - row_mean(scaled) - normed * row_mean(scaled * normed))


def fold(v):
    return jnp.sum(v.reshape(v.shape[0] // 8, 8, v.shape[1]), axis=0)


def rows_at(i, size):
    return pl.ds(pl.multiple_of(i * size, size), size)


def xor_perm(n, k):
    return [(i, i ^ k) for i in range(n)]


def blocks_of(me):
    yx, core = me // 2, me % 2
    for k in range(FS // 2):
        for side in range(2):
            yield k, side, (yx ^ k) * 2 + (core if side == 0 else 1 - core)


def first_norm_kernel(x_ref, vec_ref, *refs, chunk):
    a_ref, g_ref = refs[-2:]
    gain, shift = vec_ref[0:1, :], vec_ref[1:2, :]

    def step(i, _):
        r = rows_at(i, chunk)
        centred, inv = centre(x_ref[r, :].astype(F32))
        a, g = gelu_pair(centred * inv * gain + shift)
        a_ref[r, :] = a.astype(BF)
        g_ref[r, :] = g.astype(BF)
        return 0

    lax.fori_loop(0, x_ref.shape[0] // chunk, step, 0)


def put_block(k, side, rows, part, mine_ref, keep_ref, send_ref):
    if side == 1:
        send_ref[k, rows, :] = part.astype(BF)
    elif k == 0:
        mine_ref[0, rows, :] = part
    else:
        keep_ref[k - 1, rows, :] = part.astype(BF)


def load_in_weight(me_ref, own, sib, dst, sem, wait):
    half = dst.shape[1] // 2
    n = 0
    for k, side, block in blocks_of(me_ref[0]):
        src = own if side == 0 else sib
        for h in range(2):
            c = pltpu.make_async_copy(
                src.at[k, pl.ds(h * 80, 80), :],
                dst.at[pl.ds(pl.multiple_of(block * 80, 16), 80), pl.ds(h * half, half)],
                sem.at[n],
            )
            n += 1
            c.wait() if wait else c.start()


def in_proj_kernel(
    me_ref, len_ref, a0_ref, own, sib, vec_ref, *refs, tile, chunk, length, first
):
    a_ref, g_ref, c_ref, w, sem = refs[-5:]
    i = pl.program_id(0)

    @pl.when(i == 0)
    def _():
        load_in_weight(me_ref, own, sib, w, sem, False)
        load_in_weight(me_ref, own, sib, w, sem, True)

    bias, gain, shift = (vec_ref[j : j + 1, :] for j in range(3))
    per = length // tile
    limit = len_ref[first + i // per] - (i % per) * tile
    for lo in range(0, tile, chunk):
        r = slice(lo, lo + chunk)
        v = dot(a0_ref[r, :], w[...], NT) + bias
        centred, inv = centre(v)
        a, g = gelu_pair(centred * inv * gain + shift)
        keep = lo + lax.broadcasted_iota(jnp.int32, (chunk, 1), 0) < limit
        a_ref[r, :] = jnp.where(keep, a, 0.0).astype(BF)
        g_ref[r, :] = jnp.where(keep, g, 0.0)
        c_ref[r, :] = centred.astype(BF)


def load_conv_weight(me_ref, own, sib, dst, sem, wait, inner):
    n = 0
    for k, side, block in blocks_of(me_ref[0]):
        src = own if side == 0 else sib
        for tap in range(KERNEL):
            c = pltpu.make_async_copy(
                src.at[k, pl.ds(tap * 80, 80), :],
                dst.at[pl.ds(pl.multiple_of(tap * inner + block * 80, 16), 80), :],
                sem.at[n],
            )
            n += 1
            c.wait() if wait else c.start()


def fill_padded(pad, src_ref, length):
    zeros = jnp.zeros((REACH, pad.shape[1]), pad.dtype)
    pad[0:REACH, :] = zeros
    pad[REACH + length : 2 * REACH + length, :] = zeros
    pad[REACH : REACH + length, :] = src_ref[...]


def load_out_weight(me_ref, own, sib, dst, sem, wait):
    n = 0
    for k, side, block in blocks_of(me_ref[0]):
        src = own if side == 0 else sib
        c = pltpu.make_async_copy(
            src.at[k, pl.ds(KERNEL * 80, 160), :],
            dst.at[pl.ds(pl.multiple_of(block * 160, 16), 160), :],
            sem.at[n],
        )
        n += 1
        c.wait() if wait else c.start()


def middle_kernel(
    me_ref, len_ref, size_ref, a1_ref, x_ref, cot_ref, own, sib,
    model_ref, inner_ref, y_ref, gv_ref, mine_ref, keep_ref, send_ref, vin_ref, vmod_ref,
    wc, wo, pad, a2, gy, dw, sem_c, sem_o, *, tile, chunk, length,
):
    i = pl.program_id(0)
    inner = pad.shape[1]
    per = length // tile

    @pl.when(i == 0)
    def _():
        load_conv_weight(me_ref, own, sib, wc, sem_c, False, inner)
        load_out_weight(me_ref, own, sib, wo, sem_o, False)
        vin_ref[...] = jnp.zeros_like(vin_ref)
        vmod_ref[...] = jnp.zeros_like(vmod_ref)
        dw[...] = jnp.zeros_like(dw)

    @pl.when(i % per == 0)
    def _():
        fill_padded(pad, a1_ref, length)

    @pl.when(i == 0)
    def _():
        load_conv_weight(me_ref, own, sib, wc, sem_c, True, inner)
        load_out_weight(me_ref, own, sib, wo, sem_o, True)

    seq = i // per
    at = (i % per) * tile
    limit = len_ref[seq] - at
    scale = 1.0 / size_ref[seq].astype(F32)
    bias, gain, shift = (inner_ref[j : j + 1, :] for j in range(3, 6))
    out_bias = model_ref[2:3, :]
    for lo in range(0, tile, chunk):
        r = slice(lo, lo + chunk)
        v = bias
        for tap in range(KERNEL):
            start = pl.multiple_of(at + lo + tap * DILATION, DILATION)
            v = v + dot(pad[pl.ds(start, chunk), :], wc[tap * inner : (tap + 1) * inner, :], NT)
        centred, inv = centre(v)
        normed = centred * inv
        a, g = gelu_pair(normed * gain + shift)
        a2[r, :] = a.astype(BF)
        rows = lo + lax.broadcasted_iota(jnp.int32, (chunk, 1), 0)
        grad = jnp.where(rows < limit, cot_ref[r, :].astype(F32) * scale, 0.0).astype(BF)
        gy[r, :] = grad
        vmod_ref[...] += fold(grad.astype(F32))
        y = dot(a2[r, :], wo[...], NT) + out_bias
        y_ref[r, :] = (x_ref[r, :].astype(F32) + y).astype(BF)
        d = dot(gy[r, :], wo[...], NN) * g
        grad = norm_back(d * gain, normed, inv).astype(BF)
        gv_ref[r, :] = grad
        vin_ref[0] += fold(grad.astype(F32))
        vin_ref[1] += fold(d * normed)
        vin_ref[2] += fold(d)
    dw[...] += dot(gy[...], a2[...], TN)

    @pl.when(i == pl.num_programs(0) - 1)
    def _():
        for k, side, block in blocks_of(me_ref[0]):
            part = dw[pl.ds(pl.multiple_of(block * 160, 16), 160), :]
            put_block(k, side, slice(None), part, mine_ref, keep_ref, send_ref)


def conv_grad_kernel(
    me_ref, a1_ref, gv_ref, omine_ref, okeep_ref, osend_ref, mine_ref, keep_ref, send_ref,
    pad, gvt, dw, *, length, seqs,
):
    tap = pl.program_id(0)

    @pl.when(tap == 0)
    def _():
        zeros = jnp.zeros((REACH, pad.shape[2]), pad.dtype)
        for s in range(seqs):
            pad[s, 0:REACH, :] = zeros
            pad[s, REACH + length : 2 * REACH + length, :] = zeros
            pad[s, REACH : REACH + length, :] = a1_ref[s * length : (s + 1) * length, :]
        gvt[...] = gv_ref[...].T

    @pl.when(tap < KERNEL)
    def _():
        total = None
        for s in range(seqs):
            window = pad[s, pl.ds(pl.multiple_of(tap * DILATION, DILATION), length), :]
            part = dot(gvt[:, s * length : (s + 1) * length], window, NN)
            total = part if total is None else total + part
        dw[...] = total
        for k, side, block in blocks_of(me_ref[0]):
            part = dw[pl.ds(pl.multiple_of(block * 80, 16), 80), :]
            put_block(k, side, slice(None), part, mine_ref, keep_ref, send_ref)

    @pl.when(tap >= KERNEL)
    def _():
        mine_ref[...] = omine_ref[...]
        keep_ref[...] = okeep_ref[...]
        send_ref[...] = osend_ref[...]


def conv_back_kernel(
    me_ref, gv_ref, g_ref, c_ref, own, sib, vec_ref, *refs, tile, chunk, last
):
    if last:
        gu0_ref, a00_ref, a01_ref = refs[:3]
        gu_ref, vin_ref, mine_ref, keep_ref, send_ref, w, pad, sem, dw = refs[3:]
    else:
        gu_ref, vin_ref, w, pad, sem = refs[-5:]
    i = pl.program_id(0)
    inner = pad.shape[1]

    @pl.when(i == 0)
    def _():
        load_conv_weight(me_ref, own, sib, w, sem, False, inner)
        vin_ref[...] = jnp.zeros_like(vin_ref)
        if last:
            dw[...] = jnp.zeros_like(dw)
        fill_padded(pad, gv_ref, gv_ref.shape[0])
        load_conv_weight(me_ref, own, sib, w, sem, True, inner)

    gain = vec_ref[1:2, :]
    at = i * tile
    for lo in range(0, tile, chunk):
        r = slice(lo, lo + chunk)
        v = None
        for tap in range(KERNEL):
            start = pl.multiple_of(at + lo + (KERNEL - 1 - tap) * DILATION, DILATION)
            part = dot(pad[pl.ds(start, chunk), :], w[tap * inner : (tap + 1) * inner, :], NN)
            v = part if v is None else v + part
        centred = c_ref[r, :].astype(F32)
        inv = lax.rsqrt(row_mean(centred * centred) + EPS)
        normed = centred * inv
        d = v * g_ref[r, :]
        grad = norm_back(d * gain, normed, inv).astype(BF)
        gu_ref[r, :] = grad
        vin_ref[0] += fold(grad.astype(F32))
        vin_ref[1] += fold(d * normed)
        vin_ref[2] += fold(d)
    if last:
        part = dot(gu_ref[...], a01_ref[...], TN)
        dw[...] += part + dot(gu0_ref[...], a00_ref[...], TN)

        @pl.when(i == pl.num_programs(0) - 1)
        def _():
            half = dw.shape[1] // 2
            for k, side, block in blocks_of(me_ref[0]):
                for h in range(2):
                    rows = pl.ds(pl.multiple_of(block * 80, 16), 80)
                    part = dw[rows, h * half : (h + 1) * half]
                    at = slice(h * 80, (h + 1) * 80)
                    put_block(k, side, at, part, mine_ref, keep_ref, send_ref)


def first_back_kernel(
    me_ref, len_ref, size_ref, x_ref, cot_ref, gu_ref, g_ref, own, sib, vec_ref, *refs,
    tile, chunk, length, first,
):
    gx_ref, vmod_ref, w, sem = refs[-4:]
    i = pl.program_id(0)

    @pl.when(i == 0)
    def _():
        load_in_weight(me_ref, own, sib, w, sem, False)
        vmod_ref[...] = jnp.zeros_like(vmod_ref)
        load_in_weight(me_ref, own, sib, w, sem, True)

    per = length // tile
    seq = first + i // per
    limit = len_ref[seq] - (i % per) * tile
    scale = 1.0 / size_ref[seq].astype(F32)
    gain = vec_ref[0:1, :]
    for lo in range(0, tile, chunk):
        r = slice(lo, lo + chunk)
        rows = lo + lax.broadcasted_iota(jnp.int32, (chunk, 1), 0)
        centred, inv = centre(x_ref[r, :].astype(F32))
        normed = centred * inv
        d = dot(gu_ref[r, :], w[...], NN) * g_ref[r, :].astype(F32)
        grad = norm_back(d * gain, normed, inv)
        out = jnp.where(rows < limit, cot_ref[r, :].astype(F32) * scale, 0.0)
        gx_ref[r, :] = (out + grad).astype(BF)
        vmod_ref[0] += fold(d * normed)
        vmod_ref[1] += fold(d)


def shards_kernel(w_in, w_conv, w_out, inner_ref, model_ref, in_ref, rest_ref, both_ref, vec_ref):
    rows = w_in.shape[1]
    width = w_conv.shape[1]
    part = w_in[...].T
    in_ref[...] = part
    both_ref[:, : part.shape[1]] = part
    cut = part.shape[1]
    out = w_out[...].T
    parts = [w_conv[tap].T for tap in range(KERNEL)] + [out[:rows], out[rows:]]
    for t, part in enumerate(parts):
        rest_ref[:, t * width : (t + 1) * width] = part
        both_ref[:, cut + t * width : cut + (t + 1) * width] = part
    vec_ref[...] = jnp.zeros_like(vec_ref)
    vec_ref[0:6, :rows] = inner_ref[...].astype(F32)
    vec_ref[8:11, :] = model_ref[...].astype(F32)


def in_block_kernel(z_ref, p0, p1, p2, p3, vec_ref, got_ref, out_ref, pieces):
    rows, width = p0.shape
    half = out_ref.shape[1] // 2
    z = z_ref[0]
    for k, p in enumerate((p0, p1, p2, p3)):
        pieces[k] = p[:, :width].astype(F32)
    for d in range(4):
        row, lane = d // 2 * rows, d % 2 * half
        out_ref[row : row + rows, lane : lane + half] = pieces[z ^ d].astype(BF)
    co = vec_ref.shape[1]
    both = jnp.concatenate([vec_ref[...], got_ref[...]], axis=1).astype(BF)
    out_ref[2 * rows :, : 2 * co] = both
    out_ref[2 * rows :, 2 * co :] = jnp.zeros((16, out_ref.shape[1] - 2 * co), BF)


def unpack_kernel(
    me_ref, z_ref, b0, b1, b2, b3, p0, p1, p2, p3, in_ref, inner_ref, model_ref, a_ref, b_ref,
    vecs, pieces, block, *, cut,
):
    rows = p0.shape[0]
    width = block.shape[1] // 4
    z = z_ref[0]
    for k, (p, lane) in enumerate(zip((p0, p1, p2, p3), cut)):
        pieces[k] = p[:, lane:].astype(F32)
    for d in range(4):
        piece = pieces[z ^ d]
        for t in range(block.shape[0] // rows):
            block[t * rows : (t + 1) * rows, d * width : (d + 1) * width] = piece[
                :, t * width : (t + 1) * width
            ]
    h = a_ref.shape[0]
    a_ref[...] = block[:h].astype(BF)
    b_ref[...] = block[h:].astype(BF)
    blocks = (b0, b1, b2, b3)
    n = in_ref.shape[1]
    co = model_ref.shape[1] // FS
    ci = inner_ref.shape[1] // FS
    for k in range(4):
        in_ref[k] = blocks[k][:n, :]
    for k, side, place in blocks_of(me_ref[0]):
        vecs[place] = blocks[k][n:, side * co : (side + 1) * co].astype(F32)
    for f in range(FS):
        inner_ref[:, f * ci : (f + 1) * ci] = vecs[f, 0:8, :ci]
        model_ref[:, f * co : (f + 1) * co] = vecs[f, 8:16, :]


def pack_kernel(
    z_ref, keep_ref, got_ref, got_a_ref, got_b_ref, a_ref, b_ref, own_ref, o1, o2, o3, mine, pieces,
    *, groups, rows,
):
    h = a_ref.shape[0]
    first = keep_ref[0] + got_ref[0].astype(F32)
    mine[:h, :] = first[:h] + got_a_ref[0].astype(F32) + a_ref[...].astype(F32)
    mine[h:, :] = first[h:] + got_b_ref[0].astype(F32) + b_ref[...].astype(F32)
    for d in range(4):
        col = 0
        for width, starts in groups:
            for row, lane in starts[d]:
                pieces[d, :, col : col + width] = mine[row : row + rows, lane : lane + width]
                col += width
    z = z_ref[0]
    own_ref[...] = pieces[z]
    for k, out in ((1, o1), (2, o2), (3, o3)):
        out[...] = pieces[z ^ k].astype(BF)


def sums_kernel(me_ref, vin1a, vin1b, vin2, vmod0a, vmod0b, vmod2, counts, keep_ref, send_ref, inner, model):
    down = lambda v: jnp.sum(v, axis=0, keepdims=True)
    for j in range(3):
        inner[j : j + 1, :] = down(vin1a[j] + vin1b[j])
        inner[3 + j : 4 + j, :] = down(vin2[j])
    for j in range(2):
        model[j : j + 1, :] = down(vmod0a[j] + vmod0b[j])
    model[2:3, :] = down(vmod2[...])
    ci, co = inner.shape[1] // FS, model.shape[1] // FS
    keep_ref[...] = jnp.zeros_like(keep_ref)
    send_ref[...] = jnp.zeros_like(send_ref)
    yx, core = me_ref[0] // 2, me_ref[0] % 2
    for f in range(FS):
        k = yx ^ (f // 2)
        for dst, mine in ((keep_ref, core == f % 2), (send_ref, core != f % 2)):

            @pl.when(mine)
            def _():
                dst[k, 0:6, :ci] = inner[0:6, f * ci : (f + 1) * ci]
                dst[k, 8:11, :] = model[0:3, f * co : (f + 1) * co]
                dst[k, 11:12, :128] = counts[...]


def last_pack_kernel(
    z_ref, mine_ref, got_ref, got_a_ref, got_b_ref, a_ref, b_ref, v0, v1, v2, v3,
    own_ref, vec_ref, o1, o2, o3, mine, pieces,
):
    h = a_ref.shape[0]
    first = mine_ref[0] + got_ref[0].astype(F32)
    mine[:h, :] = first[:h] + got_a_ref[0].astype(F32) + a_ref[...].astype(F32)
    mine[h:, :] = first[h:] + got_b_ref[0].astype(F32) + b_ref[...].astype(F32)
    rows, width = own_ref.shape
    for d in range(4):
        row, lane = d // 2 * rows, d % 2 * width
        pieces[d] = mine[row : row + rows, lane : lane + width]
    vec = (v0[...] + v1[...]) + (v2[...] + v3[...])
    vec_ref[...] = vec
    high = vec.astype(BF)
    low = (vec - high.astype(F32)).astype(BF)
    z = z_ref[0]
    own_ref[...] = pieces[z]
    for k, out in ((1, o1), (2, o2), (3, o3)):
        out[:rows, :] = pieces[z ^ k].astype(BF)
        out[rows:, :] = jnp.concatenate([high, low], axis=1)


def last_kernel(own, vec, g1, g2, g3, in_ref, inner_ref, model_ref, counts_ref):
    rows = own.shape[0]
    total, sums = own[...], vec[...]
    co = vec.shape[1]
    for g in (g1, g2, g3):
        total = total + g[:rows, :].astype(F32)
        part = g[rows:, :].astype(F32)
        sums = sums + (part[:, :co] + part[:, co:])
    in_ref[...] = total.T
    inner_ref[...] = sums[0:6, : inner_ref.shape[1]]
    model_ref[...] = sums[8:11, :]
    counts_ref[...] = sums[11:12, :128]


def rest_kernel(own, g1, g2, g3, conv_ref, out_ref):
    total = own[...] + g1[...].astype(F32) + (g2[...].astype(F32) + g3[...].astype(F32))
    width = conv_ref.shape[1]
    for tap in range(KERNEL):
        conv_ref[tap] = total[:, tap * width : (tap + 1) * width].T
    cut = KERNEL * width
    out_ref[...] = jnp.concatenate([total[:, cut : cut + width], total[:, cut + width :]]).T


def fs_perm(v, k):
    return lax.ppermute(v, "fsdp", xor_perm(FS, k))


def tie(*values):
    return lax.optimization_barrier(values)


def dp_perm(v, k):
    return lax.ppermute(v, "dp", xor_perm(4, k))


def split_rows(block, axis=0):
    h = block.shape[axis] // 32 * 16
    return lax.slice_in_dim(block, 0, h, axis=axis), lax.slice_in_dim(block, h, None, axis=axis)


def scatter_first(keep, got):
    keep_a, keep_b = split_rows(keep, 1)
    got_a, got_b = split_rows(got, 1)
    plus = lambda a, b: (a.astype(F32) + b.astype(F32)).astype(BF)
    send_a = jnp.stack([plus(keep_a[k - 1], got_a[k]) for k in (1, 3)])
    return fs_perm(send_a, 2), fs_perm(plus(keep_b[1:], got_b[2:]), 4)


def scatter_second(keep, got, from_a, from_b):
    keep_a, keep_b = split_rows(keep, 1)
    got_a, got_b = split_rows(got, 1)
    send_a = total_of([keep_a[1], got_a[2], from_a[1]])
    send_b = total_of([keep_b[0], got_b[1], from_b[1]])
    return fs_perm(send_a.astype(BF), 4), fs_perm(send_b.astype(BF), 2)


def pack(z, mine, got, from_a, from_b, last_a, last_b, groups, rows):
    total, cols = mine.shape[1:]
    h = last_a.shape[0]
    lanes = sum(width * len(starts[0]) for width, starts in groups)
    shape = (rows, lanes)
    return pl.pallas_call(
        functools.partial(pack_kernel, groups=groups, rows=rows),
        grid=(1,),
        in_specs=[SMEM] + [whole((1, n, cols)) for n in (total, total, h, total - h)]
        + [whole((h, cols)), whole((total - h, cols))],
        out_specs=[whole(shape)] * 4,
        out_shape=[jax.ShapeDtypeStruct(shape, d) for d in (F32, BF, BF, BF)],
        scratch_shapes=[pltpu.VMEM((total, cols), F32), pltpu.VMEM((4,) + shape, F32)],
        compiler_params=params(20),
        cost_estimate=cost(total * cols * 8, total * cols * 12),
        name="pack",
    )(z.reshape(1), mine, got, from_a, from_b, last_a, last_b)


def total_of(terms):
    return functools.reduce(lambda a, b: a + b, [t.astype(F32) for t in terms])


def generic_blocks(full):
    blocks = full.reshape(FS // 2, 2, full.shape[0] // FS, full.shape[1])
    return blocks[:, 0], blocks[:, 1]


def generic_full(keep, send):
    full = jnp.stack([keep, send.astype(F32)], axis=1)
    return full.reshape(FS, -1, full.shape[-1])


def generic_gather(w_in, w_conv, w_out):
    both = lambda w, rows, cols: lax.all_gather(
        lax.all_gather(w, "fsdp", axis=cols, tiled=True), "dp", axis=rows, tiled=True
    )
    w_in, w_conv, w_out = both(w_in, 0, 1), both(w_conv, 1, 2), both(w_out, 0, 1)
    taps, inner = w_conv.shape[0], w_conv.shape[1]
    part = w_in.T.reshape(FS, inner // FS, 2, inner).transpose(0, 2, 1, 3).reshape(-1, inner)
    conv = w_conv.transpose(2, 0, 1).reshape(FS, inner // FS, taps, inner)
    conv = conv.transpose(0, 2, 1, 3).reshape(-1, inner)
    pairs = zip(generic_blocks(conv), generic_blocks(w_out.T))
    return generic_blocks(part), [jnp.concatenate(p, axis=1) for p in pairs]


def generic_scatter(ins, rest):
    scatter = lambda w, rows, cols: lax.psum_scatter(
        lax.psum_scatter(w, "fsdp", scatter_dimension=cols, tiled=True),
        "dp", scatter_dimension=rows, tiled=True,
    )
    d_in, rest = generic_full(*ins), generic_full(*rest)
    inner = d_in.shape[-1]
    d_conv, d_out = rest[:, : KERNEL * inner // FS], rest[:, KERNEL * inner // FS :]
    d_in = d_in.reshape(FS, 2, -1, inner).transpose(0, 2, 1, 3).reshape(inner, -1).T
    d_conv = d_conv.reshape(FS, KERNEL, -1, inner).transpose(1, 3, 0, 2).reshape(KERNEL, inner, inner)
    return scatter(d_in, 0, 1), scatter(d_conv, 1, 2), scatter(d_out.reshape(-1, inner).T, 0, 1)


def local(
    n_dp,
    n_fs,
    activations,
    cotangent,
    lengths,
    cluster_sizes,
    residue_types,
    w_in,
    w_conv,
    w_out,
    inner_shard,
    model_shard,
):
    seqs, length, model = activations.shape
    inner = w_in.shape[1] * n_fs
    tokens = seqs * length
    x = activations.reshape(tokens, model)
    cot = cotangent.reshape(tokens, model)
    staged = n_dp == 4 and n_fs == FS
    place, z = lax.axis_index("fsdp"), lax.axis_index("dp")
    me = place.reshape(1) if staged else jnp.zeros((1,), jnp.int32)
    ci, co = inner // FS, model // FS

    positions = jnp.arange(length, dtype=jnp.int32)
    valid = positions[None, :] < lengths[:, None]
    kinds = jnp.arange(TYPES, dtype=jnp.int32)
    hits = (residue_types[:, :, None] == kinds[None, None, :]) & valid[:, :, None]
    counts = jnp.sum(hits.astype(jnp.int32), axis=(0, 1))

    def sds(shape, dtype):
        return jax.ShapeDtypeStruct(shape, dtype)

    tile = 512
    per = length // tile
    row = lambda i: (i, 0)

    def first_norm(part, parts, vec, old):
        size, steps = 256, tokens // parts // 256
        block = pl.BlockSpec((size, model), lambda i: (part * steps + i, 0))
        return pl.pallas_call(
            functools.partial(first_norm_kernel, chunk=128),
            grid=(steps,),
            in_specs=[block, whole((8, model))] + [ANY] * len(old),
            out_specs=[block] * 2,
            out_shape=[sds((tokens, model), BF)] * 2,
            input_output_aliases={2: 0, 3: 1} if old else {},
            compiler_params=params(60),
            cost_estimate=cost(
                tokens * model * 60 / parts, tokens * model * 6 / parts, tokens * model * 2 / parts
            ),
            name="first_norm",
        )(x, vec, *old)

    def in_proj(part, parts, a0, own, sib, vec, old):
        steps = tokens // parts // tile
        wide = pl.BlockSpec((tile, model), lambda i: (part * steps + i, 0))
        narrow = pl.BlockSpec((tile, inner), lambda i: (part * steps + i, 0))
        return pl.pallas_call(
            functools.partial(
                in_proj_kernel, tile=tile, chunk=256, length=length, first=part * seqs // parts
            ),
            grid=(steps,),
            in_specs=[SMEM, SMEM, wide, ANY, ANY, whole((8, inner))] + [ANY] * len(old),
            out_specs=[narrow] * 3,
            out_shape=[sds((tokens, inner), d) for d in (BF, F32, BF)],
            input_output_aliases={6: 0, 7: 1, 8: 2} if old else {},
            scratch_shapes=[pltpu.VMEM((inner, model), BF), pltpu.SemaphoreType.DMA((16,))],
            compiler_params=params(60),
            cost_estimate=cost(
                2 * tokens * model * inner * 3 / parts, tokens * (model + 4 * inner) * 2 / parts
            ),
            name="in_proj",
        )(me, lengths, a0, own, sib, vec, *old)

    if staged:
        cut, width = model // 4, inner // 4
        lanes = (KERNEL + 2) * width
        shapes = [((ci, cut), BF), ((ci, lanes), BF), ((ci, cut + lanes), BF), ((16, co), F32)]
        in_t, rest_t, both, vec = small(shards_kernel, shapes, name="shards")(
            w_in, w_conv, w_out, inner_shard, model_shard
        )
        got = [fs_perm(vec, 1), dp_perm(both, 1), dp_perm(in_t, 2), dp_perm(both, 3)]
        vec, both, in_t, rest_t, *got = tie(vec, both, in_t, rest_t, *got)

        place_z = z.reshape(1)
        (block,) = small(
            in_block_kernel, [((2 * ci + 16, inner), BF)], [((4, ci, cut), F32)], name="in_block"
        )(place_z, in_t, got[1], got[2], got[3], vec, got[0])
        blocks = [block] + [fs_perm(block, k) for k in (2, 4, 6)]
        tied = tie(rest_t, got[1], dp_perm(rest_t, 2), got[3], *blocks)
        rest_z, blocks = tied[:4], tied[4:]

        h = lanes // width * ci // 32 * 16
        shapes = [
            ((4, 2 * ci, inner), BF),
            ((8, inner), F32),
            ((8, model), F32),
            ((h, inner), BF),
            ((lanes // width * ci - h, inner), BF),
        ]
        in_own, inner_vec, model_vec, a, b = small(
            unpack_kernel,
            shapes,
            [((FS, 16, co), F32), ((4, ci, lanes), F32), ((lanes // width * ci, inner), F32)],
            cut=(0, cut, 0, cut),
            name="unpack",
        )(me, place_z, *blocks, *rest_z)
        in_sib = fs_perm(in_own, 1)
        w_a1, w_b2 = fs_perm(a, 2), fs_perm(b, 4)
        a0, g0 = first_norm(0, 1, model_vec, [])
        in_own, in_sib, w_a1, w_b2, a0, g0 = tie(in_own, in_sib, w_a1, w_b2, a0, g0)

        second = [fs_perm(a, 4), fs_perm(w_a1, 4), fs_perm(b, 2), fs_perm(w_b2, 2)]
        a1, g1, c1 = in_proj(0, 1, a0, in_own, in_sib, inner_vec, [])
        a1, g1, c1, a2, a3, b1, b3 = tie(a1, g1, c1, *second)
        pairs = [(a, b), (w_a1, b1), (a2, w_b2), (a3, b3)]
        own = jnp.stack([jnp.concatenate(p) for p in pairs])
        own, a1, g1, c1 = tie(own, a1, g1, c1)
        sib = fs_perm(own, 1)
    else:
        gather = lambda v: lax.all_gather(v, "fsdp", axis=1, tiled=True).astype(F32)
        inner_vec = jnp.pad(gather(inner_shard), ((0, 2), (0, 0)))
        model_vec = jnp.pad(gather(model_shard), ((0, 5), (0, 0)))
        (in_own, in_sib), (own, sib) = generic_gather(w_in, w_conv, w_out)
        a0, g0 = first_norm(0, 1, model_vec, [])
        a1, g1, c1 = in_proj(0, 1, a0, in_own, in_sib, inner_vec, [])

    wide, narrow = pl.BlockSpec((tile, model), row), pl.BlockSpec((tile, inner), row)
    shapes = [((1, co, inner), F32), ((3, co, inner), BF), ((4, co, inner), BF)]
    block_out, gv, *out_parts, vin2, vmod2 = pl.pallas_call(
        functools.partial(middle_kernel, tile=tile, chunk=256, length=length),
        grid=(tokens // tile,),
        in_specs=[SMEM, SMEM, SMEM, pl.BlockSpec((length, inner), lambda i: (i // per, 0)),
                  wide, wide, ANY, ANY, whole((8, model)), whole((8, inner))],
        out_specs=[wide, narrow, *(whole(v) for v, _ in shapes),
                   whole((3, 8, inner)), whole((8, model))],
        out_shape=[sds((tokens, model), BF), sds((tokens, inner), BF), *(sds(*v) for v in shapes),
                   sds((3, 8, inner), F32), sds((8, model), F32)],
        scratch_shapes=[
            pltpu.VMEM((KERNEL * inner, inner), BF),
            pltpu.VMEM((model, inner), BF),
            pltpu.VMEM((length + 2 * REACH, inner), BF),
            pltpu.VMEM((tile, inner), BF),
            pltpu.VMEM((tile, model), BF),
            pltpu.VMEM((model, inner), F32),
            pltpu.SemaphoreType.DMA((40,)),
            pltpu.SemaphoreType.DMA((8,)),
        ],
        compiler_params=params(60),
        cost_estimate=cost(2 * tokens * inner * (KERNEL * inner + 3 * model) * 2, tokens * model * 10),
        name="middle",
    )(me, lengths, cluster_sizes, a1, x, cot, own, sib, model_vec, inner_vec)

    rows = KERNEL * ci + co
    block = lambda n: pl.BlockSpec((n, ci, inner), lambda k: (0, k, 0))
    late_block = lambda n: pl.BlockSpec((n, ci, inner), lambda k: (0, jnp.maximum(k - KERNEL, 0), 0))
    mine, keep, send = pl.pallas_call(
        functools.partial(conv_grad_kernel, length=length, seqs=seqs),
        grid=(KERNEL + 2,),
        in_specs=[SMEM, whole((tokens, inner)), whole((tokens, inner))]
        + [late_block(n) for n in (1, 3, 4)],
        out_specs=[block(n) for n in (1, 3, 4)],
        out_shape=[sds((n, rows, inner), d) for n, d in ((1, F32), (3, BF), (4, BF))],
        scratch_shapes=[
            pltpu.VMEM((seqs, length + 2 * REACH, inner), BF),
            pltpu.VMEM((inner, tokens), BF),
            pltpu.VMEM((inner, inner), F32),
        ],
        compiler_params=params(60),
        cost_estimate=cost(2 * tokens * KERNEL * inner * inner * 1.3, tokens * inner * 4),
        name="conv_grad",
    )(me, a1, gv, *out_parts)

    def conv_back(s, extra):
        last = bool(extra)
        at = lambda i: (s * per + i, 0)
        once = lambda i: (s, 0)
        part = pl.BlockSpec((tile, inner), at)
        ins = [SMEM, pl.BlockSpec((length, inner), once), part, part, ANY, ANY, whole((8, inner))]
        outs = [pl.BlockSpec((tile, inner), row), whole((3, 8, inner))]
        shapes = [sds((length, inner), BF), sds((3, 8, inner), F32)]
        scratch = [
            pltpu.VMEM((KERNEL * inner, inner), BF),
            pltpu.VMEM((length + 2 * REACH, inner), BF),
            pltpu.SemaphoreType.DMA((40,)),
        ]
        if last:
            ins += [
                pl.BlockSpec((tile, inner), row),
                pl.BlockSpec((tile, model), row),
                pl.BlockSpec((tile, model), at),
            ]
            for n, dtype in ((1, F32), (3, BF), (4, BF)):
                outs += [whole((n, 2 * ci, inner))]
                shapes += [sds((n, 2 * ci, inner), dtype)]
            scratch += [pltpu.VMEM((inner, model), F32)]
        return pl.pallas_call(
            functools.partial(conv_back_kernel, tile=tile, chunk=256, last=last),
            grid=(per,),
            in_specs=ins,
            out_specs=outs,
            out_shape=shapes,
            scratch_shapes=scratch,
            compiler_params=params(60),
            cost_estimate=cost(
                2 * length * inner * (KERNEL * inner + 2 * model * last) * 1.5, length * inner * 12
            ),
            name="conv_back",
        )(me, gv, g1, c1, own, sib, inner_vec, *extra)

    def first_back(s, gu, old):
        tile = 256
        per = length // tile
        at = lambda i: (s * per + i, 0)
        wide = pl.BlockSpec((tile, model), at)
        ins = [SMEM, SMEM, SMEM, wide, wide, pl.BlockSpec((tile, inner), row), wide, ANY, ANY]
        return pl.pallas_call(
            functools.partial(first_back_kernel, tile=tile, chunk=256, length=length, first=s),
            grid=(per,),
            in_specs=ins + [whole((8, model))] + [ANY] * len(old),
            out_specs=[wide, whole((2, 8, model))],
            out_shape=[sds((tokens, model), BF), sds((2, 8, model), F32)],
            input_output_aliases={10: 0} if old else {},
            scratch_shapes=[pltpu.VMEM((inner, model), BF), pltpu.SemaphoreType.DMA((16,))],
            compiler_params=params(60),
            cost_estimate=cost(2 * length * model * inner * 4, length * model * 8),
            name="first_back",
        )(me, lengths, cluster_sizes, x, cot, gu, g0, in_own, in_sib, model_vec, *old)

    if staged:
        send, gv = tie(send, gv)
        got = fs_perm(send, 1)
        gu0, vin1a = conv_back(0, [])
        got, gu0 = tie(got, gu0)

        first = scatter_first(keep, got)
        gu1, vin1b, in_mine, in_keep, in_send = conv_back(1, [gu0, a0, a0])
        *first, in_send, gu1 = tie(*first, in_send, gu1)

        second = scatter_second(keep, got, *first)
        in_got = fs_perm(in_send, 1)
        grad_x, vmod0a = first_back(0, gu0, [])
        *second, in_got, grad_x = tie(*second, in_got, grad_x)

        width = inner // 4
        groups = [(width, [[(t * ci, d * width) for t in range(KERNEL + 2)] for d in range(4)])]
        own, *sends = pack(z, mine, got, *first, *second, groups, ci)
        from_1, from_3 = dp_perm(sends[0], 1), dp_perm(sends[2], 3)
        in_first = scatter_first(in_keep, in_got)
        grad_x, vmod0b = first_back(1, gu1, [grad_x])
        own, from_1, from_3, send_2, vmod0b, *in_first = tie(
            own, from_1, from_3, sends[1], vmod0b, *in_first
        )

        counts = jnp.pad(counts.astype(F32), (0, 128 - TYPES)).reshape(1, 128)
        sums, send = small(
            sums_kernel,
            [((4, 16, co), F32)] * 2,
            [((8, inner), F32), ((8, model), F32)],
            name="sums",
        )(me, vin1a, vin1b, vin2, vmod0a, vmod0b, vmod2, counts)
        got = fs_perm(send, 1)
        in_second = scatter_second(in_keep, in_got, *in_first)
        sums, got, *in_second = tie(sums, got, *in_second)

        sums = sums + got
        from_2 = dp_perm(send_2, 2)
        got = [fs_perm(sums[k], 2 * k) for k in (1, 2, 3)]
        sums, from_2, *got = tie(sums, from_2, *got)

        shape = (ci, model // 4)
        piece = ((ci + 16, model // 4), BF)
        in_own, vec, *sends = small(
            last_pack_kernel,
            [(shape, F32), ((16, co), F32), piece, piece, piece],
            [((2 * ci, inner), F32), ((4,) + shape, F32)],
            name="last_pack",
        )(z.reshape(1), in_mine, in_got, *in_first, *in_second, sums[0], *got)
        got = [dp_perm(v, k) for k, v in zip((1, 2, 3), sends)]
        d_conv, d_out = small(
            rest_kernel, [((KERNEL, width, ci), F32), ((width, co), F32)], name="rest"
        )(own, from_1, from_2, from_3)
        d_in, d_inner, d_model, counts = small(
            last_kernel,
            [((model // 4, ci), F32), ((6, ci), F32), ((3, co), F32), ((1, 128), F32)],
            name="last",
        )(in_own, vec, *got)
        type_counts = counts[0, :TYPES].astype(jnp.int32)
    else:
        gu0, vin1a = conv_back(0, [])
        gu1, vin1b, in_mine, in_keep, in_send = conv_back(1, [gu0, a0, a0])
        grad_x, vmod0a = first_back(0, gu0, [])
        grad_x, vmod0b = first_back(1, gu1, [grad_x])
        down = lambda v: jnp.sum(v, axis=-2)
        type_counts, d_inner, d_model = lax.psum(
            (
                counts,
                jnp.concatenate([down(vin1a + vin1b), down(vin2)]),
                jnp.concatenate([down(vmod0a + vmod0b), down(vmod2)[None]]),
            ),
            ("dp", "fsdp"),
        )
        ours = lambda v, n: lax.dynamic_slice_in_dim(v, place * n, n, 1)
        d_inner, d_model = ours(d_inner, inner_shard.shape[1]), ours(d_model, model_shard.shape[1])
        with_mine = lambda m, k: jnp.concatenate([m, k.astype(F32)])
        d_in, d_conv, d_out = generic_scatter(
            (with_mine(in_mine, in_keep), in_send), (with_mine(mine, keep), send)
        )

    return (
        block_out.reshape(activations.shape),
        grad_x.reshape(activations.shape),
        d_in,
        d_conv,
        d_out,
        d_inner,
        d_model,
        type_counts,
    )


def solution(mesh):
    rows = ("dp", "fsdp")
    return jax.shard_map(
        functools.partial(local, mesh.shape["dp"], mesh.shape["fsdp"]),
        mesh=mesh,
        in_specs=(
            P(rows, None, None),
            P(rows, None, None),
            P(rows),
            P(rows),
            P(rows, None),
            P("dp", "fsdp"),
            P(None, "dp", "fsdp"),
            P("dp", "fsdp"),
            P(None, "fsdp"),
            P(None, "fsdp"),
        ),
        out_specs=(
            P(rows, None, None),
            P(rows, None, None),
            P("dp", "fsdp"),
            P(None, "dp", "fsdp"),
            P("dp", "fsdp"),
            P(None, "fsdp"),
            P(None, "fsdp"),
            P(),
        ),
        check_vma=False,
    )
```

```python
import functools

import jax
import jax.numpy as jnp
from jax import lax
from jax.experimental import pallas as pl
from jax.experimental.pallas import tpu as pltpu
from jax.sharding import PartitionSpec as P

KERNEL = 5
DILATION = 32
REACH = DILATION * (KERNEL - 1) // 2
TYPES = 25
FS = 8

EPS = 1e-05
INV_ROOT_TWO = 0.7071067811865476
INV_ROOT_TWO_PI = 0.3989422804014327

BF = jnp.bfloat16
F32 = jnp.float32
NT = (((1,), (1,)), ((), ()))
NN = (((1,), (0,)), ((), ()))
TN = (((0,), (0,)), ((), ()))
ANY = pl.BlockSpec(memory_space=pl.ANY)
SMEM = pl.BlockSpec(memory_space=pltpu.SMEM)


def dot(a, b, dims):
    return lax.dot_general(a, b, dims, preferred_element_type=F32)


def params(mib):
    return pltpu.CompilerParams(
        dimension_semantics=("arbitrary",), vmem_limit_bytes=mib * 1024 * 1024
    )


def cost(flops, nbytes, trans=0):
    return pl.CostEstimate(
        flops=int(flops / 10), bytes_accessed=int(nbytes / 10), transcendentals=int(trans / 10)
    )


def small(kernel, shapes, scratch=(), mib=20, name=None, **static):
    def call(*args):
        specs = [SMEM if a.dtype == jnp.int32 else whole(a.shape) for a in args]
        return pl.pallas_call(
            functools.partial(kernel, **static),
            grid=(1,),
            in_specs=specs,
            out_specs=[whole(v) for v, _ in shapes],
            out_shape=[jax.ShapeDtypeStruct(*v) for v in shapes],
            scratch_shapes=[pltpu.VMEM(*v) for v in scratch],
            compiler_params=params(mib),
            name=name,
        )(*args)

    return call


def whole(shape):
    return pl.BlockSpec(shape, lambda *_: (0,) * len(shape))


def row_mean(v):
    return jnp.mean(v, axis=-1, keepdims=True)


def centre(v):
    centred = v - row_mean(v)
    return centred, lax.rsqrt(row_mean(centred * centred) + EPS)


def gelu_pair(h):
    phi = 0.5 * (1.0 + lax.erf(h * INV_ROOT_TWO))
    dens = jnp.exp(-0.5 * h * h) * INV_ROOT_TWO_PI
    return h * phi, phi + h * dens


def norm_back(scaled, normed, inv):
    return inv * (scaled - row_mean(scaled) - normed * row_mean(scaled * normed))


def fold(v):
    return jnp.sum(v.reshape(v.shape[0] // 8, 8, v.shape[1]), axis=0)


def rows_at(i, size):
    return pl.ds(pl.multiple_of(i * size, size), size)


def xor_perm(n, k):
    return [(i, i ^ k) for i in range(n)]


def blocks_of(me):
    yx, core = me // 2, me % 2
    for k in range(FS // 2):
        for side in range(2):
            yield k, side, (yx ^ k) * 2 + (core if side == 0 else 1 - core)


def first_norm_kernel(x_ref, vec_ref, *refs, chunk):
    a_ref, g_ref = refs[-2:]
    gain, shift = vec_ref[0:1, :], vec_ref[1:2, :]

    def step(i, _):
        r = rows_at(i, chunk)
        centred, inv = centre(x_ref[r, :].astype(F32))
        a, g = gelu_pair(centred * inv * gain + shift)
        a_ref[r, :] = a.astype(BF)
        g_ref[r, :] = g.astype(BF)
        return 0

    lax.fori_loop(0, x_ref.shape[0] // chunk, step, 0)


def put_block(k, side, rows, part, mine_ref, keep_ref, send_ref):
    if side == 1:
        send_ref[k, rows, :] = part.astype(BF)
    elif k == 0:
        mine_ref[0, rows, :] = part
    else:
        keep_ref[k - 1, rows, :] = part.astype(BF)


def load_in_weight(me_ref, own, sib, dst, sem, wait):
    half = dst.shape[1] // 2
    n = 0
    for k, side, block in blocks_of(me_ref[0]):
        src = own if side == 0 else sib
        for h in range(2):
            c = pltpu.make_async_copy(
                src.at[k, pl.ds(h * 80, 80), :],
                dst.at[pl.ds(pl.multiple_of(block * 80, 16), 80), pl.ds(h * half, half)],
                sem.at[n],
            )
            n += 1
            c.wait() if wait else c.start()


def in_proj_kernel(
    me_ref, len_ref, a0_ref, own, sib, vec_ref, *refs, tile, chunk, length, first
):
    a_ref, g_ref, c_ref, w, sem = refs[-5:]
    i = pl.program_id(0)

    @pl.when(i == 0)
    def _():
        load_in_weight(me_ref, own, sib, w, sem, False)
        load_in_weight(me_ref, own, sib, w, sem, True)

    bias, gain, shift = (vec_ref[j : j + 1, :] for j in range(3))
    per = length // tile
    limit = len_ref[first + i // per] - (i % per) * tile
    for lo in range(0, tile, chunk):
        r = slice(lo, lo + chunk)
        v = dot(a0_ref[r, :], w[...], NT) + bias
        centred, inv = centre(v)
        a, g = gelu_pair(centred * inv * gain + shift)
        keep = lo + lax.broadcasted_iota(jnp.int32, (chunk, 1), 0) < limit
        a_ref[r, :] = jnp.where(keep, a, 0.0).astype(BF)
        g_ref[r, :] = jnp.where(keep, g, 0.0)
        c_ref[r, :] = centred.astype(BF)


def load_conv_weight(me_ref, own, sib, dst, sem, wait, inner):
    n = 0
    for k, side, block in blocks_of(me_ref[0]):
        src = own if side == 0 else sib
        for tap in range(KERNEL):
            c = pltpu.make_async_copy(
                src.at[k, pl.ds((tap + 2) * 80, 80), :],
                dst.at[pl.ds(pl.multiple_of(tap * inner + block * 80, 16), 80), :],
                sem.at[n],
            )
            n += 1
            c.wait() if wait else c.start()


def fill_padded(pad, src_ref, length):
    zeros = jnp.zeros((REACH, pad.shape[1]), pad.dtype)
    pad[0:REACH, :] = zeros
    pad[REACH + length : 2 * REACH + length, :] = zeros
    pad[REACH : REACH + length, :] = src_ref[...]


def load_out_weight(me_ref, own, sib, dst, sem, wait):
    n = 0
    for k, side, block in blocks_of(me_ref[0]):
        src = own if side == 0 else sib
        c = pltpu.make_async_copy(
            src.at[k, pl.ds(0, 160), :],
            dst.at[pl.ds(pl.multiple_of(block * 160, 16), 160), :],
            sem.at[n],
        )
        n += 1
        c.wait() if wait else c.start()


def middle_kernel(
    me_ref, len_ref, size_ref, a1_ref, x_ref, cot_ref, own, sib,
    model_ref, inner_ref, y_ref, gv_ref, mine_ref, keep_ref, send_ref, vin_ref, vmod_ref,
    wc, wo, pad, a2, gy, dw, sem_c, sem_o, *, tile, chunk, length,
):
    i = pl.program_id(0)
    inner = pad.shape[1]
    per = length // tile

    @pl.when(i == 0)
    def _():
        load_conv_weight(me_ref, own, sib, wc, sem_c, False, inner)
        load_out_weight(me_ref, own, sib, wo, sem_o, False)
        vin_ref[...] = jnp.zeros_like(vin_ref)
        vmod_ref[...] = jnp.zeros_like(vmod_ref)
        dw[...] = jnp.zeros_like(dw)

    @pl.when(i % per == 0)
    def _():
        fill_padded(pad, a1_ref, length)

    @pl.when(i == 0)
    def _():
        load_conv_weight(me_ref, own, sib, wc, sem_c, True, inner)
        load_out_weight(me_ref, own, sib, wo, sem_o, True)

    seq = i // per
    at = (i % per) * tile
    limit = len_ref[seq] - at
    scale = 1.0 / size_ref[seq].astype(F32)
    bias, gain, shift = (inner_ref[j : j + 1, :] for j in range(3, 6))
    out_bias = model_ref[2:3, :]
    for lo in range(0, tile, chunk):
        r = slice(lo, lo + chunk)
        v = bias
        for tap in range(KERNEL):
            start = pl.multiple_of(at + lo + tap * DILATION, DILATION)
            v = v + dot(pad[pl.ds(start, chunk), :], wc[tap * inner : (tap + 1) * inner, :], NT)
        centred, inv = centre(v)
        normed = centred * inv
        a, g = gelu_pair(normed * gain + shift)
        a2[r, :] = a.astype(BF)
        rows = lo + lax.broadcasted_iota(jnp.int32, (chunk, 1), 0)
        grad = jnp.where(rows < limit, cot_ref[r, :].astype(F32) * scale, 0.0).astype(BF)
        gy[r, :] = grad
        vmod_ref[...] += fold(grad.astype(F32))
        y = dot(a2[r, :], wo[...], NT) + out_bias
        y_ref[r, :] = (x_ref[r, :].astype(F32) + y).astype(BF)
        d = dot(gy[r, :], wo[...], NN) * g
        grad = norm_back(d * gain, normed, inv).astype(BF)
        gv_ref[r, :] = grad
        vin_ref[0] += fold(grad.astype(F32))
        vin_ref[1] += fold(d * normed)
        vin_ref[2] += fold(d)
    dw[...] += dot(gy[...], a2[...], TN)

    @pl.when(i == pl.num_programs(0) - 1)
    def _():
        for k, side, block in blocks_of(me_ref[0]):
            part = dw[pl.ds(pl.multiple_of(block * 160, 16), 160), :]
            put_block(k, side, slice(None), part, mine_ref, keep_ref, send_ref)


def conv_grad_kernel(
    me_ref, a1_ref, gv_ref, _mine, _keep, _send, mine_ref, keep_ref, send_ref, pad, gvt, dw,
    *, length, seqs,
):
    tap = pl.program_id(0)

    @pl.when(tap == 0)
    def _():
        zeros = jnp.zeros((REACH, pad.shape[2]), pad.dtype)
        for s in range(seqs):
            pad[s, 0:REACH, :] = zeros
            pad[s, REACH + length : 2 * REACH + length, :] = zeros
            pad[s, REACH : REACH + length, :] = a1_ref[s * length : (s + 1) * length, :]
        gvt[...] = gv_ref[...].T

    total = None
    for s in range(seqs):
        window = pad[s, pl.ds(pl.multiple_of(tap * DILATION, DILATION), length), :]
        part = dot(gvt[:, s * length : (s + 1) * length], window, NN)
        total = part if total is None else total + part
    dw[...] = total
    for k, side, block in blocks_of(me_ref[0]):
        part = dw[pl.ds(pl.multiple_of(block * 80, 16), 80), :]
        put_block(k, side, slice(None), part, mine_ref, keep_ref, send_ref)


def conv_back_kernel(
    me_ref, gv_ref, g_ref, c_ref, own, sib, vec_ref, *refs, tile, chunk, last
):
    if last:
        gu0_ref, a00_ref, a01_ref = refs[:3]
        gu_ref, vin_ref, mine_ref, keep_ref, send_ref, w, pad, sem, dw = refs[3:]
    else:
        gu_ref, vin_ref, w, pad, sem = refs[-5:]
    i = pl.program_id(0)
    inner = pad.shape[1]

    @pl.when(i == 0)
    def _():
        load_conv_weight(me_ref, own, sib, w, sem, False, inner)
        vin_ref[...] = jnp.zeros_like(vin_ref)
        if last:
            dw[...] = jnp.zeros_like(dw)
        fill_padded(pad, gv_ref, gv_ref.shape[0])
        load_conv_weight(me_ref, own, sib, w, sem, True, inner)

    gain = vec_ref[1:2, :]
    at = i * tile
    for lo in range(0, tile, chunk):
        r = slice(lo, lo + chunk)
        starts = [at + lo + shift * DILATION for shift in range(KERNEL - 1, -1, -1)]
        rows = [pad[pl.ds(pl.multiple_of(start, DILATION), chunk), :] for start in starts]
        v = dot(jnp.concatenate(rows, axis=1), w[...], NN)
        centred = c_ref[r, :].astype(F32)
        inv = lax.rsqrt(row_mean(centred * centred) + EPS)
        normed = centred * inv
        d = v * g_ref[r, :]
        grad = norm_back(d * gain, normed, inv).astype(BF)
        gu_ref[r, :] = grad
        vin_ref[0] += fold(grad.astype(F32))
        vin_ref[1] += fold(d * normed)
        vin_ref[2] += fold(d)
    if last:
        part = dot(gu_ref[...], a01_ref[...], TN)
        dw[...] += part + dot(gu0_ref[...], a00_ref[...], TN)

        @pl.when(i == pl.num_programs(0) - 1)
        def _():
            half = dw.shape[1] // 2
            for k, side, block in blocks_of(me_ref[0]):
                for h in range(2):
                    rows = pl.ds(pl.multiple_of(block * 80, 16), 80)
                    part = dw[rows, h * half : (h + 1) * half]
                    at = slice(h * 80, (h + 1) * 80)
                    put_block(k, side, at, part, mine_ref, keep_ref, send_ref)


def first_back_kernel(
    me_ref, len_ref, size_ref, x_ref, cot_ref, gu_ref, g_ref, own, sib, vec_ref, *refs,
    tile, chunk, length, first,
):
    gx_ref, vmod_ref, w, sem = refs[-4:]
    i = pl.program_id(0)

    @pl.when(i == 0)
    def _():
        load_in_weight(me_ref, own, sib, w, sem, False)
        vmod_ref[...] = jnp.zeros_like(vmod_ref)
        load_in_weight(me_ref, own, sib, w, sem, True)

    per = length // tile
    seq = first + i // per
    limit = len_ref[seq] - (i % per) * tile
    scale = 1.0 / size_ref[seq].astype(F32)
    gain = vec_ref[0:1, :]
    for lo in range(0, tile, chunk):
        r = slice(lo, lo + chunk)
        rows = lo + lax.broadcasted_iota(jnp.int32, (chunk, 1), 0)
        centred, inv = centre(x_ref[r, :].astype(F32))
        normed = centred * inv
        d = dot(gu_ref[r, :], w[...], NN) * g_ref[r, :].astype(F32)
        grad = norm_back(d * gain, normed, inv)
        out = jnp.where(rows < limit, cot_ref[r, :].astype(F32) * scale, 0.0)
        gx_ref[r, :] = (out + grad).astype(BF)
        vmod_ref[0] += fold(d * normed)
        vmod_ref[1] += fold(d)


def shards_kernel(w_in, w_conv, w_out, inner_ref, model_ref, in_ref, rest_ref, both_ref, vec_ref):
    rows = w_in.shape[0]
    width = w_conv.shape[1]
    part = w_in[...]
    in_ref[...] = part
    both_ref[:, : part.shape[1]] = part
    cut = part.shape[1]
    out = w_out[...].T
    parts = [out[:rows], out[rows:]] + [w_conv[tap].T for tap in range(KERNEL)]
    for t, part in enumerate(parts):
        rest_ref[:, t * width : (t + 1) * width] = part
        both_ref[:, cut + t * width : cut + (t + 1) * width] = part
    vec_ref[...] = jnp.zeros_like(vec_ref)
    vec_ref[0:6, :rows] = inner_ref[...].astype(F32)
    vec_ref[8:11, :] = model_ref[...].astype(F32)


def in_block_kernel(z_ref, p0, p1, p2, p3, vec_ref, got_ref, out_ref, pieces):
    rows, width = p0.shape
    half = out_ref.shape[1] // 2
    z = z_ref[0]
    for k, p in enumerate((p0, p1, p2, p3)):
        pieces[k] = p[:, :width].astype(F32)
    for d in range(4):
        row, lane = d // 2 * rows, d % 2 * half
        out_ref[row : row + rows, lane : lane + half] = pieces[z ^ d].astype(BF)
    co = vec_ref.shape[1]
    both = jnp.concatenate([vec_ref[...], got_ref[...]], axis=1).astype(BF)
    out_ref[2 * rows :, : 2 * co] = both
    out_ref[2 * rows :, 2 * co :] = jnp.zeros((16, out_ref.shape[1] - 2 * co), BF)


def unpack_kernel(
    me_ref, z_ref, b0, b1, b2, b3, p0, p1, p2, p3, in_ref, inner_ref, model_ref, a_ref, b_ref,
    vecs, pieces, block, *, cut,
):
    rows = p0.shape[0]
    width = block.shape[1] // 4
    z = z_ref[0]
    for k, (p, lane) in enumerate(zip((p0, p1, p2, p3), cut)):
        pieces[k] = p[:, lane:].astype(F32)
    for d in range(4):
        piece = pieces[z ^ d]
        for t in range(block.shape[0] // rows):
            block[t * rows : (t + 1) * rows, d * width : (d + 1) * width] = piece[
                :, t * width : (t + 1) * width
            ]
    h = a_ref.shape[0]
    a_ref[...] = block[:h].astype(BF)
    b_ref[...] = block[h:].astype(BF)
    blocks = (b0, b1, b2, b3)
    n = in_ref.shape[1]
    co = model_ref.shape[1] // FS
    ci = inner_ref.shape[1] // FS
    for k in range(4):
        in_ref[k] = blocks[k][:n, :]
    for k, side, place in blocks_of(me_ref[0]):
        vecs[place] = blocks[k][n:, side * co : (side + 1) * co].astype(F32)
    for f in range(FS):
        inner_ref[:, f * ci : (f + 1) * ci] = vecs[f, 0:8, :ci]
        model_ref[:, f * co : (f + 1) * co] = vecs[f, 8:16, :]


def pack_kernel(
    z_ref, keep_ref, got_ref, got_a_ref, got_b_ref, a_ref, b_ref, own_ref, o1, o2, o3, mine, pieces,
    *, groups, rows,
):
    h = a_ref.shape[0]
    first = keep_ref[0] + got_ref[0].astype(F32)
    mine[:h, :] = first[:h] + got_a_ref[0].astype(F32) + a_ref[...].astype(F32)
    mine[h:, :] = first[h:] + got_b_ref[0].astype(F32) + b_ref[...].astype(F32)
    for d in range(4):
        col = 0
        for width, starts in groups:
            for row, lane in starts[d]:
                pieces[d, :, col : col + width] = mine[row : row + rows, lane : lane + width]
                col += width
    z = z_ref[0]
    own_ref[...] = pieces[z]
    for k, out in ((1, o1), (2, o2), (3, o3)):
        out[...] = pieces[z ^ k].astype(BF)


def sums_kernel(me_ref, vin1a, vin1b, vin2, vmod0a, vmod0b, vmod2, counts, keep_ref, send_ref, inner, model):
    down = lambda v: jnp.sum(v, axis=0, keepdims=True)
    for j in range(3):
        inner[j : j + 1, :] = down(vin1a[j] + vin1b[j])
        inner[3 + j : 4 + j, :] = down(vin2[j])
    for j in range(2):
        model[j : j + 1, :] = down(vmod0a[j] + vmod0b[j])
    model[2:3, :] = down(vmod2[...])
    ci, co = inner.shape[1] // FS, model.shape[1] // FS
    keep_ref[...] = jnp.zeros_like(keep_ref)
    send_ref[...] = jnp.zeros_like(send_ref)
    yx, core = me_ref[0] // 2, me_ref[0] % 2
    for f in range(FS):
        k = yx ^ (f // 2)
        for dst, mine in ((keep_ref, core == f % 2), (send_ref, core != f % 2)):

            @pl.when(mine)
            def _():
                dst[k, 0:6, :ci] = inner[0:6, f * ci : (f + 1) * ci]
                dst[k, 8:11, :] = model[0:3, f * co : (f + 1) * co]
                dst[k, 11:12, :128] = counts[...]


def last_pack_kernel(
    z_ref, mine_ref, got_ref, got_a_ref, got_b_ref, a_ref, b_ref, v0, v1, v2, v3,
    own_ref, vec_ref, o1, o2, o3, mine, pieces,
):
    h = a_ref.shape[0]
    first = mine_ref[0] + got_ref[0].astype(F32)
    mine[:h, :] = first[:h] + got_a_ref[0].astype(F32) + a_ref[...].astype(F32)
    mine[h:, :] = first[h:] + got_b_ref[0].astype(F32) + b_ref[...].astype(F32)
    rows, width = own_ref.shape
    for d in range(4):
        row, lane = d // 2 * rows, d % 2 * width
        pieces[d] = mine[row : row + rows, lane : lane + width]
    vec = (v0[...] + v1[...]) + (v2[...] + v3[...])
    vec_ref[...] = vec
    high = vec.astype(BF)
    low = (vec - high.astype(F32)).astype(BF)
    z = z_ref[0]
    own_ref[...] = pieces[z]
    for k, out in ((1, o1), (2, o2), (3, o3)):
        out[:rows, :] = pieces[z ^ k].astype(BF)
        out[rows:, :] = jnp.concatenate([high, low], axis=1)


def last_kernel(own, vec, g1, g2, g3, in_ref, inner_ref, model_ref, counts_ref):
    rows = own.shape[0]
    total, sums = own[...], vec[...]
    co = vec.shape[1]
    for g in (g1, g2, g3):
        total = total + g[:rows, :].astype(F32)
        part = g[rows:, :].astype(F32)
        sums = sums + (part[:, :co] + part[:, co:])
    in_ref[...] = total
    inner_ref[...] = sums[0:6, : inner_ref.shape[1]]
    model_ref[...] = sums[8:11, :]
    counts_ref[...] = sums[11:12, :128]


def rest_kernel(own, g1, upper, lower, g3, conv_ref, out_ref):
    g2 = jnp.concatenate([upper[...].astype(F32), lower[...].astype(F32)])
    total = own[...] + g1[...].astype(F32) + (g2 + g3[...].astype(F32))
    width = conv_ref.shape[1]
    out_ref[...] = jnp.concatenate([total[:, :width], total[:, width : 2 * width]]).T
    for tap in range(KERNEL):
        conv_ref[tap] = total[:, (tap + 2) * width : (tap + 3) * width].T


def fs_perm(v, k):
    return lax.ppermute(v, "fsdp", xor_perm(FS, k))


def tie(*values):
    return lax.optimization_barrier(values)


def dp_perm(v, k):
    return lax.ppermute(v, "dp", xor_perm(4, k))


def split_rows(block, axis=0):
    h = block.shape[axis] // 32 * 16
    return lax.slice_in_dim(block, 0, h, axis=axis), lax.slice_in_dim(block, h, None, axis=axis)


def scatter_first(keep, got):
    keep_a, keep_b = split_rows(keep, 1)
    got_a, got_b = split_rows(got, 1)
    plus = lambda a, b: (a.astype(F32) + b.astype(F32)).astype(BF)
    send_a = jnp.stack([plus(keep_a[k - 1], got_a[k]) for k in (1, 3)])
    return fs_perm(send_a, 2), fs_perm(plus(keep_b[1:], got_b[2:]), 4)


def scatter_second(keep, got, from_a, from_b):
    keep_a, keep_b = split_rows(keep, 1)
    got_a, got_b = split_rows(got, 1)
    send_a = total_of([keep_a[1], got_a[2], from_a[1]])
    send_b = total_of([keep_b[0], got_b[1], from_b[1]])
    return fs_perm(send_a.astype(BF), 4), fs_perm(send_b.astype(BF), 2)


def pack(z, mine, got, from_a, from_b, last_a, last_b, groups, rows):
    total, cols = mine.shape[1:]
    h = last_a.shape[0]
    lanes = sum(width * len(starts[0]) for width, starts in groups)
    shape = (rows, lanes)
    return pl.pallas_call(
        functools.partial(pack_kernel, groups=groups, rows=rows),
        grid=(1,),
        in_specs=[SMEM] + [whole((1, n, cols)) for n in (total, total, h, total - h)]
        + [whole((h, cols)), whole((total - h, cols))],
        out_specs=[whole(shape)] * 4,
        out_shape=[jax.ShapeDtypeStruct(shape, d) for d in (F32, BF, BF, BF)],
        scratch_shapes=[pltpu.VMEM((total, cols), F32), pltpu.VMEM((4,) + shape, F32)],
        compiler_params=params(20),
        cost_estimate=cost(total * cols * 8, total * cols * 12),
        name="pack",
    )(z.reshape(1), mine, got, from_a, from_b, last_a, last_b)


def total_of(terms):
    return functools.reduce(lambda a, b: a + b, [t.astype(F32) for t in terms])


def generic_blocks(full):
    blocks = full.reshape(FS // 2, 2, full.shape[0] // FS, full.shape[1])
    return blocks[:, 0], blocks[:, 1]


def generic_full(keep, send):
    full = jnp.stack([keep, send.astype(F32)], axis=1)
    return full.reshape(FS, -1, full.shape[-1])


def generic_gather(w_in, w_conv, w_out):
    both = lambda w, rows, cols: lax.all_gather(
        lax.all_gather(w, "fsdp", axis=cols, tiled=True), "dp", axis=rows, tiled=True
    )
    w_in, w_conv, w_out = both(w_in, 0, 1), both(w_conv, 1, 2), both(w_out, 0, 1)
    taps, inner = w_conv.shape[0], w_conv.shape[1]
    part = w_in.T.reshape(FS, inner // FS, 2, inner).transpose(0, 2, 1, 3).reshape(-1, inner)
    conv = w_conv.transpose(2, 0, 1).reshape(FS, inner // FS, taps, inner)
    conv = conv.transpose(0, 2, 1, 3).reshape(-1, inner)
    pairs = zip(generic_blocks(w_out.T), generic_blocks(conv))
    return generic_blocks(part), [jnp.concatenate(p, axis=1) for p in pairs]


def generic_scatter(ins, rest):
    scatter = lambda w, rows, cols: lax.psum_scatter(
        lax.psum_scatter(w, "fsdp", scatter_dimension=cols, tiled=True),
        "dp", scatter_dimension=rows, tiled=True,
    )
    d_in, rest = generic_full(*ins), generic_full(*rest)
    inner = d_in.shape[-1]
    cut = rest.shape[1] - KERNEL * inner // FS
    d_out, d_conv = rest[:, :cut], rest[:, cut:]
    d_in = d_in.reshape(FS, 2, -1, inner).transpose(0, 2, 1, 3).reshape(inner, -1).T
    d_conv = d_conv.reshape(FS, KERNEL, -1, inner).transpose(1, 3, 0, 2).reshape(KERNEL, inner, inner)
    return scatter(d_in, 0, 1), scatter(d_conv, 1, 2), scatter(d_out.reshape(-1, inner).T, 0, 1)


def local(
    n_dp,
    n_fs,
    activations,
    cotangent,
    lengths,
    cluster_sizes,
    residue_types,
    w_in,
    w_conv,
    w_out,
    inner_shard,
    model_shard,
):
    seqs, length, model = activations.shape
    inner = w_in.shape[1] * n_fs
    tokens = seqs * length
    x = activations.reshape(tokens, model)
    cot = cotangent.reshape(tokens, model)
    staged = n_dp == 4 and n_fs == FS
    place, z = lax.axis_index("fsdp"), lax.axis_index("dp")
    me = place.reshape(1) if staged else jnp.zeros((1,), jnp.int32)
    ci, co = inner // FS, model // FS

    positions = jnp.arange(length, dtype=jnp.int32)
    valid = positions[None, :] < lengths[:, None]
    kinds = jnp.arange(TYPES, dtype=jnp.int32)
    hits = (residue_types[:, :, None] == kinds[None, None, :]) & valid[:, :, None]
    counts = jnp.sum(hits.astype(jnp.int32), axis=(0, 1))

    def sds(shape, dtype):
        return jax.ShapeDtypeStruct(shape, dtype)

    tile = 512
    per = length // tile
    row = lambda i: (i, 0)

    def first_norm(part, parts, vec, old):
        size, steps = 256, tokens // parts // 256
        block = pl.BlockSpec((size, model), lambda i: (part * steps + i, 0))
        return pl.pallas_call(
            functools.partial(first_norm_kernel, chunk=128),
            grid=(steps,),
            in_specs=[block, whole((8, model))] + [ANY] * len(old),
            out_specs=[block] * 2,
            out_shape=[sds((tokens, model), BF)] * 2,
            input_output_aliases={2: 0, 3: 1} if old else {},
            compiler_params=params(48),
            cost_estimate=cost(
                tokens * model * 60 / parts, tokens * model * 6 / parts, tokens * model * 2 / parts
            ),
            name="first_norm",
        )(x, vec, *old)

    def in_proj(part, parts, a0, own, sib, vec, old):
        steps = tokens // parts // tile
        wide = pl.BlockSpec((tile, model), lambda i: (part * steps + i, 0))
        narrow = pl.BlockSpec((tile, inner), lambda i: (part * steps + i, 0))
        return pl.pallas_call(
            functools.partial(
                in_proj_kernel, tile=tile, chunk=256, length=length, first=part * seqs // parts
            ),
            grid=(steps,),
            in_specs=[SMEM, SMEM, wide, ANY, ANY, whole((8, inner))] + [ANY] * len(old),
            out_specs=[narrow] * 3,
            out_shape=[sds((tokens, inner), d) for d in (BF, F32, BF)],
            input_output_aliases={6: 0, 7: 1, 8: 2} if old else {},
            scratch_shapes=[pltpu.VMEM((inner, model), BF), pltpu.SemaphoreType.DMA((16,))],
            compiler_params=params(48),
            cost_estimate=cost(
                2 * tokens * model * inner * 3 / parts, tokens * (model + 4 * inner) * 2 / parts
            ),
            name="in_proj",
        )(me, lengths, a0, own, sib, vec, *old)

    if staged:
        cut, width = model // 4, inner // 4
        lanes = (KERNEL + 2) * width
        shapes = [((ci, cut), BF), ((ci, lanes), BF), ((ci, cut + lanes), BF), ((16, co), F32)]
        in_t, rest_t, both, vec = small(shards_kernel, shapes, name="shards")(
            w_in.T, w_conv, w_out, inner_shard, model_shard
        )
        got = [fs_perm(vec, 1), dp_perm(both, 1), dp_perm(in_t, 2), dp_perm(both, 3)]
        vec, both, in_t, rest_t, *got = tie(vec, both, in_t, rest_t, *got)

        place_z = z.reshape(1)
        (block,) = small(
            in_block_kernel, [((2 * ci + 16, inner), BF)], [((4, ci, cut), F32)], name="in_block"
        )(place_z, in_t, got[1], got[2], got[3], vec, got[0])
        blocks = [block] + [fs_perm(block, k) for k in (2, 4, 6)]
        tied = tie(rest_t, got[1], dp_perm(rest_t, 2), got[3], *blocks)
        rest_z, blocks = tied[:4], tied[4:]

        h = lanes // width * ci // 32 * 16
        shapes = [
            ((4, 2 * ci, inner), BF),
            ((8, inner), F32),
            ((8, model), F32),
            ((h, inner), BF),
            ((lanes // width * ci - h, inner), BF),
        ]
        in_own, inner_vec, model_vec, a, b = small(
            unpack_kernel,
            shapes,
            [((FS, 16, co), F32), ((4, ci, lanes), F32), ((lanes // width * ci, inner), F32)],
            cut=(0, cut, 0, cut),
            name="unpack",
        )(me, place_z, *blocks, *rest_z)
        in_sib = fs_perm(in_own, 1)
        w_a1, w_b2 = fs_perm(a, 2), fs_perm(b, 4)
        a0, g0 = first_norm(0, 1, model_vec, [])
        in_own, in_sib, w_a1, w_b2, a0, g0 = tie(in_own, in_sib, w_a1, w_b2, a0, g0)

        second = [fs_perm(a, 4), fs_perm(w_a1, 4), fs_perm(b, 2), fs_perm(w_b2, 2)]
        a1, g1, c1 = in_proj(0, 1, a0, in_own, in_sib, inner_vec, [])
        a1, g1, c1, a2, a3, b1, b3 = tie(a1, g1, c1, *second)
        pairs = [(a, b), (w_a1, b1), (a2, w_b2), (a3, b3)]
        own = jnp.stack([jnp.concatenate(p) for p in pairs])
        own, a1, g1, c1 = tie(own, a1, g1, c1)
        sib = fs_perm(own, 1)
    else:
        gather = lambda v: lax.all_gather(v, "fsdp", axis=1, tiled=True).astype(F32)
        inner_vec = jnp.pad(gather(inner_shard), ((0, 2), (0, 0)))
        model_vec = jnp.pad(gather(model_shard), ((0, 5), (0, 0)))
        (in_own, in_sib), (own, sib) = generic_gather(w_in, w_conv, w_out)
        a0, g0 = first_norm(0, 1, model_vec, [])
        a1, g1, c1 = in_proj(0, 1, a0, in_own, in_sib, inner_vec, [])

    wide, narrow = pl.BlockSpec((tile, model), row), pl.BlockSpec((tile, inner), row)
    rows = co + KERNEL * ci
    shapes = [((1, rows, inner), F32), ((3, rows, inner), BF), ((4, rows, inner), BF)]
    block_out, gv, *out_parts, vin2, vmod2 = pl.pallas_call(
        functools.partial(middle_kernel, tile=tile, chunk=256, length=length),
        grid=(tokens // tile,),
        in_specs=[SMEM, SMEM, SMEM, pl.BlockSpec((length, inner), lambda i: (i // per, 0)),
                  wide, wide, ANY, ANY, whole((8, model)), whole((8, inner))],
        out_specs=[wide, narrow, *(whole((n, co, inner)) for n in (1, 3, 4)),
                   whole((3, 8, inner)), whole((8, model))],
        out_shape=[sds((tokens, model), BF), sds((tokens, inner), BF), *(sds(*v) for v in shapes),
                   sds((3, 8, inner), F32), sds((8, model), F32)],
        scratch_shapes=[
            pltpu.VMEM((KERNEL * inner, inner), BF),
            pltpu.VMEM((model, inner), BF),
            pltpu.VMEM((length + 2 * REACH, inner), BF),
            pltpu.VMEM((tile, inner), BF),
            pltpu.VMEM((tile, model), BF),
            pltpu.VMEM((model, inner), F32),
            pltpu.SemaphoreType.DMA((40,)),
            pltpu.SemaphoreType.DMA((8,)),
        ],
        compiler_params=params(48),
        cost_estimate=cost(2 * tokens * inner * (KERNEL * inner + 3 * model) * 2, tokens * model * 10),
        name="middle",
    )(me, lengths, cluster_sizes, a1, x, cot, own, sib, model_vec, inner_vec)

    block = lambda n: pl.BlockSpec((n, ci, inner), lambda k: (0, k + 2, 0))
    mine, keep, send = pl.pallas_call(
        functools.partial(conv_grad_kernel, length=length, seqs=seqs),
        grid=(KERNEL,),
        in_specs=[SMEM, whole((tokens, inner)), whole((tokens, inner)), ANY, ANY, ANY],
        out_specs=[block(n) for n in (1, 3, 4)],
        out_shape=[sds(*v) for v in shapes],
        input_output_aliases={3: 0, 4: 1, 5: 2},
        scratch_shapes=[
            pltpu.VMEM((seqs, length + 2 * REACH, inner), BF),
            pltpu.VMEM((inner, tokens), BF),
            pltpu.VMEM((inner, inner), F32),
        ],
        compiler_params=params(48),
        cost_estimate=cost(2 * tokens * KERNEL * inner * inner * 1.3, tokens * inner * 4),
        name="conv_grad",
    )(me, a1, gv, *out_parts)

    def conv_back(s, extra):
        last = bool(extra)
        at = lambda i: (s * per + i, 0)
        once = lambda i: (s, 0)
        part = pl.BlockSpec((tile, inner), at)
        ins = [SMEM, pl.BlockSpec((length, inner), once), part, part, ANY, ANY, whole((8, inner))]
        outs = [pl.BlockSpec((tile, inner), row), whole((3, 8, inner))]
        shapes = [sds((length, inner), BF), sds((3, 8, inner), F32)]
        scratch = [
            pltpu.VMEM((KERNEL * inner, inner), BF),
            pltpu.VMEM((length + 2 * REACH, inner), BF),
            pltpu.SemaphoreType.DMA((40,)),
        ]
        if last:
            ins += [
                pl.BlockSpec((tile, inner), row),
                pl.BlockSpec((tile, model), row),
                pl.BlockSpec((tile, model), at),
            ]
            for n, dtype in ((1, F32), (3, BF), (4, BF)):
                outs += [whole((n, 2 * ci, inner))]
                shapes += [sds((n, 2 * ci, inner), dtype)]
            scratch += [pltpu.VMEM((inner, model), F32)]
        return pl.pallas_call(
            functools.partial(conv_back_kernel, tile=tile, chunk=256, last=last),
            grid=(per,),
            in_specs=ins,
            out_specs=outs,
            out_shape=shapes,
            scratch_shapes=scratch,
            compiler_params=params(48),
            cost_estimate=cost(
                2 * length * inner * (KERNEL * inner + 2 * model * last) * 1.5, length * inner * 12
            ),
            name="conv_back",
        )(me, gv, g1, c1, own, sib, inner_vec, *extra)

    def first_back(s, gu, old):
        tile = 256
        per = length // tile
        at = lambda i: (s * per + i, 0)
        wide = pl.BlockSpec((tile, model), at)
        ins = [SMEM, SMEM, SMEM, wide, wide, pl.BlockSpec((tile, inner), row), wide, ANY, ANY]
        return pl.pallas_call(
            functools.partial(first_back_kernel, tile=tile, chunk=256, length=length, first=s),
            grid=(per,),
            in_specs=ins + [whole((8, model))] + [ANY] * len(old),
            out_specs=[wide, whole((2, 8, model))],
            out_shape=[sds((tokens, model), BF), sds((2, 8, model), F32)],
            input_output_aliases={10: 0} if old else {},
            scratch_shapes=[pltpu.VMEM((inner, model), BF), pltpu.SemaphoreType.DMA((16,))],
            compiler_params=params(48),
            cost_estimate=cost(2 * length * model * inner * 4, length * model * 8),
            name="first_back",
        )(me, lengths, cluster_sizes, x, cot, gu, g0, in_own, in_sib, model_vec, *old)

    if staged:
        send, gv = tie(send, gv)
        got = fs_perm(send, 1)
        gu0, vin1a = conv_back(0, [])
        got, gu0 = tie(got, gu0)

        first = scatter_first(keep, got)
        gu1, vin1b, in_mine, in_keep, in_send = conv_back(1, [gu0, a0, a0])
        *first, in_send, gu1 = tie(*first, in_send, gu1)

        second = scatter_second(keep, got, *first)
        in_got = fs_perm(in_send, 1)
        grad_x, vmod0a = first_back(0, gu0, [])
        *second, in_got, grad_x = tie(*second, in_got, grad_x)

        width = inner // 4
        groups = [(width, [[(t * ci, d * width) for t in range(KERNEL + 2)] for d in range(4)])]
        own, *sends = pack(z, mine, got, *first, *second, groups, ci)
        from_1, from_3 = dp_perm(sends[0], 1), dp_perm(sends[2], 3)
        in_first = scatter_first(in_keep, in_got)
        grad_x, vmod0b = first_back(1, gu1, [grad_x])
        own, from_1, from_3, send_2, vmod0b, *in_first = tie(
            own, from_1, from_3, sends[1], vmod0b, *in_first
        )

        counts = jnp.pad(counts.astype(F32), (0, 128 - TYPES)).reshape(1, 128)
        sums, send = small(
            sums_kernel,
            [((4, 16, co), F32)] * 2,
            [((8, inner), F32), ((8, model), F32)],
            name="sums",
        )(me, vin1a, vin1b, vin2, vmod0a, vmod0b, vmod2, counts)
        got = fs_perm(send, 1)
        in_second = scatter_second(in_keep, in_got, *in_first)
        upper = dp_perm(send_2[: ci // 2], 2)
        sums, got, upper, *in_second = tie(sums, got, upper, *in_second)

        sums = sums + got
        lower = dp_perm(send_2[ci // 2 :], 2)
        got = [fs_perm(sums[k], 2 * k) for k in (1, 2, 3)]
        sums, lower, *got = tie(sums, lower, *got)

        shape = (ci, model // 4)
        piece = ((ci + 16, model // 4), BF)
        in_own, vec, *sends = small(
            last_pack_kernel,
            [(shape, F32), ((16, co), F32), piece, piece, piece],
            [((2 * ci, inner), F32), ((4,) + shape, F32)],
            name="last_pack",
        )(z.reshape(1), in_mine, in_got, *in_first, *in_second, sums[0], *got)
        got = [dp_perm(v, k) for k, v in zip((1, 2, 3), sends)]
        d_conv, d_out = small(
            rest_kernel, [((KERNEL, width, ci), F32), ((width, co), F32)], name="rest"
        )(own, from_1, upper, lower, from_3)
        d_in, d_inner, d_model, counts = small(
            last_kernel,
            [(shape, F32), ((6, ci), F32), ((3, co), F32), ((1, 128), F32)],
            name="last",
        )(in_own, vec, *got)
        d_in = d_in.T
        type_counts = counts[0, :TYPES].astype(jnp.int32)
    else:
        gu0, vin1a = conv_back(0, [])
        gu1, vin1b, in_mine, in_keep, in_send = conv_back(1, [gu0, a0, a0])
        grad_x, vmod0a = first_back(0, gu0, [])
        grad_x, vmod0b = first_back(1, gu1, [grad_x])
        down = lambda v: jnp.sum(v, axis=-2)
        type_counts, d_inner, d_model = lax.psum(
            (
                counts,
                jnp.concatenate([down(vin1a + vin1b), down(vin2)]),
                jnp.concatenate([down(vmod0a + vmod0b), down(vmod2)[None]]),
            ),
            ("dp", "fsdp"),
        )
        ours = lambda v, n: lax.dynamic_slice_in_dim(v, place * n, n, 1)
        d_inner, d_model = ours(d_inner, inner_shard.shape[1]), ours(d_model, model_shard.shape[1])
        with_mine = lambda m, k: jnp.concatenate([m, k.astype(F32)])
        d_in, d_conv, d_out = generic_scatter(
            (with_mine(in_mine, in_keep), in_send), (with_mine(mine, keep), send)
        )

    return (
        block_out.reshape(activations.shape),
        grad_x.reshape(activations.shape),
        d_in,
        d_conv,
        d_out,
        d_inner,
        d_model,
        type_counts,
    )


def solution(mesh):
    rows = ("dp", "fsdp")
    return jax.shard_map(
        functools.partial(local, mesh.shape["dp"], mesh.shape["fsdp"]),
        mesh=mesh,
        in_specs=(
            P(rows, None, None),
            P(rows, None, None),
            P(rows),
            P(rows),
            P(rows, None),
            P("dp", "fsdp"),
            P(None, "dp", "fsdp"),
            P("dp", "fsdp"),
            P(None, "fsdp"),
            P(None, "fsdp"),
        ),
        out_specs=(
            P(rows, None, None),
            P(rows, None, None),
            P("dp", "fsdp"),
            P(None, "dp", "fsdp"),
            P("dp", "fsdp"),
            P(None, "fsdp"),
            P(None, "fsdp"),
            P(),
        ),
        check_vma=False,
    )
```

```python
import functools

import jax
import jax.numpy as jnp
from jax import lax
from jax.experimental import pallas as pl
from jax.experimental.pallas import tpu as pltpu
from jax.sharding import PartitionSpec as P

KERNEL = 5
DILATION = 32
REACH = DILATION * (KERNEL - 1) // 2
TYPES = 25
FS = 8

EPS = 1e-05
INV_ROOT_TWO = 0.7071067811865476
INV_ROOT_TWO_PI = 0.3989422804014327

BF = jnp.bfloat16
F32 = jnp.float32
NT = (((1,), (1,)), ((), ()))
NN = (((1,), (0,)), ((), ()))
TN = (((0,), (0,)), ((), ()))
ANY = pl.BlockSpec(memory_space=pl.ANY)
SMEM = pl.BlockSpec(memory_space=pltpu.SMEM)


def dot(a, b, dims):
    return lax.dot_general(a, b, dims, preferred_element_type=F32)


def params(mib):
    return pltpu.CompilerParams(
        dimension_semantics=("arbitrary",), vmem_limit_bytes=mib * 1024 * 1024
    )


def cost(flops, nbytes, trans=0):
    return pl.CostEstimate(
        flops=int(flops / 10), bytes_accessed=int(nbytes / 10), transcendentals=int(trans / 10)
    )


def small(kernel, shapes, scratch=(), mib=20, name=None, **static):
    def call(*args):
        specs = [SMEM if a.dtype == jnp.int32 else whole(a.shape) for a in args]
        return pl.pallas_call(
            functools.partial(kernel, **static),
            grid=(1,),
            in_specs=specs,
            out_specs=[whole(v) for v, _ in shapes],
            out_shape=[jax.ShapeDtypeStruct(*v) for v in shapes],
            scratch_shapes=[pltpu.VMEM(*v) for v in scratch],
            compiler_params=params(mib),
            name=name,
        )(*args)

    return call


def whole(shape):
    return pl.BlockSpec(shape, lambda *_: (0,) * len(shape))


def row_mean(v):
    return jnp.mean(v, axis=-1, keepdims=True)


def centre(v):
    centred = v - row_mean(v)
    return centred, lax.rsqrt(row_mean(centred * centred) + EPS)


def gelu_pair(h):
    phi = 0.5 * (1.0 + lax.erf(h * INV_ROOT_TWO))
    dens = jnp.exp(-0.5 * h * h) * INV_ROOT_TWO_PI
    return h * phi, phi + h * dens


def norm_back(scaled, normed, inv):
    return inv * (scaled - row_mean(scaled) - normed * row_mean(scaled * normed))


def fold(v):
    return jnp.sum(v.reshape(v.shape[0] // 8, 8, v.shape[1]), axis=0)


def rows_at(i, size):
    return pl.ds(pl.multiple_of(i * size, size), size)


def xor_perm(n, k):
    return [(i, i ^ k) for i in range(n)]


def blocks_of(me):
    yx, core = me // 2, me % 2
    for k in range(FS // 2):
        for side in range(2):
            yield k, side, (yx ^ k) * 2 + (core if side == 0 else 1 - core)


def first_norm_kernel(x_ref, vec_ref, *refs, chunk):
    a_ref, g_ref = refs[-2:]
    gain, shift = vec_ref[0:1, :], vec_ref[1:2, :]
    for lo in range(0, x_ref.shape[0], chunk):
        r = slice(lo, lo + chunk)
        centred, inv = centre(x_ref[r, :].astype(F32))
        a, g = gelu_pair(centred * inv * gain + shift)
        a_ref[r, :] = a.astype(BF)
        g_ref[r, :] = g.astype(BF)


def put_block(k, side, rows, part, mine_ref, keep_ref, send_ref):
    if side == 1:
        send_ref[k, rows, :] = part.astype(BF)
    elif k == 0:
        mine_ref[0, rows, :] = part
    else:
        keep_ref[k - 1, rows, :] = part.astype(BF)


def load_in_weight(me_ref, own, sib, dst, sem, wait):
    half = dst.shape[1] // 2
    n = 0
    for k, side, block in blocks_of(me_ref[0]):
        src = own if side == 0 else sib
        for h in range(2):
            c = pltpu.make_async_copy(
                src.at[k, pl.ds(h * 80, 80), :],
                dst.at[pl.ds(pl.multiple_of(block * 80, 16), 80), pl.ds(h * half, half)],
                sem.at[n],
            )
            n += 1
            c.wait() if wait else c.start()


def in_proj_kernel(
    me_ref, len_ref, a0_ref, own, sib, vec_ref, *refs, tile, chunk, length, first
):
    a_ref, g_ref, c_ref, w, sem = refs[-5:]
    i = pl.program_id(0)

    @pl.when(i == 0)
    def _():
        load_in_weight(me_ref, own, sib, w, sem, False)
        load_in_weight(me_ref, own, sib, w, sem, True)

    bias, gain, shift = (vec_ref[j : j + 1, :] for j in range(3))
    per = length // tile
    limit = len_ref[first + i // per] - (i % per) * tile
    for lo in range(0, tile, chunk):
        r = slice(lo, lo + chunk)
        v = dot(a0_ref[r, :], w[...], NT) + bias
        centred, inv = centre(v)
        a, g = gelu_pair(centred * inv * gain + shift)
        keep = lo + lax.broadcasted_iota(jnp.int32, (chunk, 1), 0) < limit
        a_ref[r, :] = jnp.where(keep, a, 0.0).astype(BF)
        g_ref[r, :] = jnp.where(keep, g, 0.0)
        c_ref[r, :] = centred.astype(BF)


def load_conv_weight(me_ref, own, sib, dst, sem, wait, inner):
    n = 0
    for k, side, block in blocks_of(me_ref[0]):
        src = own if side == 0 else sib
        for tap in range(KERNEL):
            c = pltpu.make_async_copy(
                src.at[k, pl.ds((tap + 2) * 80, 80), :],
                dst.at[pl.ds(pl.multiple_of(tap * inner + block * 80, 16), 80), :],
                sem.at[n],
            )
            n += 1
            c.wait() if wait else c.start()


def fill_padded(pad, src_ref, length):
    zeros = jnp.zeros((REACH, pad.shape[1]), pad.dtype)
    pad[0:REACH, :] = zeros
    pad[REACH + length : 2 * REACH + length, :] = zeros
    pad[REACH : REACH + length, :] = src_ref[...]


def load_out_weight(me_ref, own, sib, dst, sem, wait):
    n = 0
    for k, side, block in blocks_of(me_ref[0]):
        src = own if side == 0 else sib
        c = pltpu.make_async_copy(
            src.at[k, pl.ds(0, 160), :],
            dst.at[pl.ds(pl.multiple_of(block * 160, 16), 160), :],
            sem.at[n],
        )
        n += 1
        c.wait() if wait else c.start()


def middle_kernel(
    me_ref, len_ref, size_ref, a1_ref, x_ref, cot_ref, own, sib,
    model_ref, inner_ref, y_ref, gv_ref, mine_ref, keep_ref, send_ref, vin_ref, vmod_ref,
    wc, wo, pad, a2, gy, dw, sem_c, sem_o, *, tile, chunk, length,
):
    i = pl.program_id(0)
    inner = pad.shape[1]
    per = length // tile

    @pl.when(i == 0)
    def _():
        load_conv_weight(me_ref, own, sib, wc, sem_c, False, inner)
        load_out_weight(me_ref, own, sib, wo, sem_o, False)
        vin_ref[...] = jnp.zeros_like(vin_ref)
        vmod_ref[...] = jnp.zeros_like(vmod_ref)
        dw[...] = jnp.zeros_like(dw)

    @pl.when(i % per == 0)
    def _():
        fill_padded(pad, a1_ref, length)

    @pl.when(i == 0)
    def _():
        load_conv_weight(me_ref, own, sib, wc, sem_c, True, inner)
        load_out_weight(me_ref, own, sib, wo, sem_o, True)

    seq = i // per
    at = (i % per) * tile
    limit = len_ref[seq] - at
    scale = 1.0 / size_ref[seq].astype(F32)
    bias, gain, shift = (inner_ref[j : j + 1, :] for j in range(3, 6))
    out_bias = model_ref[2:3, :]
    kept = []
    for lo in range(0, tile, chunk):
        r = slice(lo, lo + chunk)
        v = bias
        for tap in range(KERNEL):
            start = pl.multiple_of(at + lo + tap * DILATION, DILATION)
            v = v + dot(pad[pl.ds(start, chunk), :], wc[tap * inner : (tap + 1) * inner, :], NT)
        centred, inv = centre(v)
        normed = centred * inv
        a, g = gelu_pair(normed * gain + shift)
        a2[r, :] = a.astype(BF)
        rows = lo + lax.broadcasted_iota(jnp.int32, (chunk, 1), 0)
        grad = jnp.where(rows < limit, cot_ref[r, :].astype(F32) * scale, 0.0).astype(BF)
        gy[r, :] = grad
        vmod_ref[...] += fold(grad.astype(F32))
        kept.append((r, normed, inv, g))
    for r, normed, inv, g in kept:
        d = dot(gy[r, :], wo[...], NN) * g
        grad = norm_back(d * gain, normed, inv).astype(BF)
        gv_ref[r, :] = grad
        vin_ref[0] += fold(grad.astype(F32))
        vin_ref[1] += fold(d * normed)
        vin_ref[2] += fold(d)
        y = dot(a2[r, :], wo[...], NT) + out_bias
        y_ref[r, :] = (x_ref[r, :].astype(F32) + y).astype(BF)
    dw[...] += dot(gy[...], a2[...], TN)

    @pl.when(i == pl.num_programs(0) - 1)
    def _():
        for k, side, block in blocks_of(me_ref[0]):
            part = dw[pl.ds(pl.multiple_of(block * 160, 16), 160), :]
            put_block(k, side, slice(None), part, mine_ref, keep_ref, send_ref)


def conv_grad_kernel(
    me_ref, a1_ref, gv_ref, _mine, _keep, _send, mine_ref, keep_ref, send_ref, pad, dw,
    *, length, seqs,
):
    tap = pl.program_id(0)

    @pl.when(tap == 0)
    def _():
        zeros = jnp.zeros((REACH, pad.shape[2]), pad.dtype)
        for s in range(seqs):
            pad[s, 0:REACH, :] = zeros
            pad[s, REACH + length : 2 * REACH + length, :] = zeros
            pad[s, REACH : REACH + length, :] = a1_ref[s * length : (s + 1) * length, :]

    total = None
    for s in range(seqs):
        window = pad[s, pl.ds(pl.multiple_of(tap * DILATION, DILATION), length), :]
        part = dot(gv_ref[s * length : (s + 1) * length, :], window, TN)
        total = part if total is None else total + part
    dw[...] = total
    for k, side, block in blocks_of(me_ref[0]):
        part = dw[pl.ds(pl.multiple_of(block * 80, 16), 80), :]
        put_block(k, side, slice(None), part, mine_ref, keep_ref, send_ref)


def conv_back_kernel(
    me_ref, gv_ref, g_ref, c_ref, own, sib, vec_ref, *refs, tile, chunk, last
):
    if last:
        gu0_ref, a00_ref, a01_ref = refs[:3]
        gu_ref, vin_ref, mine_ref, keep_ref, send_ref, w, pad, sem, dw = refs[3:]
    else:
        gu_ref, vin_ref, w, pad, sem = refs[-5:]
    i = pl.program_id(0)
    inner = pad.shape[1]

    @pl.when(i == 0)
    def _():
        load_conv_weight(me_ref, own, sib, w, sem, False, inner)
        vin_ref[...] = jnp.zeros_like(vin_ref)
        if last:
            dw[...] = jnp.zeros_like(dw)
        fill_padded(pad, gv_ref, gv_ref.shape[0])
        load_conv_weight(me_ref, own, sib, w, sem, True, inner)

    gain = vec_ref[1:2, :]
    at = i * tile
    for lo in range(0, tile, chunk):
        r = slice(lo, lo + chunk)
        starts = [at + lo + shift * DILATION for shift in range(KERNEL - 1, -1, -1)]
        rows = [pad[pl.ds(pl.multiple_of(start, DILATION), chunk), :] for start in starts]
        v = dot(jnp.concatenate(rows, axis=1), w[...], NN)
        centred = c_ref[r, :].astype(F32)
        inv = lax.rsqrt(row_mean(centred * centred) + EPS)
        normed = centred * inv
        d = v * g_ref[r, :]
        grad = norm_back(d * gain, normed, inv).astype(BF)
        gu_ref[r, :] = grad
        vin_ref[0] += fold(grad.astype(F32))
        vin_ref[1] += fold(d * normed)
        vin_ref[2] += fold(d)
    if last:
        part = dot(gu_ref[...], a01_ref[...], TN)
        dw[...] += part + dot(gu0_ref[...], a00_ref[...], TN)

        @pl.when(i == pl.num_programs(0) - 1)
        def _():
            half = dw.shape[1] // 2
            for k, side, block in blocks_of(me_ref[0]):
                for h in range(2):
                    rows = pl.ds(pl.multiple_of(block * 80, 16), 80)
                    part = dw[rows, h * half : (h + 1) * half]
                    at = slice(h * 80, (h + 1) * 80)
                    put_block(k, side, at, part, mine_ref, keep_ref, send_ref)


def first_back_kernel(
    me_ref, len_ref, size_ref, x_ref, cot_ref, gu_ref, g_ref, own, sib, vec_ref, *refs,
    tile, chunk, length, first,
):
    gx_ref, vmod_ref, w, sem = refs[-4:]
    i = pl.program_id(0)

    @pl.when(i == 0)
    def _():
        load_in_weight(me_ref, own, sib, w, sem, False)
        vmod_ref[...] = jnp.zeros_like(vmod_ref)
        load_in_weight(me_ref, own, sib, w, sem, True)

    per = length // tile
    seq = first + i // per
    limit = len_ref[seq] - (i % per) * tile
    scale = 1.0 / size_ref[seq].astype(F32)
    gain = vec_ref[0:1, :]
    for lo in range(0, tile, chunk):
        r = slice(lo, lo + chunk)
        rows = lo + lax.broadcasted_iota(jnp.int32, (chunk, 1), 0)
        centred, inv = centre(x_ref[r, :].astype(F32))
        normed = centred * inv
        d = dot(gu_ref[r, :], w[...], NN) * g_ref[r, :].astype(F32)
        grad = norm_back(d * gain, normed, inv)
        out = jnp.where(rows < limit, cot_ref[r, :].astype(F32) * scale, 0.0)
        gx_ref[r, :] = (out + grad).astype(BF)
        vmod_ref[0] += fold(d * normed)
        vmod_ref[1] += fold(d)


def shards_kernel(w_in, w_conv, w_out, inner_ref, model_ref, in_ref, rest_ref, both_ref, vec_ref):
    rows = w_in.shape[0]
    width = w_conv.shape[1]
    part = w_in[...]
    in_ref[...] = part
    both_ref[:, : part.shape[1]] = part
    cut = part.shape[1]
    out = w_out[...].T
    parts = [out[:rows], out[rows:]] + [w_conv[tap].T for tap in range(KERNEL)]
    for t, part in enumerate(parts):
        rest_ref[:, t * width : (t + 1) * width] = part
        both_ref[:, cut + t * width : cut + (t + 1) * width] = part
    vec_ref[...] = jnp.zeros_like(vec_ref)
    vec_ref[0:6, :rows] = inner_ref[...].astype(F32)
    vec_ref[8:11, :] = model_ref[...].astype(F32)


def in_block_kernel(
    me_ref, z_ref, p0, p1, p2, p3, vec_ref, out_ref, inner_ref, model_ref, pieces, vecs
):
    rows, width = p0.shape
    half = out_ref.shape[1] // 2
    z = z_ref[0]
    for k, p in enumerate((p0, p1, p2, p3)):
        pieces[k] = p[:, :width].astype(F32)
    for d in range(4):
        row, lane = d // 2 * rows, d % 2 * half
        out_ref[row : row + rows, lane : lane + half] = pieces[z ^ d].astype(BF)
    for j in range(FS):
        vecs[me_ref[0] ^ j] = vec_ref[j]
    ci, co = inner_ref.shape[1] // FS, model_ref.shape[1] // FS
    for f in range(FS):
        inner_ref[:, f * ci : (f + 1) * ci] = vecs[f, 0:8, :ci]
        model_ref[:, f * co : (f + 1) * co] = vecs[f, 8:16, :]


def unpack_kernel(z_ref, b0, b1, b2, b3, p0, p1, p2, p3, in_ref, a_ref, b_ref, pieces, block, *, cut):
    rows = p0.shape[0]
    width = block.shape[1] // 4
    z = z_ref[0]
    for k, (p, lane) in enumerate(zip((p0, p1, p2, p3), cut)):
        pieces[k] = p[:, lane:].astype(F32)
    for d in range(4):
        piece = pieces[z ^ d]
        for t in range(block.shape[0] // rows):
            block[t * rows : (t + 1) * rows, d * width : (d + 1) * width] = piece[
                :, t * width : (t + 1) * width
            ]
    h = a_ref.shape[0]
    a_ref[...] = block[:h].astype(BF)
    b_ref[...] = block[h:].astype(BF)
    for k, b in enumerate((b0, b1, b2, b3)):
        in_ref[k] = b[...]


def pack_kernel(
    z_ref, keep_ref, got_ref, got_a_ref, got_b_ref, a_ref, b_ref, own_ref, o1, o2, o3, mine, pieces,
    *, groups, rows,
):
    h = a_ref.shape[0]
    first = keep_ref[0] + got_ref[0].astype(F32)
    mine[:h, :] = first[:h] + got_a_ref[0].astype(F32) + a_ref[...].astype(F32)
    mine[h:, :] = first[h:] + got_b_ref[0].astype(F32) + b_ref[...].astype(F32)
    for d in range(4):
        col = 0
        for width, starts in groups:
            for row, lane in starts[d]:
                pieces[d, :, col : col + width] = mine[row : row + rows, lane : lane + width]
                col += width
    z = z_ref[0]
    own_ref[...] = pieces[z]
    for k, out in ((1, o1), (2, o2), (3, o3)):
        out[...] = pieces[z ^ k].astype(BF)


def sums_kernel(me_ref, vin1a, vin1b, vin2, vmod0a, vmod0b, vmod2, counts, keep_ref, send_ref, inner, model):
    down = lambda v: jnp.sum(v, axis=0, keepdims=True)
    for j in range(3):
        inner[j : j + 1, :] = down(vin1a[j] + vin1b[j])
        inner[3 + j : 4 + j, :] = down(vin2[j])
    for j in range(2):
        model[j : j + 1, :] = down(vmod0a[j] + vmod0b[j])
    model[2:3, :] = down(vmod2[...])
    ci, co = inner.shape[1] // FS, model.shape[1] // FS
    keep_ref[...] = jnp.zeros_like(keep_ref)
    send_ref[...] = jnp.zeros_like(send_ref)
    yx, core = me_ref[0] // 2, me_ref[0] % 2
    for f in range(FS):
        k = yx ^ (f // 2)
        for dst, mine in ((keep_ref, core == f % 2), (send_ref, core != f % 2)):

            @pl.when(mine)
            def _():
                dst[k, 0:6, :ci] = inner[0:6, f * ci : (f + 1) * ci]
                dst[k, 8:11, :] = model[0:3, f * co : (f + 1) * co]
                dst[k, 11:12, :128] = counts[...]


def last_pack_kernel(
    z_ref, mine_ref, got_ref, got_a_ref, got_b_ref, a_ref, b_ref, v0, v1, v2, v3,
    own_ref, vec_ref, o1, o2, o3, mine, pieces,
):
    h = a_ref.shape[0]
    first = mine_ref[0] + got_ref[0].astype(F32)
    mine[:h, :] = first[:h] + got_a_ref[0].astype(F32) + a_ref[...].astype(F32)
    mine[h:, :] = first[h:] + got_b_ref[0].astype(F32) + b_ref[...].astype(F32)
    rows, width = own_ref.shape
    for d in range(4):
        row, lane = d // 2 * rows, d % 2 * width
        pieces[d] = mine[row : row + rows, lane : lane + width]
    vec = (v0[...] + v1[...]) + (v2[...] + v3[...])
    vec_ref[...] = vec
    high = vec.astype(BF)
    low = (vec - high.astype(F32)).astype(BF)
    z = z_ref[0]
    own_ref[...] = pieces[z]
    for k, out in ((1, o1), (2, o2), (3, o3)):
        out[:rows, :] = pieces[z ^ k].astype(BF)
        out[rows:, :] = jnp.concatenate([high, low], axis=1)


def last_kernel(own, vec, g1, g2, g3, in_ref, inner_ref, model_ref, counts_ref):
    rows = own.shape[0]
    total, sums = own[...], vec[...]
    co = vec.shape[1]
    for g in (g1, g2, g3):
        total = total + g[:rows, :].astype(F32)
        part = g[rows:, :].astype(F32)
        sums = sums + (part[:, :co] + part[:, co:])
    in_ref[...] = total
    inner_ref[...] = sums[0:6, : inner_ref.shape[1]]
    model_ref[...] = sums[8:11, :]
    counts_ref[...] = sums[11:12, :128]


def rest_kernel(own, g1, upper, lower, g3, conv_ref, out_ref):
    g2 = jnp.concatenate([upper[...].astype(F32), lower[...].astype(F32)])
    total = own[...] + g1[...].astype(F32) + (g2 + g3[...].astype(F32))
    width = conv_ref.shape[1]
    out_ref[...] = jnp.concatenate([total[:, :width], total[:, width : 2 * width]]).T
    for tap in range(KERNEL):
        conv_ref[tap] = total[:, (tap + 2) * width : (tap + 3) * width].T


def fs_perm(v, k):
    return lax.ppermute(v, "fsdp", xor_perm(FS, k))


def in_hbm(v):
    return pltpu.with_memory_space_constraint(v, pltpu.HBM)


def tie(*values):
    return lax.optimization_barrier(values)


def dp_perm(v, k):
    return lax.ppermute(v, "dp", xor_perm(4, k))


def split_rows(block, axis=0):
    h = block.shape[axis] // 32 * 16
    return lax.slice_in_dim(block, 0, h, axis=axis), lax.slice_in_dim(block, h, None, axis=axis)


def scatter_first(keep, got):
    keep_a, keep_b = split_rows(keep, 1)
    got_a, got_b = split_rows(got, 1)
    plus = lambda a, b: (a.astype(F32) + b.astype(F32)).astype(BF)
    send_a = jnp.stack([plus(keep_a[k - 1], got_a[k]) for k in (1, 3)])
    return fs_perm(send_a, 2), fs_perm(plus(keep_b[1:], got_b[2:]), 4)


def scatter_second(keep, got, from_a, from_b):
    keep_a, keep_b = split_rows(keep, 1)
    got_a, got_b = split_rows(got, 1)
    send_a = total_of([keep_a[1], got_a[2], from_a[1]])
    send_b = total_of([keep_b[0], got_b[1], from_b[1]])
    return fs_perm(send_a.astype(BF), 4), fs_perm(send_b.astype(BF), 2)


def pack(z, mine, got, from_a, from_b, last_a, last_b, groups, rows):
    total, cols = mine.shape[1:]
    h = last_a.shape[0]
    lanes = sum(width * len(starts[0]) for width, starts in groups)
    shape = (rows, lanes)
    return pl.pallas_call(
        functools.partial(pack_kernel, groups=groups, rows=rows),
        grid=(1,),
        in_specs=[SMEM] + [whole((1, n, cols)) for n in (total, total, h, total - h)]
        + [whole((h, cols)), whole((total - h, cols))],
        out_specs=[whole(shape)] * 4,
        out_shape=[jax.ShapeDtypeStruct(shape, d) for d in (F32, BF, BF, BF)],
        scratch_shapes=[pltpu.VMEM((total, cols), F32), pltpu.VMEM((4,) + shape, F32)],
        compiler_params=params(20),
        cost_estimate=cost(total * cols * 8, total * cols * 12),
        name="pack",
    )(z.reshape(1), mine, got, from_a, from_b, last_a, last_b)


def total_of(terms):
    return functools.reduce(lambda a, b: a + b, [t.astype(F32) for t in terms])


def generic_blocks(full):
    blocks = full.reshape(FS // 2, 2, full.shape[0] // FS, full.shape[1])
    return blocks[:, 0], blocks[:, 1]


def generic_full(keep, send):
    full = jnp.stack([keep, send.astype(F32)], axis=1)
    return full.reshape(FS, -1, full.shape[-1])


def generic_gather(w_in, w_conv, w_out):
    both = lambda w, rows, cols: lax.all_gather(
        lax.all_gather(w, "fsdp", axis=cols, tiled=True), "dp", axis=rows, tiled=True
    )
    w_in, w_conv, w_out = both(w_in, 0, 1), both(w_conv, 1, 2), both(w_out, 0, 1)
    taps, inner = w_conv.shape[0], w_conv.shape[1]
    part = w_in.T.reshape(FS, inner // FS, 2, inner).transpose(0, 2, 1, 3).reshape(-1, inner)
    conv = w_conv.transpose(2, 0, 1).reshape(FS, inner // FS, taps, inner)
    conv = conv.transpose(0, 2, 1, 3).reshape(-1, inner)
    pairs = zip(generic_blocks(w_out.T), generic_blocks(conv))
    return generic_blocks(part), [jnp.concatenate(p, axis=1) for p in pairs]


def generic_scatter(ins, rest):
    scatter = lambda w, rows, cols: lax.psum_scatter(
        lax.psum_scatter(w, "fsdp", scatter_dimension=cols, tiled=True),
        "dp", scatter_dimension=rows, tiled=True,
    )
    d_in, rest = generic_full(*ins), generic_full(*rest)
    inner = d_in.shape[-1]
    cut = rest.shape[1] - KERNEL * inner // FS
    d_out, d_conv = rest[:, :cut], rest[:, cut:]
    d_in = d_in.reshape(FS, 2, -1, inner).transpose(0, 2, 1, 3).reshape(inner, -1).T
    d_conv = d_conv.reshape(FS, KERNEL, -1, inner).transpose(1, 3, 0, 2).reshape(KERNEL, inner, inner)
    return scatter(d_in, 0, 1), scatter(d_conv, 1, 2), scatter(d_out.reshape(-1, inner).T, 0, 1)


def local(
    n_dp,
    n_fs,
    activations,
    cotangent,
    lengths,
    cluster_sizes,
    residue_types,
    w_in,
    w_conv,
    w_out,
    inner_shard,
    model_shard,
):
    seqs, length, model = activations.shape
    inner = w_in.shape[1] * n_fs
    tokens = seqs * length
    x = activations.reshape(tokens, model)
    cot = cotangent.reshape(tokens, model)
    x, cot = in_hbm(x), in_hbm(cot)
    staged = n_dp == 4 and n_fs == FS
    place, z = lax.axis_index("fsdp"), lax.axis_index("dp")
    me = place.reshape(1) if staged else jnp.zeros((1,), jnp.int32)
    ci, co = inner // FS, model // FS

    positions = jnp.arange(length, dtype=jnp.int32)
    valid = positions[None, :] < lengths[:, None]
    kinds = jnp.arange(TYPES, dtype=jnp.int32)
    hits = (residue_types[:, :, None] == kinds[None, None, :]) & valid[:, :, None]
    counts = jnp.sum(hits.astype(jnp.int32), axis=(0, 1))

    def sds(shape, dtype):
        return jax.ShapeDtypeStruct(shape, dtype)

    tile = 512
    per = length // tile
    row = lambda i: (i, 0)

    def first_norm(part, parts, vec, old):
        size, steps = tile, tokens // parts // tile
        block = pl.BlockSpec((size, model), lambda i: (part * steps + i, 0))
        return pl.pallas_call(
            functools.partial(first_norm_kernel, chunk=256),
            grid=(steps,),
            in_specs=[block, whole((8, model))] + [ANY] * len(old),
            out_specs=[block] * 2,
            out_shape=[pltpu.HBM((tokens, model), BF)] * 2,
            input_output_aliases={2: 0, 3: 1} if old else {},
            compiler_params=params(48),
            cost_estimate=cost(
                tokens * model * 60 / parts, tokens * model * 6 / parts, tokens * model * 2 / parts
            ),
            name="first_norm",
        )(x, vec, *old)

    def in_proj(part, parts, a0, own, sib, vec, old):
        steps = tokens // parts // tile
        wide = pl.BlockSpec((tile, model), lambda i: (part * steps + i, 0))
        narrow = pl.BlockSpec((tile, inner), lambda i: (part * steps + i, 0))
        return pl.pallas_call(
            functools.partial(
                in_proj_kernel, tile=tile, chunk=256, length=length, first=part * seqs // parts
            ),
            grid=(steps,),
            in_specs=[SMEM, SMEM, wide, ANY, ANY, whole((8, inner))] + [ANY] * len(old),
            out_specs=[narrow] * 3,
            out_shape=[pltpu.HBM((tokens, inner), d) for d in (BF, F32, BF)],
            input_output_aliases={6: 0, 7: 1, 8: 2} if old else {},
            scratch_shapes=[pltpu.VMEM((inner, model), BF), pltpu.SemaphoreType.DMA((16,))],
            compiler_params=params(48),
            cost_estimate=cost(
                2 * tokens * model * inner * 3 / parts, tokens * (model + 4 * inner) * 2 / parts
            ),
            name="in_proj",
        )(me, lengths, a0, own, sib, vec, *old)

    if staged:
        cut, width = model // 4, inner // 4
        lanes = (KERNEL + 2) * width
        shapes = [((ci, cut), BF), ((ci, lanes), BF), ((ci, cut + lanes), BF), ((16, co), F32)]
        in_t, rest_t, both, vec = small(shards_kernel, shapes, name="shards")(
            *map(in_hbm, (w_in.T, w_conv, w_out, inner_shard, model_shard))
        )
        got = [dp_perm(both, 1), dp_perm(in_t, 2), dp_perm(both, 3)]
        for k in (1, 2, 4):
            vec = jnp.stack([vec, fs_perm(vec, k)])
        vec, in_t, rest_t, *got = tie(vec, in_t, rest_t, *got)

        place_z = z.reshape(1)
        block, inner_vec, model_vec = small(
            in_block_kernel,
            [((2 * ci, inner), BF), ((8, inner), F32), ((8, model), F32)],
            [((4, ci, cut), F32), ((FS, 16, co), F32)],
            name="in_block",
        )(me, place_z, in_t, *got, vec.reshape(FS, 16, co))
        blocks = [block] + [fs_perm(block, k) for k in (2, 4, 6)]
        rest_z = [rest_t, got[0], dp_perm(rest_t, 2), got[2]]
        a0, g0 = first_norm(0, 1, model_vec, [])
        tied = tie(a0, g0, *rest_z, *blocks)
        (a0, g0), rest_z, blocks = tied[:2], tied[2:6], tied[6:]

        total = lanes // width * ci
        h = total // 32 * 16
        in_own, a, b = small(
            unpack_kernel,
            [((4, 2 * ci, inner), BF), ((h, inner), BF), ((total - h, inner), BF)],
            [((4, ci, lanes), F32), ((total, inner), F32)],
            cut=(0, cut, 0, cut),
            name="unpack",
        )(place_z, *blocks, *rest_z)
        in_sib = fs_perm(in_own, 1)
        w_a1, w_b2 = fs_perm(a, 2), fs_perm(b, 4)
        in_own, in_sib, w_a1, w_b2 = tie(in_own, in_sib, w_a1, w_b2)

        second = [fs_perm(a, 4), fs_perm(w_a1, 4), fs_perm(b, 2), fs_perm(w_b2, 2)]
        a1, g1, c1 = in_proj(0, 1, a0, in_own, in_sib, inner_vec, [])
        a1, g1, c1, a2, a3, b1, b3 = tie(a1, g1, c1, *second)
        pairs = [(a, b), (w_a1, b1), (a2, w_b2), (a3, b3)]
        own = jnp.stack([jnp.concatenate(p) for p in pairs])
        own, a1, g1, c1 = tie(own, a1, g1, c1)
        sib = fs_perm(own, 1)
    else:
        gather = lambda v: lax.all_gather(v, "fsdp", axis=1, tiled=True).astype(F32)
        inner_vec = jnp.pad(gather(inner_shard), ((0, 2), (0, 0)))
        model_vec = jnp.pad(gather(model_shard), ((0, 5), (0, 0)))
        (in_own, in_sib), (own, sib) = generic_gather(w_in, w_conv, w_out)
        a0, g0 = first_norm(0, 1, model_vec, [])
        a1, g1, c1 = in_proj(0, 1, a0, in_own, in_sib, inner_vec, [])

    wide, narrow = pl.BlockSpec((tile, model), row), pl.BlockSpec((tile, inner), row)
    rows = co + KERNEL * ci
    shapes = [((1, rows, inner), F32), ((3, rows, inner), BF), ((4, rows, inner), BF)]
    block_out, gv, *out_parts, vin2, vmod2 = pl.pallas_call(
        functools.partial(middle_kernel, tile=tile, chunk=256, length=length),
        grid=(tokens // tile,),
        in_specs=[SMEM, SMEM, SMEM, pl.BlockSpec((length, inner), lambda i: (i // per, 0)),
                  wide, wide, ANY, ANY, whole((8, model)), whole((8, inner))],
        out_specs=[wide, narrow, *(whole((n, co, inner)) for n in (1, 3, 4)),
                   whole((3, 8, inner)), whole((8, model))],
        out_shape=[sds((tokens, model), BF), sds((tokens, inner), BF), *(sds(*v) for v in shapes),
                   sds((3, 8, inner), F32), sds((8, model), F32)],
        scratch_shapes=[
            pltpu.VMEM((KERNEL * inner, inner), BF),
            pltpu.VMEM((model, inner), BF),
            pltpu.VMEM((length + 2 * REACH, inner), BF),
            pltpu.VMEM((tile, inner), BF),
            pltpu.VMEM((tile, model), BF),
            pltpu.VMEM((model, inner), F32),
            pltpu.SemaphoreType.DMA((40,)),
            pltpu.SemaphoreType.DMA((8,)),
        ],
        compiler_params=params(48),
        cost_estimate=cost(2 * tokens * inner * (KERNEL * inner + 3 * model) * 2, tokens * model * 10),
        name="middle",
    )(me, lengths, cluster_sizes, a1, x, cot, own, sib, model_vec, inner_vec)

    block = lambda n: pl.BlockSpec((n, ci, inner), lambda k: (0, k + 2, 0))
    mine, keep, send = pl.pallas_call(
        functools.partial(conv_grad_kernel, length=length, seqs=seqs),
        grid=(KERNEL,),
        in_specs=[SMEM, whole((tokens, inner)), whole((tokens, inner)), ANY, ANY, ANY],
        out_specs=[block(n) for n in (1, 3, 4)],
        out_shape=[sds(*v) for v in shapes],
        input_output_aliases={3: 0, 4: 1, 5: 2},
        scratch_shapes=[
            pltpu.VMEM((seqs, length + 2 * REACH, inner), BF),
            pltpu.VMEM((inner, inner), F32),
        ],
        compiler_params=params(48),
        cost_estimate=cost(2 * tokens * KERNEL * inner * inner * 1.3, tokens * inner * 4),
        name="conv_grad",
    )(me, a1, gv, *out_parts)

    def conv_back(s, extra):
        last = bool(extra)
        at = lambda i: (s * per + i, 0)
        once = lambda i: (s, 0)
        part = pl.BlockSpec((tile, inner), at)
        ins = [SMEM, pl.BlockSpec((length, inner), once), part, part, ANY, ANY, whole((8, inner))]
        outs = [pl.BlockSpec((tile, inner), row), whole((3, 8, inner))]
        shapes = [sds((length, inner), BF), sds((3, 8, inner), F32)]
        scratch = [
            pltpu.VMEM((KERNEL * inner, inner), BF),
            pltpu.VMEM((length + 2 * REACH, inner), BF),
            pltpu.SemaphoreType.DMA((40,)),
        ]
        if last:
            ins += [
                pl.BlockSpec((tile, inner), row),
                pl.BlockSpec((tile, model), row),
                pl.BlockSpec((tile, model), at),
            ]
            for n, dtype in ((1, F32), (3, BF), (4, BF)):
                outs += [whole((n, 2 * ci, inner))]
                shapes += [sds((n, 2 * ci, inner), dtype)]
            scratch += [pltpu.VMEM((inner, model), F32)]
        return pl.pallas_call(
            functools.partial(conv_back_kernel, tile=tile, chunk=256, last=last),
            grid=(per,),
            in_specs=ins,
            out_specs=outs,
            out_shape=shapes,
            scratch_shapes=scratch,
            compiler_params=params(48),
            cost_estimate=cost(
                2 * length * inner * (KERNEL * inner + 2 * model * last) * 1.5, length * inner * 12
            ),
            name="conv_back",
        )(me, gv, g1, c1, own, sib, inner_vec, *extra)

    def first_back(s, gu, old):
        tile = 256
        per = length // tile
        at = lambda i: (s * per + i, 0)
        wide = pl.BlockSpec((tile, model), at)
        ins = [SMEM, SMEM, SMEM, wide, wide, pl.BlockSpec((tile, inner), row), wide, ANY, ANY]
        return pl.pallas_call(
            functools.partial(first_back_kernel, tile=tile, chunk=256, length=length, first=s),
            grid=(per,),
            in_specs=ins + [whole((8, model))] + [ANY] * len(old),
            out_specs=[wide, whole((2, 8, model))],
            out_shape=[sds((tokens, model), BF), sds((2, 8, model), F32)],
            input_output_aliases={10: 0} if old else {},
            scratch_shapes=[pltpu.VMEM((inner, model), BF), pltpu.SemaphoreType.DMA((16,))],
            compiler_params=params(48),
            cost_estimate=cost(2 * length * model * inner * 4, length * model * 8),
            name="first_back",
        )(me, lengths, cluster_sizes, x, cot, gu, g0, in_own, in_sib, model_vec, *old)

    if staged:
        send, gv = tie(send, gv)
        got = fs_perm(send, 1)
        gu0, vin1a = conv_back(0, [])
        got, gu0 = tie(got, gu0)

        first = scatter_first(keep, got)
        gu1, vin1b, in_mine, in_keep, in_send = conv_back(1, [gu0, a0, a0])
        *first, in_send, gu1 = tie(*first, in_send, gu1)

        second = scatter_second(keep, got, *first)
        in_got = fs_perm(in_send, 1)
        grad_x, vmod0a = first_back(0, gu0, [])
        *second, in_got, grad_x = tie(*second, in_got, grad_x)

        width = inner // 4
        groups = [(width, [[(t * ci, d * width) for t in range(KERNEL + 2)] for d in range(4)])]
        own, *sends = pack(z, mine, got, *first, *second, groups, ci)
        from_1, from_3 = dp_perm(sends[0], 1), dp_perm(sends[2], 3)
        in_first = scatter_first(in_keep, in_got)
        grad_x, vmod0b = first_back(1, gu1, [grad_x])
        own, from_1, from_3, send_2, vmod0b, *in_first = tie(
            own, from_1, from_3, sends[1], vmod0b, *in_first
        )

        counts = jnp.pad(counts.astype(F32), (0, 128 - TYPES)).reshape(1, 128)
        sums, send = small(
            sums_kernel,
            [((4, 16, co), F32)] * 2,
            [((8, inner), F32), ((8, model), F32)],
            name="sums",
        )(me, vin1a, vin1b, vin2, vmod0a, vmod0b, vmod2, counts)
        got = fs_perm(send, 1)
        in_second = scatter_second(in_keep, in_got, *in_first)
        upper = dp_perm(send_2[: ci // 2], 2)
        sums, got, upper, *in_second = tie(sums, got, upper, *in_second)

        sums = sums + got
        lower = dp_perm(send_2[ci // 2 :], 2)
        got = [fs_perm(sums[k], 2 * k) for k in (1, 2, 3)]
        sums, lower, *got = tie(sums, lower, *got)

        shape = (ci, model // 4)
        piece = ((ci + 16, model // 4), BF)
        in_own, vec, *sends = small(
            last_pack_kernel,
            [(shape, F32), ((16, co), F32), piece, piece, piece],
            [((2 * ci, inner), F32), ((4,) + shape, F32)],
            name="last_pack",
        )(z.reshape(1), in_mine, in_got, *in_first, *in_second, sums[0], *got)
        got = [dp_perm(v, k) for k, v in zip((1, 2, 3), sends)]
        d_conv, d_out = small(
            rest_kernel, [((KERNEL, width, ci), F32), ((width, co), F32)], name="rest"
        )(own, from_1, upper, lower, from_3)
        d_in, d_inner, d_model, counts = small(
            last_kernel,
            [(shape, F32), ((6, ci), F32), ((3, co), F32), ((1, 128), F32)],
            name="last",
        )(in_own, vec, *got)
        d_in = d_in.T
        type_counts = counts[0, :TYPES].astype(jnp.int32)
    else:
        gu0, vin1a = conv_back(0, [])
        gu1, vin1b, in_mine, in_keep, in_send = conv_back(1, [gu0, a0, a0])
        grad_x, vmod0a = first_back(0, gu0, [])
        grad_x, vmod0b = first_back(1, gu1, [grad_x])
        down = lambda v: jnp.sum(v, axis=-2)
        type_counts, d_inner, d_model = lax.psum(
            (
                counts,
                jnp.concatenate([down(vin1a + vin1b), down(vin2)]),
                jnp.concatenate([down(vmod0a + vmod0b), down(vmod2)[None]]),
            ),
            ("dp", "fsdp"),
        )
        ours = lambda v, n: lax.dynamic_slice_in_dim(v, place * n, n, 1)
        d_inner, d_model = ours(d_inner, inner_shard.shape[1]), ours(d_model, model_shard.shape[1])
        with_mine = lambda m, k: jnp.concatenate([m, k.astype(F32)])
        d_in, d_conv, d_out = generic_scatter(
            (with_mine(in_mine, in_keep), in_send), (with_mine(mine, keep), send)
        )

    return (
        block_out.reshape(activations.shape),
        grad_x.reshape(activations.shape),
        d_in,
        d_conv,
        d_out,
        d_inner,
        d_model,
        type_counts,
    )


def solution(mesh):
    rows = ("dp", "fsdp")
    return jax.shard_map(
        functools.partial(local, mesh.shape["dp"], mesh.shape["fsdp"]),
        mesh=mesh,
        in_specs=(
            P(rows, None, None),
            P(rows, None, None),
            P(rows),
            P(rows),
            P(rows, None),
            P("dp", "fsdp"),
            P(None, "dp", "fsdp"),
            P("dp", "fsdp"),
            P(None, "fsdp"),
            P(None, "fsdp"),
        ),
        out_specs=(
            P(rows, None, None),
            P(rows, None, None),
            P("dp", "fsdp"),
            P(None, "dp", "fsdp"),
            P("dp", "fsdp"),
            P(None, "fsdp"),
            P(None, "fsdp"),
            P(),
        ),
        check_vma=False,
    )
```

```python
import functools

import jax
import jax.numpy as jnp
from jax import lax
from jax.experimental import pallas as pl
from jax.experimental.pallas import tpu as pltpu
from jax.sharding import PartitionSpec as P

KERNEL = 5
DILATION = 32
REACH = DILATION * (KERNEL - 1) // 2
TYPES = 25
FS = 8

EPS = 1e-05
INV_ROOT_TWO = 0.7071067811865476
INV_ROOT_TWO_PI = 0.3989422804014327

BF = jnp.bfloat16
F32 = jnp.float32
NT = (((1,), (1,)), ((), ()))
NN = (((1,), (0,)), ((), ()))
TN = (((0,), (0,)), ((), ()))
ANY = pl.BlockSpec(memory_space=pl.ANY)
SMEM = pl.BlockSpec(memory_space=pltpu.SMEM)


def dot(a, b, dims):
    return lax.dot_general(a, b, dims, preferred_element_type=F32)


def params(mib):
    return pltpu.CompilerParams(
        dimension_semantics=("arbitrary",), vmem_limit_bytes=mib * 1024 * 1024
    )


def cost(flops, nbytes, trans=0):
    return pl.CostEstimate(
        flops=int(flops / 10), bytes_accessed=int(nbytes / 10), transcendentals=int(trans / 10)
    )


def small(kernel, shapes, scratch=(), mib=20, name=None, **static):
    def call(*args):
        specs = [SMEM if a.dtype == jnp.int32 else whole(a.shape) for a in args]
        return pl.pallas_call(
            functools.partial(kernel, **static),
            grid=(1,),
            in_specs=specs,
            out_specs=[whole(v) for v, _ in shapes],
            out_shape=[jax.ShapeDtypeStruct(*v) for v in shapes],
            scratch_shapes=[pltpu.VMEM(*v) for v in scratch],
            compiler_params=params(mib),
            name=name,
        )(*args)

    return call


def whole(shape):
    return pl.BlockSpec(shape, lambda *_: (0,) * len(shape))


def row_mean(v):
    return jnp.mean(v, axis=-1, keepdims=True)


def centre(v):
    centred = v - row_mean(v)
    return centred, lax.rsqrt(row_mean(centred * centred) + EPS)


def gelu_pair(h):
    phi = 0.5 * (1.0 + lax.erf(h * INV_ROOT_TWO))
    dens = jnp.exp(-0.5 * h * h) * INV_ROOT_TWO_PI
    return h * phi, phi + h * dens


def norm_back(scaled, normed, inv):
    return inv * (scaled - row_mean(scaled) - normed * row_mean(scaled * normed))


def fold(v):
    return jnp.sum(v.reshape(v.shape[0] // 8, 8, v.shape[1]), axis=0)


def rows_at(i, size):
    return pl.ds(pl.multiple_of(i * size, size), size)


def xor_perm(n, k):
    return [(i, i ^ k) for i in range(n)]


def blocks_of(me):
    yx, core = me // 2, me % 2
    for k in range(FS // 2):
        for side in range(2):
            yield k, side, (yx ^ k) * 2 + (core if side == 0 else 1 - core)


def first_norm_kernel(x_ref, vec_ref, *refs, chunk):
    a_ref, g_ref = refs[-2:]
    gain, shift = vec_ref[0:1, :], vec_ref[1:2, :]
    for lo in range(0, x_ref.shape[0], chunk):
        r = slice(lo, lo + chunk)
        centred, inv = centre(x_ref[r, :].astype(F32))
        a, g = gelu_pair(centred * inv * gain + shift)
        a_ref[r, :] = a.astype(BF)
        g_ref[r, :] = g.astype(BF)


def put_block(k, side, rows, part, mine_ref, keep_ref, send_ref):
    if side == 1:
        send_ref[k, rows, :] = part.astype(BF)
    elif k == 0:
        mine_ref[0, rows, :] = part
    else:
        keep_ref[k - 1, rows, :] = part.astype(BF)


def load_in_weight(me_ref, own, sib, dst, sem, wait):
    half = dst.shape[1] // 2
    n = 0
    for k, side, block in blocks_of(me_ref[0]):
        src = own if side == 0 else sib
        for h in range(2):
            c = pltpu.make_async_copy(
                src.at[k, pl.ds(h * 80, 80), :],
                dst.at[pl.ds(pl.multiple_of(block * 80, 16), 80), pl.ds(h * half, half)],
                sem.at[n],
            )
            n += 1
            c.wait() if wait else c.start()


def in_proj_kernel(
    me_ref, len_ref, a0_ref, own, sib, vec_ref, *refs, tile, chunk, length, first
):
    a_ref, g_ref, c_ref, w, sem = refs[-5:]
    i = pl.program_id(0)

    @pl.when(i == 0)
    def _():
        load_in_weight(me_ref, own, sib, w, sem, False)
        load_in_weight(me_ref, own, sib, w, sem, True)

    bias, gain, shift = (vec_ref[j : j + 1, :] for j in range(3))
    per = length // tile
    limit = len_ref[first + i // per] - (i % per) * tile
    for lo in range(0, tile, chunk):
        r = slice(lo, lo + chunk)
        v = dot(a0_ref[r, :], w[...], NT) + bias
        centred, inv = centre(v)
        a, g = gelu_pair(centred * inv * gain + shift)
        keep = lo + lax.broadcasted_iota(jnp.int32, (chunk, 1), 0) < limit
        a_ref[r, :] = jnp.where(keep, a, 0.0).astype(BF)
        g_ref[r, :] = jnp.where(keep, g, 0.0)
        c_ref[r, :] = centred.astype(BF)


def pieces_of(src, k, row, size):
    if not isinstance(src, (tuple, list)):
        return [(src.at[k, pl.ds(row, size), :], 0, size)]
    a01, b02, a23, b13 = src
    h = a01.shape[1]
    found = []
    cut = min(max(h - row, 0), size)
    if cut:
        found.append(((a01, a23)[k // 2].at[k % 2, pl.ds(row, cut), :], 0, cut))
    if cut < size:
        half = (b02, b13)[k % 2].at[k // 2, pl.ds(row + cut - h, size - cut), :]
        found.append((half, cut, size - cut))
    return found


def load_conv_weight(me_ref, own, sib, dst, sem, wait, inner):
    n = 0
    for k, side, block in blocks_of(me_ref[0]):
        src = own if side == 0 else sib
        for tap in range(KERNEL):
            for piece, offset, size in pieces_of(src, k, (tap + 2) * 80, 80):
                row = pl.multiple_of(tap * inner + block * 80 + offset, 16)
                c = pltpu.make_async_copy(piece, dst.at[pl.ds(row, size), :], sem.at[n])
                n += 1
                c.wait() if wait else c.start()


def fill_padded(pad, src_ref, length):
    zeros = jnp.zeros((REACH, pad.shape[1]), pad.dtype)
    pad[0:REACH, :] = zeros
    pad[REACH + length : 2 * REACH + length, :] = zeros
    pad[REACH : REACH + length, :] = src_ref[...]


def load_out_weight(me_ref, own, sib, dst, sem, wait):
    n = 0
    for k, side, block in blocks_of(me_ref[0]):
        src = own if side == 0 else sib
        for piece, offset, size in pieces_of(src, k, 0, 160):
            row = pl.multiple_of(block * 160 + offset, 16)
            c = pltpu.make_async_copy(piece, dst.at[pl.ds(row, size), :], sem.at[n])
            n += 1
            c.wait() if wait else c.start()


def middle_kernel(
    me_ref, len_ref, size_ref, a1_ref, x_ref, cot_ref, own, sib,
    model_ref, inner_ref, y_ref, gv_ref, mine_ref, keep_ref, send_ref, vin_ref, vmod_ref,
    wc, wo, pad, a2, gy, dw, sem_c, sem_o, *, tile, chunk, length,
):
    i = pl.program_id(0)
    inner = pad.shape[1]
    per = length // tile

    @pl.when(i == 0)
    def _():
        load_conv_weight(me_ref, own, sib, wc, sem_c, False, inner)
        load_out_weight(me_ref, own, sib, wo, sem_o, False)
        vin_ref[...] = jnp.zeros_like(vin_ref)
        vmod_ref[...] = jnp.zeros_like(vmod_ref)
        dw[...] = jnp.zeros_like(dw)

    @pl.when(i % per == 0)
    def _():
        fill_padded(pad, a1_ref, length)

    @pl.when(i == 0)
    def _():
        load_conv_weight(me_ref, own, sib, wc, sem_c, True, inner)
        load_out_weight(me_ref, own, sib, wo, sem_o, True)

    seq = i // per
    at = (i % per) * tile
    limit = len_ref[seq] - at
    scale = 1.0 / size_ref[seq].astype(F32)
    bias, gain, shift = (inner_ref[j : j + 1, :] for j in range(3, 6))
    out_bias = model_ref[2:3, :]
    kept = []
    for lo in range(0, tile, chunk):
        r = slice(lo, lo + chunk)
        v = bias
        for tap in range(KERNEL):
            start = pl.multiple_of(at + lo + tap * DILATION, DILATION)
            v = v + dot(pad[pl.ds(start, chunk), :], wc[tap * inner : (tap + 1) * inner, :], NT)
        centred, inv = centre(v)
        normed = centred * inv
        a, g = gelu_pair(normed * gain + shift)
        a2[r, :] = a.astype(BF)
        rows = lo + lax.broadcasted_iota(jnp.int32, (chunk, 1), 0)
        grad = jnp.where(rows < limit, cot_ref[r, :].astype(F32) * scale, 0.0).astype(BF)
        gy[r, :] = grad
        vmod_ref[...] += fold(grad.astype(F32))
        kept.append((r, normed, inv, g))
    for r, normed, inv, g in kept:
        d = dot(gy[r, :], wo[...], NN) * g
        grad = norm_back(d * gain, normed, inv).astype(BF)
        gv_ref[r, :] = grad
        vin_ref[0] += fold(grad.astype(F32))
        vin_ref[1] += fold(d * normed)
        vin_ref[2] += fold(d)
        y = dot(a2[r, :], wo[...], NT) + out_bias
        y_ref[r, :] = (x_ref[r, :].astype(F32) + y).astype(BF)
    dw[...] += dot(gy[...], a2[...], TN)

    @pl.when(i == pl.num_programs(0) - 1)
    def _():
        for k, side, block in blocks_of(me_ref[0]):
            part = dw[pl.ds(pl.multiple_of(block * 160, 16), 160), :]
            put_block(k, side, slice(None), part, mine_ref, keep_ref, send_ref)


def conv_grad_kernel(
    me_ref, a1_ref, gv_ref, _mine, _keep, _send, mine_ref, keep_ref, send_ref, pad, dw,
    *, length, seqs,
):
    tap = pl.program_id(0)

    @pl.when(tap == 0)
    def _():
        zeros = jnp.zeros((REACH, pad.shape[2]), pad.dtype)
        for s in range(seqs):
            pad[s, 0:REACH, :] = zeros
            pad[s, REACH + length : 2 * REACH + length, :] = zeros
            pad[s, REACH : REACH + length, :] = a1_ref[s * length : (s + 1) * length, :]

    total = None
    for s in range(seqs):
        window = pad[s, pl.ds(pl.multiple_of(tap * DILATION, DILATION), length), :]
        part = dot(gv_ref[s * length : (s + 1) * length, :], window, TN)
        total = part if total is None else total + part
    dw[...] = total
    for k, side, block in blocks_of(me_ref[0]):
        part = dw[pl.ds(pl.multiple_of(block * 80, 16), 80), :]
        put_block(k, side, slice(None), part, mine_ref, keep_ref, send_ref)


def conv_back_kernel(
    me_ref, gv_ref, g_ref, c_ref, own, sib, vec_ref, *refs, tile, chunk, last
):
    if last:
        gu0_ref, a00_ref, a01_ref = refs[:3]
        gu_ref, vin_ref, mine_ref, keep_ref, send_ref, w, pad, sem, dw = refs[3:]
    else:
        gu_ref, vin_ref, w, pad, sem = refs[-5:]
    i = pl.program_id(0)
    inner = pad.shape[1]

    @pl.when(i == 0)
    def _():
        load_conv_weight(me_ref, own, sib, w, sem, False, inner)
        vin_ref[...] = jnp.zeros_like(vin_ref)
        if last:
            dw[...] = jnp.zeros_like(dw)
        fill_padded(pad, gv_ref, gv_ref.shape[0])
        load_conv_weight(me_ref, own, sib, w, sem, True, inner)

    gain = vec_ref[1:2, :]
    at = i * tile
    for lo in range(0, tile, chunk):
        r = slice(lo, lo + chunk)
        starts = [at + lo + shift * DILATION for shift in range(KERNEL - 1, -1, -1)]
        rows = [pad[pl.ds(pl.multiple_of(start, DILATION), chunk), :] for start in starts]
        v = dot(jnp.concatenate(rows, axis=1), w[...], NN)
        centred = c_ref[r, :].astype(F32)
        inv = lax.rsqrt(row_mean(centred * centred) + EPS)
        normed = centred * inv
        d = v * g_ref[r, :]
        grad = norm_back(d * gain, normed, inv).astype(BF)
        gu_ref[r, :] = grad
        vin_ref[0] += fold(grad.astype(F32))
        vin_ref[1] += fold(d * normed)
        vin_ref[2] += fold(d)
    if last:
        part = dot(gu_ref[...], a01_ref[...], TN)
        dw[...] += part + dot(gu0_ref[...], a00_ref[...], TN)

        @pl.when(i == pl.num_programs(0) - 1)
        def _():
            half = dw.shape[1] // 2
            for k, side, block in blocks_of(me_ref[0]):
                for h in range(2):
                    rows = pl.ds(pl.multiple_of(block * 80, 16), 80)
                    part = dw[rows, h * half : (h + 1) * half]
                    at = slice(h * 80, (h + 1) * 80)
                    put_block(k, side, at, part, mine_ref, keep_ref, send_ref)


def first_back_kernel(
    me_ref, len_ref, size_ref, x_ref, cot_ref, gu_ref, g_ref, own, sib, vec_ref, *refs,
    tile, chunk, length, first,
):
    gx_ref, vmod_ref, w, sem = refs[-4:]
    i = pl.program_id(0)

    @pl.when(i == 0)
    def _():
        load_in_weight(me_ref, own, sib, w, sem, False)
        vmod_ref[...] = jnp.zeros_like(vmod_ref)
        load_in_weight(me_ref, own, sib, w, sem, True)

    per = length // tile
    seq = first + i // per
    limit = len_ref[seq] - (i % per) * tile
    scale = 1.0 / size_ref[seq].astype(F32)
    gain = vec_ref[0:1, :]
    for lo in range(0, tile, chunk):
        r = slice(lo, lo + chunk)
        rows = lo + lax.broadcasted_iota(jnp.int32, (chunk, 1), 0)
        centred, inv = centre(x_ref[r, :].astype(F32))
        normed = centred * inv
        d = dot(gu_ref[r, :], w[...], NN) * g_ref[r, :].astype(F32)
        grad = norm_back(d * gain, normed, inv)
        out = jnp.where(rows < limit, cot_ref[r, :].astype(F32) * scale, 0.0)
        gx_ref[r, :] = (out + grad).astype(BF)
        vmod_ref[0] += fold(d * normed)
        vmod_ref[1] += fold(d)


def shards_kernel(w_in, w_conv, w_out, inner_ref, model_ref, in_ref, rest_ref, both_ref, vec_ref):
    rows = w_in.shape[0]
    width = w_conv.shape[1]
    part = w_in[...]
    in_ref[...] = part
    both_ref[:, : part.shape[1]] = part
    cut = part.shape[1]
    out = w_out[...].T
    parts = [out[:rows], out[rows:]] + [w_conv[tap].T for tap in range(KERNEL)]
    for t, part in enumerate(parts):
        rest_ref[:, t * width : (t + 1) * width] = part
        both_ref[:, cut + t * width : cut + (t + 1) * width] = part
    vec_ref[...] = jnp.zeros_like(vec_ref)
    vec_ref[0:6, :rows] = inner_ref[...].astype(F32)
    vec_ref[8:11, :] = model_ref[...].astype(F32)


def in_block_kernel(
    me_ref, z_ref, p0, p1, p2, p3, vec_ref, out_ref, inner_ref, model_ref, pieces, vecs
):
    rows, width = p0.shape
    half = out_ref.shape[1] // 2
    z = z_ref[0]
    for k, p in enumerate((p0, p1, p2, p3)):
        pieces[k] = p[:, :width].astype(F32)
    for d in range(4):
        row, lane = d // 2 * rows, d % 2 * half
        out_ref[row : row + rows, lane : lane + half] = pieces[z ^ d].astype(BF)
    for j in range(FS):
        vecs[me_ref[0] ^ j] = vec_ref[j]
    ci, co = inner_ref.shape[1] // FS, model_ref.shape[1] // FS
    for f in range(FS):
        inner_ref[:, f * ci : (f + 1) * ci] = vecs[f, 0:8, :ci]
        model_ref[:, f * co : (f + 1) * co] = vecs[f, 8:16, :]


def unpack_kernel(z_ref, b0, b1, b2, b3, p0, p1, p2, p3, in_ref, a_ref, b_ref, pieces, block, *, cut):
    rows = p0.shape[0]
    width = block.shape[1] // 4
    z = z_ref[0]
    for k, (p, lane) in enumerate(zip((p0, p1, p2, p3), cut)):
        pieces[k] = p[:, lane:].astype(F32)
    for d in range(4):
        piece = pieces[z ^ d]
        for t in range(block.shape[0] // rows):
            block[t * rows : (t + 1) * rows, d * width : (d + 1) * width] = piece[
                :, t * width : (t + 1) * width
            ]
    h = a_ref.shape[0]
    a_ref[...] = block[:h].astype(BF)
    b_ref[...] = block[h:].astype(BF)
    for k, b in enumerate((b0, b1, b2, b3)):
        in_ref[k] = b[...]


def pack_kernel(
    z_ref, keep_ref, got_ref, got_a_ref, got_b_ref, a_ref, b_ref, own_ref, o1, o2, o3, mine, pieces,
    *, groups, rows,
):
    h = a_ref.shape[0]
    first = keep_ref[0] + got_ref[0].astype(F32)
    mine[:h, :] = first[:h] + got_a_ref[0].astype(F32) + a_ref[...].astype(F32)
    mine[h:, :] = first[h:] + got_b_ref[0].astype(F32) + b_ref[...].astype(F32)
    for d in range(4):
        col = 0
        for width, starts in groups:
            for row, lane in starts[d]:
                pieces[d, :, col : col + width] = mine[row : row + rows, lane : lane + width]
                col += width
    z = z_ref[0]
    own_ref[...] = pieces[z]
    for k, out in ((1, o1), (2, o2), (3, o3)):
        out[...] = pieces[z ^ k].astype(BF)


def sums_kernel(me_ref, vin1a, vin1b, vin2, vmod0a, vmod0b, vmod2, counts, keep_ref, send_ref, inner, model):
    down = lambda v: jnp.sum(v, axis=0, keepdims=True)
    for j in range(3):
        inner[j : j + 1, :] = down(vin1a[j] + vin1b[j])
        inner[3 + j : 4 + j, :] = down(vin2[j])
    for j in range(2):
        model[j : j + 1, :] = down(vmod0a[j] + vmod0b[j])
    model[2:3, :] = down(vmod2[...])
    ci, co = inner.shape[1] // FS, model.shape[1] // FS
    keep_ref[...] = jnp.zeros_like(keep_ref)
    send_ref[...] = jnp.zeros_like(send_ref)
    yx, core = me_ref[0] // 2, me_ref[0] % 2
    for f in range(FS):
        k = yx ^ (f // 2)
        for dst, mine in ((keep_ref, core == f % 2), (send_ref, core != f % 2)):

            @pl.when(mine)
            def _():
                dst[k, 0:6, :ci] = inner[0:6, f * ci : (f + 1) * ci]
                dst[k, 8:11, :] = model[0:3, f * co : (f + 1) * co]
                dst[k, 11:12, :128] = counts[...]


def last_pack_kernel(
    z_ref, mine_ref, got_ref, got_a_ref, got_b_ref, a_ref, b_ref, v0, v1, v2, v3,
    own_ref, vec_ref, o1, o2, o3, mine, pieces,
):
    h = a_ref.shape[0]
    first = mine_ref[0] + got_ref[0].astype(F32)
    mine[:h, :] = first[:h] + got_a_ref[0].astype(F32) + a_ref[...].astype(F32)
    mine[h:, :] = first[h:] + got_b_ref[0].astype(F32) + b_ref[...].astype(F32)
    rows, width = own_ref.shape
    for d in range(4):
        row, lane = d // 2 * rows, d % 2 * width
        pieces[d] = mine[row : row + rows, lane : lane + width]
    vec = (v0[...] + v1[...]) + (v2[...] + v3[...])
    vec_ref[...] = vec
    high = vec.astype(BF)
    low = (vec - high.astype(F32)).astype(BF)
    z = z_ref[0]
    own_ref[...] = pieces[z]
    for k, out in ((1, o1), (2, o2), (3, o3)):
        out[:rows, :] = pieces[z ^ k].astype(BF)
        out[rows:, :] = jnp.concatenate([high, low], axis=1)


def last_kernel(own, vec, g1, g2, g3, in_ref, inner_ref, model_ref, counts_ref):
    rows = own.shape[0]
    total, sums = own[...], vec[...]
    co = vec.shape[1]
    for g in (g1, g2, g3):
        total = total + g[:rows, :].astype(F32)
        part = g[rows:, :].astype(F32)
        sums = sums + (part[:, :co] + part[:, co:])
    in_ref[...] = total
    inner_ref[...] = sums[0:6, : inner_ref.shape[1]]
    model_ref[...] = sums[8:11, :]
    counts_ref[...] = sums[11:12, :128]


def rest_kernel(own, g1, upper, lower, g3, conv_ref, out_ref):
    g2 = jnp.concatenate([upper[...].astype(F32), lower[...].astype(F32)])
    total = own[...] + g1[...].astype(F32) + (g2 + g3[...].astype(F32))
    width = conv_ref.shape[1]
    out_ref[...] = jnp.concatenate([total[:, :width], total[:, width : 2 * width]]).T
    for tap in range(KERNEL):
        conv_ref[tap] = total[:, (tap + 2) * width : (tap + 3) * width].T


def fs_perm(v, k):
    return lax.ppermute(v, "fsdp", xor_perm(FS, k))


def in_hbm(v):
    return pltpu.with_memory_space_constraint(v, pltpu.HBM)


def tie(*values):
    return lax.optimization_barrier(values)


def dp_perm(v, k):
    return lax.ppermute(v, "dp", xor_perm(4, k))


def split_rows(block, axis=0):
    h = block.shape[axis] // 32 * 16
    return lax.slice_in_dim(block, 0, h, axis=axis), lax.slice_in_dim(block, h, None, axis=axis)


def scatter_first(keep, got):
    keep_a, keep_b = split_rows(keep, 1)
    got_a, got_b = split_rows(got, 1)
    plus = lambda a, b: (a.astype(F32) + b.astype(F32)).astype(BF)
    send_a = jnp.stack([plus(keep_a[k - 1], got_a[k]) for k in (1, 3)])
    return fs_perm(send_a, 2), fs_perm(plus(keep_b[1:], got_b[2:]), 4)


def scatter_second(keep, got, from_a, from_b):
    keep_a, keep_b = split_rows(keep, 1)
    got_a, got_b = split_rows(got, 1)
    send_a = total_of([keep_a[1], got_a[2], from_a[1]])
    send_b = total_of([keep_b[0], got_b[1], from_b[1]])
    return fs_perm(send_a.astype(BF), 4), fs_perm(send_b.astype(BF), 2)


def pack(z, mine, got, from_a, from_b, last_a, last_b, groups, rows):
    total, cols = mine.shape[1:]
    h = last_a.shape[0]
    lanes = sum(width * len(starts[0]) for width, starts in groups)
    shape = (rows, lanes)
    return pl.pallas_call(
        functools.partial(pack_kernel, groups=groups, rows=rows),
        grid=(1,),
        in_specs=[SMEM] + [whole((1, n, cols)) for n in (total, total, h, total - h)]
        + [whole((h, cols)), whole((total - h, cols))],
        out_specs=[whole(shape)] * 4,
        out_shape=[jax.ShapeDtypeStruct(shape, d) for d in (F32, BF, BF, BF)],
        scratch_shapes=[pltpu.VMEM((total, cols), F32), pltpu.VMEM((4,) + shape, F32)],
        compiler_params=params(20),
        cost_estimate=cost(total * cols * 8, total * cols * 12),
        name="pack",
    )(z.reshape(1), mine, got, from_a, from_b, last_a, last_b)


def total_of(terms):
    return functools.reduce(lambda a, b: a + b, [t.astype(F32) for t in terms])


def generic_blocks(full):
    blocks = full.reshape(FS // 2, 2, full.shape[0] // FS, full.shape[1])
    return blocks[:, 0], blocks[:, 1]


def generic_full(keep, send):
    full = jnp.stack([keep, send.astype(F32)], axis=1)
    return full.reshape(FS, -1, full.shape[-1])


def generic_gather(w_in, w_conv, w_out):
    both = lambda w, rows, cols: lax.all_gather(
        lax.all_gather(w, "fsdp", axis=cols, tiled=True), "dp", axis=rows, tiled=True
    )
    w_in, w_conv, w_out = both(w_in, 0, 1), both(w_conv, 1, 2), both(w_out, 0, 1)
    taps, inner = w_conv.shape[0], w_conv.shape[1]
    part = w_in.T.reshape(FS, inner // FS, 2, inner).transpose(0, 2, 1, 3).reshape(-1, inner)
    conv = w_conv.transpose(2, 0, 1).reshape(FS, inner // FS, taps, inner)
    conv = conv.transpose(0, 2, 1, 3).reshape(-1, inner)
    pairs = zip(generic_blocks(w_out.T), generic_blocks(conv))
    return generic_blocks(part), [jnp.concatenate(p, axis=1) for p in pairs]


def generic_scatter(ins, rest):
    scatter = lambda w, rows, cols: lax.psum_scatter(
        lax.psum_scatter(w, "fsdp", scatter_dimension=cols, tiled=True),
        "dp", scatter_dimension=rows, tiled=True,
    )
    d_in, rest = generic_full(*ins), generic_full(*rest)
    inner = d_in.shape[-1]
    cut = rest.shape[1] - KERNEL * inner // FS
    d_out, d_conv = rest[:, :cut], rest[:, cut:]
    d_in = d_in.reshape(FS, 2, -1, inner).transpose(0, 2, 1, 3).reshape(inner, -1).T
    d_conv = d_conv.reshape(FS, KERNEL, -1, inner).transpose(1, 3, 0, 2).reshape(KERNEL, inner, inner)
    return scatter(d_in, 0, 1), scatter(d_conv, 1, 2), scatter(d_out.reshape(-1, inner).T, 0, 1)


def local(
    n_dp,
    n_fs,
    activations,
    cotangent,
    lengths,
    cluster_sizes,
    residue_types,
    w_in,
    w_conv,
    w_out,
    inner_shard,
    model_shard,
):
    seqs, length, model = activations.shape
    inner = w_in.shape[1] * n_fs
    tokens = seqs * length
    x = activations.reshape(tokens, model)
    cot = cotangent.reshape(tokens, model)
    x, cot = in_hbm(x), in_hbm(cot)
    staged = n_dp == 4 and n_fs == FS
    place, z = lax.axis_index("fsdp"), lax.axis_index("dp")
    me = place.reshape(1) if staged else jnp.zeros((1,), jnp.int32)
    ci, co = inner // FS, model // FS

    positions = jnp.arange(length, dtype=jnp.int32)
    valid = positions[None, :] < lengths[:, None]
    kinds = jnp.arange(TYPES, dtype=jnp.int32)
    hits = (residue_types[:, :, None] == kinds[None, None, :]) & valid[:, :, None]
    counts = jnp.sum(hits.astype(jnp.int32), axis=(0, 1))

    def sds(shape, dtype):
        return jax.ShapeDtypeStruct(shape, dtype)

    tile = 512
    per = length // tile
    row = lambda i: (i, 0)

    def first_norm(part, parts, vec, old):
        size, steps = tile, tokens // parts // tile
        block = pl.BlockSpec((size, model), lambda i: (part * steps + i, 0))
        return pl.pallas_call(
            functools.partial(first_norm_kernel, chunk=256),
            grid=(steps,),
            in_specs=[block, whole((8, model))] + [ANY] * len(old),
            out_specs=[block] * 2,
            out_shape=[pltpu.HBM((tokens, model), BF)] * 2,
            input_output_aliases={2: 0, 3: 1} if old else {},
            compiler_params=params(48),
            cost_estimate=cost(
                tokens * model * 60 / parts, tokens * model * 6 / parts, tokens * model * 2 / parts
            ),
            name="first_norm",
        )(x, vec, *old)

    def in_proj(part, parts, a0, own, sib, vec, old):
        steps = tokens // parts // tile
        wide = pl.BlockSpec((tile, model), lambda i: (part * steps + i, 0))
        narrow = pl.BlockSpec((tile, inner), lambda i: (part * steps + i, 0))
        return pl.pallas_call(
            functools.partial(
                in_proj_kernel, tile=tile, chunk=256, length=length, first=part * seqs // parts
            ),
            grid=(steps,),
            in_specs=[SMEM, SMEM, wide, ANY, ANY, whole((8, inner))] + [ANY] * len(old),
            out_specs=[narrow] * 3,
            out_shape=[pltpu.HBM((tokens, inner), d) for d in (BF, F32, BF)],
            input_output_aliases={6: 0, 7: 1, 8: 2} if old else {},
            scratch_shapes=[pltpu.VMEM((inner, model), BF), pltpu.SemaphoreType.DMA((16,))],
            compiler_params=params(48),
            cost_estimate=cost(
                2 * tokens * model * inner * 3 / parts, tokens * (model + 4 * inner) * 2 / parts
            ),
            name="in_proj",
        )(me, lengths, a0, own, sib, vec, *old)

    if staged:
        cut, width = model // 4, inner // 4
        lanes = (KERNEL + 2) * width
        shapes = [((ci, cut), BF), ((ci, lanes), BF), ((ci, cut + lanes), BF), ((16, co), F32)]
        in_t, rest_t, both, vec = small(shards_kernel, shapes, name="shards")(
            *map(in_hbm, (w_in.T, w_conv, w_out, inner_shard, model_shard))
        )
        got = [dp_perm(both, 1), dp_perm(in_t, 2), dp_perm(both, 3)]
        for k in (1, 2, 4):
            vec = jnp.stack([vec, fs_perm(vec, k)])
        vec, in_t, rest_t, *got = tie(vec, in_t, rest_t, *got)

        place_z = z.reshape(1)
        block, inner_vec, model_vec = small(
            in_block_kernel,
            [((2 * ci, inner), BF), ((8, inner), F32), ((8, model), F32)],
            [((4, ci, cut), F32), ((FS, 16, co), F32)],
            name="in_block",
        )(me, place_z, in_t, *got, vec.reshape(FS, 16, co))
        blocks = [block] + [fs_perm(block, k) for k in (2, 4, 6)]
        rest_z = [rest_t, got[0], dp_perm(rest_t, 2), got[2]]
        a0, g0 = first_norm(0, 1, model_vec, [])
        tied = tie(a0, g0, *rest_z, *blocks)
        (a0, g0), rest_z, blocks = tied[:2], tied[2:6], tied[6:]

        total = lanes // width * ci
        h = total // 32 * 16
        in_own, a, b = small(
            unpack_kernel,
            [((4, 2 * ci, inner), BF), ((h, inner), BF), ((total - h, inner), BF)],
            [((4, ci, lanes), F32), ((total, inner), F32)],
            cut=(0, cut, 0, cut),
            name="unpack",
        )(place_z, *blocks, *rest_z)
        in_sib = fs_perm(in_own, 1)
        w_a1, w_b2 = fs_perm(a, 2), fs_perm(b, 4)
        in_own, in_sib, w_a1, w_b2 = tie(in_own, in_sib, w_a1, w_b2)

        a01, b02 = jnp.stack([a, w_a1]), jnp.stack([b, w_b2])
        second = [fs_perm(a01, 4), fs_perm(b02, 2), fs_perm(a01, 1), fs_perm(b02, 1)]
        a1, g1, c1 = in_proj(0, 1, a0, in_own, in_sib, inner_vec, [])
        a1, g1, c1, a01, b02, a23, b13, *early = tie(a1, g1, c1, a01, b02, *second)
        own = (a01, b02, a23, b13)
        sib = (*early, fs_perm(a23, 1), fs_perm(b13, 1))
    else:
        gather = lambda v: lax.all_gather(v, "fsdp", axis=1, tiled=True).astype(F32)
        inner_vec = jnp.pad(gather(inner_shard), ((0, 2), (0, 0)))
        model_vec = jnp.pad(gather(model_shard), ((0, 5), (0, 0)))
        (in_own, in_sib), (own, sib) = generic_gather(w_in, w_conv, w_out)
        a0, g0 = first_norm(0, 1, model_vec, [])
        a1, g1, c1 = in_proj(0, 1, a0, in_own, in_sib, inner_vec, [])

    anywhere = jax.tree.map(lambda _: ANY, own)

    wide, narrow = pl.BlockSpec((tile, model), row), pl.BlockSpec((tile, inner), row)
    rows = co + KERNEL * ci
    shapes = [((1, rows, inner), F32), ((3, rows, inner), BF), ((4, rows, inner), BF)]
    block_out, gv, *out_parts, vin2, vmod2 = pl.pallas_call(
        functools.partial(middle_kernel, tile=tile, chunk=256, length=length),
        grid=(tokens // tile,),
        in_specs=[SMEM, SMEM, SMEM, pl.BlockSpec((length, inner), lambda i: (i // per, 0)),
                  wide, wide, anywhere, anywhere, whole((8, model)), whole((8, inner))],
        out_specs=[wide, narrow, *(whole((n, co, inner)) for n in (1, 3, 4)),
                   whole((3, 8, inner)), whole((8, model))],
        out_shape=[sds((tokens, model), BF), sds((tokens, inner), BF), *(sds(*v) for v in shapes),
                   sds((3, 8, inner), F32), sds((8, model), F32)],
        scratch_shapes=[
            pltpu.VMEM((KERNEL * inner, inner), BF),
            pltpu.VMEM((model, inner), BF),
            pltpu.VMEM((length + 2 * REACH, inner), BF),
            pltpu.VMEM((tile, inner), BF),
            pltpu.VMEM((tile, model), BF),
            pltpu.VMEM((model, inner), F32),
            pltpu.SemaphoreType.DMA((48,)),
            pltpu.SemaphoreType.DMA((8,)),
        ],
        compiler_params=params(48),
        cost_estimate=cost(2 * tokens * inner * (KERNEL * inner + 3 * model) * 2, tokens * model * 10),
        name="middle",
    )(me, lengths, cluster_sizes, a1, x, cot, own, sib, model_vec, inner_vec)

    block = lambda n: pl.BlockSpec((n, ci, inner), lambda k: (0, k + 2, 0))
    mine, keep, send = pl.pallas_call(
        functools.partial(conv_grad_kernel, length=length, seqs=seqs),
        grid=(KERNEL,),
        in_specs=[SMEM, whole((tokens, inner)), whole((tokens, inner)), ANY, ANY, ANY],
        out_specs=[block(n) for n in (1, 3, 4)],
        out_shape=[sds(*v) for v in shapes],
        input_output_aliases={3: 0, 4: 1, 5: 2},
        scratch_shapes=[
            pltpu.VMEM((seqs, length + 2 * REACH, inner), BF),
            pltpu.VMEM((inner, inner), F32),
        ],
        compiler_params=params(48),
        cost_estimate=cost(2 * tokens * KERNEL * inner * inner * 1.3, tokens * inner * 4),
        name="conv_grad",
    )(me, a1, gv, *out_parts)

    def conv_back(s, extra):
        last = bool(extra)
        at = lambda i: (s * per + i, 0)
        once = lambda i: (s, 0)
        part = pl.BlockSpec((tile, inner), at)
        ins = [SMEM, pl.BlockSpec((length, inner), once), part, part, anywhere, anywhere, whole((8, inner))]
        outs = [pl.BlockSpec((tile, inner), row), whole((3, 8, inner))]
        shapes = [sds((length, inner), BF), sds((3, 8, inner), F32)]
        scratch = [
            pltpu.VMEM((KERNEL * inner, inner), BF),
            pltpu.VMEM((length + 2 * REACH, inner), BF),
            pltpu.SemaphoreType.DMA((48,)),
        ]
        if last:
            ins += [
                pl.BlockSpec((tile, inner), row),
                pl.BlockSpec((tile, model), row),
                pl.BlockSpec((tile, model), at),
            ]
            for n, dtype in ((1, F32), (3, BF), (4, BF)):
                outs += [whole((n, 2 * ci, inner))]
                shapes += [sds((n, 2 * ci, inner), dtype)]
            scratch += [pltpu.VMEM((inner, model), F32)]
        return pl.pallas_call(
            functools.partial(conv_back_kernel, tile=tile, chunk=256, last=last),
            grid=(per,),
            in_specs=ins,
            out_specs=outs,
            out_shape=shapes,
            scratch_shapes=scratch,
            compiler_params=params(48),
            cost_estimate=cost(
                2 * length * inner * (KERNEL * inner + 2 * model * last) * 1.5, length * inner * 12
            ),
            name="conv_back",
        )(me, gv, g1, c1, own, sib, inner_vec, *extra)

    def first_back(s, gu, old):
        tile = 256
        per = length // tile
        at = lambda i: (s * per + i, 0)
        wide = pl.BlockSpec((tile, model), at)
        ins = [SMEM, SMEM, SMEM, wide, wide, pl.BlockSpec((tile, inner), row), wide, ANY, ANY]
        return pl.pallas_call(
            functools.partial(first_back_kernel, tile=tile, chunk=256, length=length, first=s),
            grid=(per,),
            in_specs=ins + [whole((8, model))] + [ANY] * len(old),
            out_specs=[wide, whole((2, 8, model))],
            out_shape=[sds((tokens, model), BF), sds((2, 8, model), F32)],
            input_output_aliases={10: 0} if old else {},
            scratch_shapes=[pltpu.VMEM((inner, model), BF), pltpu.SemaphoreType.DMA((16,))],
            compiler_params=params(48),
            cost_estimate=cost(2 * length * model * inner * 4, length * model * 8),
            name="first_back",
        )(me, lengths, cluster_sizes, x, cot, gu, g0, in_own, in_sib, model_vec, *old)

    if staged:
        send, gv = tie(send, gv)
        got = fs_perm(send, 1)
        gu0, vin1a = conv_back(0, [])
        got, gu0 = tie(got, gu0)

        first = scatter_first(keep, got)
        gu1, vin1b, in_mine, in_keep, in_send = conv_back(1, [gu0, a0, a0])
        *first, in_send, gu1 = tie(*first, in_send, gu1)

        second = scatter_second(keep, got, *first)
        in_got = fs_perm(in_send, 1)
        grad_x, vmod0a = first_back(0, gu0, [])
        *second, in_got, grad_x = tie(*second, in_got, grad_x)

        width = inner // 4
        groups = [(width, [[(t * ci, d * width) for t in range(KERNEL + 2)] for d in range(4)])]
        own, *sends = pack(z, mine, got, *first, *second, groups, ci)
        from_1, from_3 = dp_perm(sends[0], 1), dp_perm(sends[2], 3)
        in_first = scatter_first(in_keep, in_got)
        grad_x, vmod0b = first_back(1, gu1, [grad_x])
        own, from_1, from_3, send_2, vmod0b, *in_first = tie(
            own, from_1, from_3, sends[1], vmod0b, *in_first
        )

        counts = jnp.pad(counts.astype(F32), (0, 128 - TYPES)).reshape(1, 128)
        sums, send = small(
            sums_kernel,
            [((4, 16, co), F32)] * 2,
            [((8, inner), F32), ((8, model), F32)],
            name="sums",
        )(me, vin1a, vin1b, vin2, vmod0a, vmod0b, vmod2, counts)
        got = fs_perm(send, 1)
        in_second = scatter_second(in_keep, in_got, *in_first)
        upper = dp_perm(send_2[: ci // 2], 2)
        sums, got, upper, *in_second = tie(sums, got, upper, *in_second)

        sums = sums + got
        lower = dp_perm(send_2[ci // 2 :], 2)
        got = [fs_perm(sums[k], 2 * k) for k in (1, 2, 3)]
        sums, lower, *got = tie(sums, lower, *got)

        shape = (ci, model // 4)
        piece = ((ci + 16, model // 4), BF)
        in_own, vec, *sends = small(
            last_pack_kernel,
            [(shape, F32), ((16, co), F32), piece, piece, piece],
            [((2 * ci, inner), F32), ((4,) + shape, F32)],
            name="last_pack",
        )(z.reshape(1), in_mine, in_got, *in_first, *in_second, sums[0], *got)
        got = [dp_perm(v, k) for k, v in zip((1, 2, 3), sends)]
        d_conv, d_out = small(
            rest_kernel, [((KERNEL, width, ci), F32), ((width, co), F32)], name="rest"
        )(own, from_1, upper, lower, from_3)
        d_in, d_inner, d_model, counts = small(
            last_kernel,
            [(shape, F32), ((6, ci), F32), ((3, co), F32), ((1, 128), F32)],
            name="last",
        )(in_own, vec, *got)
        d_in = d_in.T
        type_counts = counts[0, :TYPES].astype(jnp.int32)
    else:
        gu0, vin1a = conv_back(0, [])
        gu1, vin1b, in_mine, in_keep, in_send = conv_back(1, [gu0, a0, a0])
        grad_x, vmod0a = first_back(0, gu0, [])
        grad_x, vmod0b = first_back(1, gu1, [grad_x])
        down = lambda v: jnp.sum(v, axis=-2)
        type_counts, d_inner, d_model = lax.psum(
            (
                counts,
                jnp.concatenate([down(vin1a + vin1b), down(vin2)]),
                jnp.concatenate([down(vmod0a + vmod0b), down(vmod2)[None]]),
            ),
            ("dp", "fsdp"),
        )
        ours = lambda v, n: lax.dynamic_slice_in_dim(v, place * n, n, 1)
        d_inner, d_model = ours(d_inner, inner_shard.shape[1]), ours(d_model, model_shard.shape[1])
        with_mine = lambda m, k: jnp.concatenate([m, k.astype(F32)])
        d_in, d_conv, d_out = generic_scatter(
            (with_mine(in_mine, in_keep), in_send), (with_mine(mine, keep), send)
        )

    return (
        block_out.reshape(activations.shape),
        grad_x.reshape(activations.shape),
        d_in,
        d_conv,
        d_out,
        d_inner,
        d_model,
        type_counts,
    )


def solution(mesh):
    rows = ("dp", "fsdp")
    return jax.shard_map(
        functools.partial(local, mesh.shape["dp"], mesh.shape["fsdp"]),
        mesh=mesh,
        in_specs=(
            P(rows, None, None),
            P(rows, None, None),
            P(rows),
            P(rows),
            P(rows, None),
            P("dp", "fsdp"),
            P(None, "dp", "fsdp"),
            P("dp", "fsdp"),
            P(None, "fsdp"),
            P(None, "fsdp"),
        ),
        out_specs=(
            P(rows, None, None),
            P(rows, None, None),
            P("dp", "fsdp"),
            P(None, "dp", "fsdp"),
            P("dp", "fsdp"),
            P(None, "fsdp"),
            P(None, "fsdp"),
            P(),
        ),
        check_vma=False,
    )
```
